128 devices in a mesh: group: 4 (over x), bulk: 32 (over z, y, core).
Axes of the slice: x: 4, y: 4, z: 4, core: 2. Of those that a mesh axis runs over, the one named last changes fastest.
Arguments:
- rhs: float32 [512, 64, 128], P(('group', 'bulk')), may hold values from -90 to 90, as said below
- diag_tiles: float32 [512, 128, 128], P(('group', 'bulk')), may hold values from -0.06 to 0.06
- offdiag_blocks: float32 [512, 11, 128, 128], P(('group', 'bulk')), may hold values from -0.026 to 0.026
- coupling: float32 [256, 4, 128, 128], P(('group', 'bulk')), may hold values from -0.05 to 0.05, as said below
- col_index: int32 [512, 11], replicated, may hold values from 0 to 511, as said below
- load: int32 [512], replicated, may hold values from 3 to 11
- new_slot: int32 [512], replicated, may hold values from 0 to 511, as said below
Outputs:
- solution_out: float32 [512, 64, 128], P(('group', 'bulk'))
- residual_out: float32 [512, 64, 128], P(('group', 'bulk'))
The draws below stay inside these ranges and needn't reach their ends.
Inputs may be any that keep to these rules, and one draw needn't show every extreme that they name: `rhs`: made of random entries times scales of the rows and of the columns. `coupling`: entry [d * 2 + k, h] is the transpose of entry [(h * 32 + d % 32) * 2 + k, d // 32]. `col_index`: for each part g and each tile position t, the column t of the 128 block rows of part g is a permutation of that part's slots g * 128 to (g + 1) * 128 - 1. Of the 44 entries of the 4 block rows of one device (slots d * 4 to (d + 1) * 4 - 1), at most 2 name slots of any one device, and exactly 2 name slots of some device. `new_slot`: A permutation. On every device exactly one block row moves, from a slot k with 2 <= k % 4; it stays in its part, goes from owner b to owner b XOR m, where m (1 to 31) is one number for the whole part, and takes the slot that the moving row of that device leaves.
All inputs are finite; a program needn't handle non-finite values.
Results may differ from the reference program's by a relative error of at most 0.0003.
Values sent between devices are 32-bit elements; how exact they have to be, the bound alone decides.
A program may use at most 64 MiB of HBM per device.

```python
import math
import jax
import jax.numpy as jnp
from jax import lax

TILE_ORDER = 128
RIGHT_HAND_COUNT = 64
OFFDIAG_TILES = 11
ROWS_DEV = 4
ITERS = 2
IFACE = 2
PART_BLOCK_ROWS = 128
TOTAL_BLOCK_ROWS = 512


def draw_rhs(key, part):
    noise_key, rows_key, key_cols = jax.random.split(key, 3)
    random_jitter = jnp.clip(jax.random.normal(noise_key, (TOTAL_BLOCK_ROWS, RIGHT_HAND_COUNT, TILE_ORDER), jnp.float32), -6.0, 6.0)
    row_history = jax.random.uniform(rows_key, (TOTAL_BLOCK_ROWS, 1, TILE_ORDER), jnp.float32, 0.0, math.log(10.0))
    col_log = jax.random.uniform(key_cols, (1, RIGHT_HAND_COUNT, 1), jnp.float32, 0.0, math.log(10.0))
    ascending_order = 1.0 + 2.0 * jnp.arange(TOTAL_BLOCK_ROWS, dtype=jnp.float32) / max(TOTAL_BLOCK_ROWS - 1, 1)
    return 0.03 * random_jitter * jnp.exp(row_history) * jnp.exp(col_log) * ascending_order[:, None, None]


def draw_diag_tiles(key, part):
    unsorted_draws = jax.random.uniform(key, (TOTAL_BLOCK_ROWS, TILE_ORDER, TILE_ORDER), jnp.float32, -0.06, 0.06)
    return 0.5 * (unsorted_draws + jnp.swapaxes(unsorted_draws, 1, 2))


def draw_coupling(key, part):
    part_count = TOTAL_BLOCK_ROWS // PART_BLOCK_ROWS
    boundary_rows = TOTAL_BLOCK_ROWS // 2 // part_count
    unsorted_draws = jax.random.uniform(key, (part_count, boundary_rows, part_count, TILE_ORDER, TILE_ORDER), jnp.float32, -0.03, 0.03)
    mirrored = jnp.swapaxes(jnp.transpose(unsorted_draws, (2, 1, 0, 3, 4)), 3, 4)
    joined = (unsorted_draws + mirrored) * 0.7071067811865476
    return joined.reshape(part_count * boundary_rows, part_count, TILE_ORDER, TILE_ORDER)


def draw_col_index(key, part):
    part_count = TOTAL_BLOCK_ROWS // PART_BLOCK_ROWS
    owner_count = PART_BLOCK_ROWS // ROWS_DEV
    read_count = OFFDIAG_TILES * ROWS_DEV
    key_off, key_row, key_shift = jax.random.split(key, 3)
    off_keys = jax.random.split(key_off, part_count)
    orders = jax.vmap(lambda one_key: jax.random.permutation(one_key, read_count))(off_keys).astype(jnp.int32)
    shifts = jax.random.randint(key_shift, (part_count, 1), 0, owner_count, dtype=jnp.int32)
    offsets = jnp.remainder(orders + shifts, owner_count).reshape(part_count, ROWS_DEV, OFFDIAG_TILES)
    row_keys = jax.random.split(key_row, part_count * OFFDIAG_TILES)
    row_perm = jax.vmap(lambda one_key: jax.random.permutation(one_key, ROWS_DEV))(row_keys).astype(jnp.int32)
    row_perm = jnp.transpose(row_perm.reshape(part_count, OFFDIAG_TILES, ROWS_DEV), (0, 2, 1))
    owners = jnp.arange(owner_count, dtype=jnp.int32)[None, :, None, None]
    target = jnp.remainder(owners + offsets[:, None], owner_count)
    bases = (jnp.arange(part_count, dtype=jnp.int32) * PART_BLOCK_ROWS)[:, None, None, None]
    column_ids = bases + target * ROWS_DEV + row_perm[:, None]
    return column_ids.reshape(TOTAL_BLOCK_ROWS, OFFDIAG_TILES).astype(jnp.int32)


def draw_new_slot(key, part):
    part_count = TOTAL_BLOCK_ROWS // PART_BLOCK_ROWS
    owner_count = PART_BLOCK_ROWS // ROWS_DEV
    device_count = part_count * owner_count
    key_mover, key_mask = jax.random.split(key, 2)
    mover = IFACE + jax.random.randint(key_mover, (device_count,), 0, ROWS_DEV - IFACE, dtype=jnp.int32)
    xor_vals = jax.random.randint(key_mask, (part_count,), 1, owner_count, dtype=jnp.int32)
    devices = jnp.arange(device_count, dtype=jnp.int32)
    group_of = devices // owner_count
    owner_of = devices % owner_count
    target_dev = group_of * owner_count + jnp.bitwise_xor(owner_of, xor_vals[group_of])
    source_rows = devices * ROWS_DEV + mover
    target_rows = target_dev * ROWS_DEV + mover[target_dev]
    return jnp.arange(TOTAL_BLOCK_ROWS, dtype=jnp.int32).at[source_rows].set(target_rows)


def place_ends(result, key, low, top_value):
    spot = [jax.random.randint(jax.random.fold_in(key, axis), (), 0, length) for axis, length in enumerate(result.shape)]
    main_axis = result.shape.index(max(result.shape))
    beside = spot[:main_axis] + [(spot[main_axis] + 1) % result.shape[main_axis]] + spot[main_axis + 1:]
    return result.at[tuple(spot)].set(low).at[tuple(beside)].set(top_value)


def steps_of(rng, dims, pieces, smallest, largest):
    gain, own = 1.0, jax.random.fold_in(rng, 6)
    for position, parts in pieces:
        steps = jnp.exp(jax.random.uniform(jax.random.fold_in(own, position), (parts,), jnp.float32, smallest / len(pieces), largest / len(pieces)))
        gain = gain * jnp.repeat(steps, dims[position] // parts).reshape([-1 if axis == position else 1 for axis in range(len(dims))])
    return gain


def setup_inputs(seed: int = 0) -> dict:
    key_of = jax.random.split(jax.random.key(seed), 8)
    return {
        "rhs": draw_rhs(jax.random.fold_in(key_of[7], 71), 0),
        "diag_tiles": draw_diag_tiles(jax.random.fold_in(key_of[7], 71), 0),
        "offdiag_blocks": jnp.clip(jax.random.uniform(key_of[2], (TOTAL_BLOCK_ROWS, OFFDIAG_TILES, TILE_ORDER, TILE_ORDER), jnp.float32, -0.026, 0.026) * steps_of(key_of[2], (TOTAL_BLOCK_ROWS, OFFDIAG_TILES, TILE_ORDER, TILE_ORDER), ((0, 128),), -0.4, 0.0), -0.026, 0.026),
        "coupling": draw_coupling(jax.random.fold_in(key_of[7], 71), 0),
        "col_index": draw_col_index(jax.random.fold_in(key_of[7], 71), 0),
        "load": place_ends(jax.random.randint(key_of[5], (TOTAL_BLOCK_ROWS,), 3, OFFDIAG_TILES + 1), jax.random.fold_in(key_of[5], 1), 3, OFFDIAG_TILES).astype(jnp.int32),
        "new_slot": draw_new_slot(jax.random.fold_in(key_of[7], 71), 0),
    }


highest = lax.Precision.HIGHEST

def chol_apply(matrix, right):
    factor = jnp.linalg.cholesky(matrix)
    middle = lax.linalg.triangular_solve(factor, right, left_side=True, lower=True)
    return lax.linalg.triangular_solve(factor, middle, left_side=True, lower=True, transpose_a=True)

def gram_of(left, right):
    total = jnp.einsum('snt,smt->nm', left, right, precision=highest)
    return 0.5 * (total + total.T)

def operate(vectors, diag_tiles, offdiag_blocks, coupling, col_index, load):
    mask = (jnp.arange(OFFDIAG_TILES)[None, :] < load[:, None]).astype(jnp.float32)
    final_output = 4.0 * vectors + jnp.einsum('snj,sij->sni', vectors, diag_tiles, precision=highest)
    for tile_pos in range(OFFDIAG_TILES):
        masked = offdiag_blocks[:, tile_pos] * mask[:, tile_pos, None, None]
        picked = vectors[col_index[:, tile_pos]]
        final_output = final_output + jnp.einsum('snj,sij->sni', picked, masked, precision=highest)
        returned = jnp.einsum('sni,sij->snj', vectors, masked, precision=highest)
        final_output = final_output.at[col_index[:, tile_pos]].add(returned)
    part_count = TOTAL_BLOCK_ROWS // PART_BLOCK_ROWS
    owner_count = PART_BLOCK_ROWS // ROWS_DEV
    shaped = vectors.reshape(part_count, owner_count, ROWS_DEV, RIGHT_HAND_COUNT, TILE_ORDER)
    border = shaped[:, :, :IFACE]
    tiles = coupling.reshape(part_count, owner_count, IFACE, part_count, TILE_ORDER, TILE_ORDER)
    crossed = jnp.einsum('gbkhij,hbknj->gbkni', tiles, border, precision=highest)
    final_output = final_output.reshape(part_count, owner_count, ROWS_DEV, RIGHT_HAND_COUNT, TILE_ORDER)
    final_output = final_output.at[:, :, :IFACE].add(crossed)
    return final_output.reshape(TOTAL_BLOCK_ROWS, RIGHT_HAND_COUNT, TILE_ORDER)

def reference(rhs, diag_tiles, offdiag_blocks, coupling, col_index, load, new_slot):
    solution = jnp.zeros_like(rhs)
    resid = rhs
    direction = rhs
    gram_rr = gram_of(resid, resid)
    for step_id in range(ITERS):
        image = operate(direction, diag_tiles, offdiag_blocks, coupling, col_index, load)
        gram_pq = gram_of(direction, image)
        alpha = chol_apply(gram_pq, gram_rr)
        solution = solution + jnp.einsum('mn,smt->snt', alpha, direction, precision=highest)
        resid = resid - jnp.einsum('mn,smt->snt', alpha, image, precision=highest)
        if step_id + 1 < ITERS:
            gram_new = gram_of(resid, resid)
            beta = chol_apply(gram_rr, gram_new)
            direction = resid + jnp.einsum('mn,smt->snt', beta, direction, precision=highest)
            gram_rr = gram_new
    solution_out = jnp.zeros_like(solution).at[new_slot].set(solution)
    residual_out = jnp.zeros_like(resid).at[new_slot].set(resid)
    return (solution_out, residual_out)
```

```python
import jax
import jax.numpy as jnp
from jax import lax
from jax.sharding import PartitionSpec as P

highest = lax.Precision.HIGHEST
diagonal_shift = 4.0


def chol_apply(matrix, right):
    factor = jnp.linalg.cholesky(matrix)
    middle = lax.linalg.triangular_solve(factor, right, left_side=True, lower=True)
    return lax.linalg.triangular_solve(factor, middle, left_side=True, lower=True, transpose_a=True)


def gram(left, right):
    return jnp.einsum("snt,smt->nm", left, right, precision=highest)


def sym(m):
    return 0.5 * (m + m.T)


def mm(a, b):
    return jnp.dot(a, b, precision=highest)


def off_part(vectors, diag, masked, column_ids, coupling):
    boundary_rows = coupling.shape[0]
    part_count = coupling.shape[1]
    border = lax.all_gather(vectors[:boundary_rows], "group", axis=0, tiled=True)
    own = jnp.einsum("rnj,rij->rni", vectors, diag, precision=highest)
    returned = jnp.einsum("rni,rkij->rknj", vectors, masked, precision=highest)
    panel = lax.all_gather(vectors, "bulk", axis=0, tiled=True)
    picked = panel[column_ids]
    own = own + jnp.einsum("rknj,rkij->rni", picked, masked, precision=highest)
    border = border.reshape((part_count, boundary_rows) + vectors.shape[1:])
    crossed = jnp.einsum("khij,hknj->kni", coupling, border, precision=highest)
    return own.at[:boundary_rows].add(crossed), returned.reshape((-1,) + vectors.shape[1:]), panel


def coefficients(n0, n1, n2, n3):
    n = n0.shape[0]
    eye = jnp.eye(n, dtype=n0.dtype)
    n0, n1, n2, n3 = sym(n0), sym(n1), sym(n2), sym(n3)
    delta = chol_apply(diagonal_shift * n0 + n1, n1)
    alpha = (eye - delta) / diagonal_shift
    b = -alpha
    cross = mm(delta.T, mm(n1, b))
    gram_new = sym(mm(delta.T, mm(n0, delta)) + cross + cross.T + mm(b.T, mm(n2, b)))
    beta = chol_apply(n0, gram_new)
    a = delta + beta
    c1 = mm(a.T, mm(n1, b))
    c2 = mm(a.T, mm(n2, b))
    pp = mm(a.T, mm(n0, a)) + c1 + c1.T + mm(b.T, mm(n2, b))
    pep = mm(a.T, mm(n1, a)) + c2 + c2.T + mm(b.T, mm(n3, b))
    alpha2 = chol_apply(sym(diagonal_shift * pp + pep), gram_new)
    ba = mm(b, alpha2)
    aa = mm(a, alpha2)
    sol = (alpha + aa, ba)
    res = (delta - diagonal_shift * aa, b - diagonal_shift * ba - aa, -ba)
    return sol, res


def local(rhs, diag_tiles, offdiag_blocks, coupling, col_index, load, new_slot):
    row_count = rhs.shape[0]
    off_count = offdiag_blocks.shape[1]
    bulk_count = lax.axis_size("bulk")
    group_rows = row_count * bulk_count
    group_base = lax.axis_index("group") * group_rows
    first = lax.axis_index("bulk") * row_count
    cols = lax.dynamic_slice_in_dim(col_index, group_base, group_rows) - group_base
    moved = lax.dynamic_slice_in_dim(new_slot, group_base, group_rows) - group_base
    loads = lax.dynamic_slice_in_dim(load, group_base + first, row_count)
    my_cols = lax.dynamic_slice_in_dim(cols, first, row_count)
    my_new = lax.dynamic_slice_in_dim(moved, first, row_count)
    tile_ids = jnp.arange(off_count, dtype=jnp.int32)
    mask = (tile_ids[None, :] < loads[:, None]).astype(jnp.float32)
    masked = offdiag_blocks * mask[:, :, None, None]
    u0 = rhs
    own, returned, panel0 = off_part(u0, diag_tiles, masked, my_cols, coupling)
    buffer = jax.ops.segment_sum(returned, my_cols.reshape(-1), num_segments=group_rows)
    u1 = own + lax.psum_scatter(buffer, "bulk", scatter_dimension=0, tiled=True)
    own, returned, panel1 = off_part(u1, diag_tiles, masked, my_cols, coupling)
    ids = jnp.concatenate([moved[my_cols.reshape(-1)], my_new])
    buffer = jax.ops.segment_sum(
        jnp.concatenate([returned, own]), ids, num_segments=group_rows
    )
    u2 = lax.psum_scatter(buffer, "bulk", scatter_dimension=0, tiled=True)
    inverse = jnp.zeros_like(moved).at[moved].set(jnp.arange(group_rows, dtype=jnp.int32))
    mine = lax.dynamic_slice_in_dim(inverse, first, row_count)
    v0, v1 = panel0[mine], panel1[mine]
    grams = jnp.stack([gram(v0, v0), gram(v0, v1), gram(v1, v1), gram(v1, u2)])
    grams = lax.psum(grams, ("group", "bulk"))
    sol, res = coefficients(grams[0], grams[1], grams[2], grams[3])
    basis = jnp.concatenate([v0, v1, u2], axis=1)
    zero = jnp.zeros_like(sol[0])
    weights = jnp.concatenate(
        [jnp.concatenate(sol + (zero,), axis=0), jnp.concatenate(res, axis=0)], axis=1
    )
    out = jnp.einsum("mn,smt->snt", weights, basis, precision=highest)
    n = rhs.shape[1]
    return out[:, :n], out[:, n:]


def solution(mesh):
    return jax.shard_map(
        local,
        mesh=mesh,
        in_specs=(
            P(("group", "bulk"), None, None),
            P(("group", "bulk"), None, None),
            P(("group", "bulk"), None, None, None),
            P(("group", "bulk"), None, None, None),
            P(),
            P(),
            P(),
        ),
        out_specs=(P(("group", "bulk"), None, None), P(("group", "bulk"), None, None)),
        check_vma=False,
    )
```

```python
import functools

import jax
import jax.numpy as jnp
from jax import lax
from jax.experimental import pallas as pl
from jax.experimental.pallas import tpu as pltpu
from jax.sharding import PartitionSpec as P

highest = lax.Precision.HIGHEST
shift = 4.0
f32 = jnp.float32
bf16 = jnp.bfloat16
RING = 4
MESH = pl.DeviceIdType.MESH


class Net:
    def __init__(self, send, recv):
        self.g = lax.axis_index("group")
        b = lax.axis_index("bulk")
        self.c = lax.rem(b, 2)
        self.y = lax.rem(b // 2, RING)
        self.z = b // (2 * RING)
        self.send, self.recv = send, recv
        self.count = 0
        self.pending = []

    def device(self, dx=0, dy=0, dz=0, partner=False):
        c = 1 - self.c if partner else self.c
        y = lax.rem(self.y + dy, RING)
        z = lax.rem(self.z + dz, RING)
        return (lax.rem(self.g + dx, RING), (z * RING + y) * 2 + c)

    def copy(self, src, dst, device):
        i = self.count
        self.count += 1
        d = pltpu.make_async_remote_copy(
            src_ref=src,
            dst_ref=dst,
            send_sem=self.send.at[i],
            recv_sem=self.recv.at[i],
            device_id=device,
            device_id_type=MESH,
        )
        d.start()
        self.pending.append(d)
        return d

    def drain(self):
        for d in self.pending:
            d.wait_send()


def plus(a, k):
    return lax.rem(a + k, RING)


def greet(net, devices):
    barrier = pltpu.get_barrier_semaphore()
    for d in devices:
        pl.semaphore_signal(barrier, inc=1, device_id=d, device_id_type=MESH)
    pl.semaphore_wait(barrier, len(devices))


def gather_steps(net, j, u, panel, local_sem):
    c, y, z = net.c, net.y, net.z
    f0, s0 = (y, z) if j == 0 else (z, y)

    def unit(fi, si):
        return panel.at[c, j, si, fi] if j == 0 else panel.at[c, j, fi, si]

    def column(si):
        return panel.at[c, j, si] if j == 0 else panel.at[c, j, :, si]

    def to(df, ds):
        return net.device(dy=df, dz=ds) if j == 0 else net.device(dy=ds, dz=df)

    partner = net.device(partner=True)
    mine = unit(f0, s0)
    own = pltpu.make_async_copy(u.at[j], mine, local_sem)
    own.start()
    up = net.copy(u.at[j], mine, to(1, 0))
    down = net.copy(u.at[j], mine, to(3, 0))
    ups = [net.copy(u.at[j], mine, to(0, 1))]
    downs = [net.copy(u.at[j], mine, to(0, 3))]
    lo, hi = pl.ds(0, 2), pl.ds(2, 2)

    def pass_on(piece):
        ups.append(net.copy(piece, piece, to(0, 1)))
        downs.append(net.copy(piece, piece, to(0, 3)))

    yield
    up.wait_recv()
    piece = unit(plus(f0, 3), s0)
    up2 = net.copy(piece.at[lo], piece.at[lo], to(1, 0))
    pass_on(piece)
    yield
    down.wait_recv()
    piece = unit(plus(f0, 1), s0)
    down2 = net.copy(piece.at[hi], piece.at[hi], to(3, 0))
    pass_on(piece)
    order = [f0, plus(f0, 3), plus(f0, 1), plus(f0, 2)]
    ups2, downs2 = [], []
    for p in range(4):
        if p == 1:
            yield
            up2.wait_recv()
            down2.wait_recv()
            pass_on(unit(plus(f0, 2), s0))
            own.wait()
            exchanged = [net.copy(column(s0), column(s0), partner)]
        yield
        ups[p].wait_recv()
        piece = unit(order[p], plus(s0, 3))
        ups2.append(net.copy(piece.at[lo], piece.at[lo], to(0, 1)))
        yield
        downs[p].wait_recv()
        piece = unit(order[p], plus(s0, 1))
        downs2.append(net.copy(piece.at[hi], piece.at[hi], to(0, 3)))
    for k in (3, 1):
        exchanged.append(net.copy(column(plus(s0, k)), column(plus(s0, k)), partner))
    for d in ups2 + downs2:
        yield
        d.wait_recv()
    exchanged.append(net.copy(column(plus(s0, 2)), column(plus(s0, 2)), partner))
    for d in exchanged:
        yield
        d.wait_recv()


def scatter_steps(net, j, buf, owed, r, t0, t1, t2, t3, t4):
    c, y, z = net.c, net.y, net.z
    f0, s0 = (y, z) if j == 0 else (z, y)

    def column(ref, si):
        return ref.at[j, si] if j == 0 else ref.at[j, :, si]

    def to(df, ds):
        return net.device(dy=df, dz=ds) if j == 0 else net.device(dy=ds, dz=df)

    partner = net.device(partner=True)
    lo, hi = pl.ds(0, 2), pl.ds(2, 2)
    first = {}
    for k in (2, 1, 3, 0):
        si = plus(s0, k)
        src = buf.at[1 - c]
        first[k] = net.copy(column(src, si), column(t0, si), partner)
    cols = {k: column(r, plus(s0, k)) for k in range(4)}

    def start(k):
        si = plus(s0, k)
        a, b = column(buf.at[c], si), column(t0, si)
        for fi in range(RING):
            cols[k][fi] = a[fi] + b[fi]

    yield
    first[2].wait_recv()
    start(2)
    up = net.copy(cols[2].at[:, lo], t1.at[j, 0], to(0, 1))
    down = net.copy(cols[2].at[:, hi], t1.at[j, 1], to(0, 3))
    yield
    first[1].wait_recv()
    start(1)
    yield
    first[3].wait_recv()
    start(3)
    yield
    up.wait_recv()
    for fi in range(RING):
        cols[1][fi, lo] = cols[1][fi, lo] + t1[j, 0, fi]
    up2 = net.copy(cols[1], t2.at[j, 0], to(0, 1))
    yield
    down.wait_recv()
    for fi in range(RING):
        cols[3][fi, hi] = cols[3][fi, hi] + t1[j, 1, fi]
    down2 = net.copy(cols[3], t2.at[j, 1], to(0, 3))
    yield
    first[0].wait_recv()
    start(0)
    yield
    up2.wait_recv()
    down2.wait_recv()
    mine = cols[0]

    def add(k):
        fi = plus(f0, k)
        mine[fi] = mine[fi] + (t2[j, 0, fi] + t2[j, 1, fi])

    add(2)
    far = mine.at[plus(f0, 2)]
    up3 = net.copy(far.at[lo], t3.at[j, 0], to(1, 0))
    down3 = net.copy(far.at[hi], t3.at[j, 1], to(3, 0))
    add(1)
    add(3)
    add(0)
    yield
    up3.wait_recv()
    fi = plus(f0, 1)
    mine[fi, lo] = mine[fi, lo] + t3[j, 0]
    up4 = net.copy(mine.at[fi], t4.at[j, 0], to(1, 0))
    yield
    down3.wait_recv()
    fi = plus(f0, 3)
    mine[fi, hi] = mine[fi, hi] + t3[j, 1]
    down4 = net.copy(mine.at[fi], t4.at[j, 1], to(3, 0))
    yield
    up4.wait_recv()
    down4.wait_recv()
    owed[j] = mine[f0] + (t4[j, 0] + t4[j, 1])


def border_steps(net, u, border, local_sem):
    src = u.at[:, pl.ds(0, 2)]
    own = pltpu.make_async_copy(src, border.at[net.g], local_sem)
    own.start()
    sent = [net.copy(src, border.at[net.g], net.device(dx=k)) for k in (1, 3, 2)]
    yield
    own.wait()
    for d in sent:
        d.wait_recv()


def reduce_steps(net, m, out, acc, slots, halves):
    c = net.c
    rows = acc.shape[1]
    partner = net.device(partner=True)
    d = net.copy(m.at[pl.ds((1 - c) * rows, rows)], halves, partner)
    yield
    d.wait_recv()
    acc[0] = m[pl.ds(c * rows, rows)] + halves[...]
    for t in range(3):
        sent = []
        for k in (1, 3, 2):
            step = [0, 0, 0]
            step[t] = k * (1 - c)
            step[(t + 1) % 3] = step[(t + 1) % 3] + k * c
            sent.append(
                net.copy(acc.at[t], slots.at[t, k - 1], net.device(step[0], step[1], step[2]))
            )
        yield
        for d in sent:
            d.wait_recv()
        acc[t + 1] = (acc[t] + slots[t, 0]) + (slots[t, 1] + slots[t, 2])
    out[pl.ds(c * rows, rows)] = acc[3]
    d = net.copy(acc.at[3], out.at[pl.ds(c * rows, rows)], partner)
    yield
    d.wait_recv()


def run(steps):
    steps = list(steps)
    while steps:
        left = []
        for s in steps:
            try:
                next(s)
                left.append(s)
            except StopIteration:
                pass
        steps = left


def exchange_kernel(gather, scatter, reduce, *refs):
    refs = list(refs)
    u = refs.pop(0) if gather else None
    buf = refs.pop(0) if scatter else None
    m = refs.pop(0) if reduce else None
    panel = refs.pop(0) if gather else None
    border = refs.pop(0) if gather else None
    owed = refs.pop(0) if scatter else None
    total = refs.pop(0) if reduce else None
    parts = [refs.pop(0) for _ in range(6)] if scatter else None
    work = [refs.pop(0) for _ in range(3)] if reduce else None
    send, recv, local_sems = refs
    net = Net(send, recv)
    devices = [net.device(partner=True)]
    devices += [net.device(dy=k) for k in (1, 3)] + [net.device(dz=k) for k in (1, 3)]
    if gather or reduce:
        devices += [net.device(dx=k) for k in (1, 2, 3)]
    if reduce:
        devices += [net.device(dy=2), net.device(dz=2)]
    greet(net, devices)
    steps = []
    if reduce:
        steps.append(reduce_steps(net, m, total, *work))
    if scatter:
        steps += [scatter_steps(net, j, buf, owed, *parts) for j in range(2)]
    if gather:
        steps += [gather_steps(net, j, u, panel, local_sems.at[j]) for j in range(2)]
        steps.append(border_steps(net, u, border, local_sems.at[2]))
    run(steps)
    net.drain()


def exchange(u, buf, m, ident):
    gather, scatter, reduce = u is not None, buf is not None, m is not None
    n, w = (u if gather else buf).shape[-2:]
    ins = [a for a in (u, buf, m) if a is not None]
    outs, scratch = [], []
    copies = 0
    if gather:
        outs.append(jax.ShapeDtypeStruct((2, 2, RING, RING, 4, n, w), f32))
        outs.append(jax.ShapeDtypeStruct((RING, 2, 2, n, w), f32))
        copies += 2 * 24 + 3
    if scatter:
        outs.append(jax.ShapeDtypeStruct((2, 4, n, w), f32))
        scratch += [
            pltpu.VMEM((2, RING, RING, 4, n, w), f32),
            pltpu.VMEM((2, RING, RING, 4, n, w), f32),
            pltpu.VMEM((2, 2, RING, 2, n, w), f32),
            pltpu.VMEM((2, 2, RING, 4, n, w), f32),
            pltpu.VMEM((2, 2, 2, n, w), f32),
            pltpu.VMEM((2, 2, 4, n, w), f32),
        ]
        copies += 2 * 12
    if reduce:
        half = (m.shape[0] // 2, m.shape[1])
        outs.append(jax.ShapeDtypeStruct(m.shape, f32))
        scratch += [pltpu.VMEM((4,) + half, f32), pltpu.VMEM((3, 3) + half, f32), pltpu.VMEM(half, f32)]
        copies += 11
    scratch += [pltpu.SemaphoreType.DMA((copies,))] * 2 + [pltpu.SemaphoreType.DMA((3,))]
    vm = pl.BlockSpec(memory_space=pltpu.VMEM)
    return pl.pallas_call(
        functools.partial(exchange_kernel, gather, scatter, reduce),
        out_shape=outs,
        in_specs=[vm] * len(ins),
        out_specs=[vm] * len(outs),
        scratch_shapes=scratch,
        compiler_params=pltpu.CompilerParams(
            collective_id=ident, has_side_effects=True, vmem_limit_bytes=40 << 20
        ),
        name=f"exchange{ident}",
    )(*ins)


def split(a):
    top = a.astype(bf16)
    return top, (a - top.astype(f32)).astype(bf16)


def dot3(a, b, dims):
    dot = functools.partial(
        lax.dot_general, dimension_numbers=(dims, ((), ())), preferred_element_type=f32
    )
    return dot(a[0], b[0]) + (dot(a[0], b[1]) + dot(a[1], b[0]))


ROWS = ((1,), (1,))
COLS = ((1,), (0,))


def joined(ref, *idx):
    return jnp.concatenate([ref[idx[0], 0, idx[1]], ref[idx[0], 1, idx[1]]], axis=0)


def place(slot):
    return lax.rem(slot // 4, 2), (slot // 8) * 4 + lax.rem(slot, 4)


def fetch_tables(col_hbm, cols, sem):
    first = (lax.axis_index("group") * 32 + lax.axis_index("bulk")) * 4
    d = pltpu.make_async_copy(col_hbm.at[pl.ds(first, 4)], cols, sem)
    d.start()
    d.wait()
    return first


def returned_products(u, off, cols, load, first, base, buf, target):
    def zero(i, _):
        buf[0, 0, i] = jnp.zeros(buf.shape[3:], f32)
        buf[0, 1, i] = jnp.zeros(buf.shape[3:], f32)
        buf[1, 0, i] = jnp.zeros(buf.shape[3:], f32)
        buf[1, 1, i] = jnp.zeros(buf.shape[3:], f32)
        return 0

    lax.fori_loop(0, buf.shape[2], zero, 0)
    n = u.shape[2]

    def row(s, _):
        v = split(jnp.concatenate([u[0, s], u[1, s]], axis=0))
        for t in range(off.shape[1]):
            live = (t < load[first + s]).astype(f32)
            p = dot3(v, split(off[s, t]), COLS) * live
            c, i = place(target(cols[s, t]) - base)
            buf[c, 0, i] = buf[c, 0, i] + p[:n]
            buf[c, 1, i] = buf[c, 1, i] + p[n:]
        return 0

    lax.fori_loop(0, off.shape[0], row, 0)


def returned_kernel(col_hbm, load, u, off, buf, cols, sem):
    first = fetch_tables(col_hbm, cols, sem)
    base = lax.axis_index("group") * 128
    returned_products(u, off, cols, load, first, base, buf, lambda a: a)


def own_products(s, panel, border, u, diag, coup, off, cols, load, first, base):
    v = split(jnp.concatenate([u[0, s], u[1, s]], axis=0))
    rest = dot3(v, split(diag[s]), ROWS)
    tiles = jnp.zeros_like(rest)
    for t in range(off.shape[1]):
        live = (t < load[first + s]).astype(f32)
        c, i = place(cols[s, t] - base)
        tiles = tiles + dot3(split(joined(panel, c, i)), split(off[s, t]), ROWS) * live
    return tiles, rest


def crossed(s, border, coup):
    out = None
    for h in range(coup.shape[1]):
        v = split(jnp.concatenate([border[h, 0, s], border[h, 1, s]], axis=0))
        p = dot3(v, split(coup[s, h]), ROWS)
        out = p if out is None else out + p
    return out


def gram(a, b):
    return lax.dot_general(a, b, (ROWS, ((), ())), precision=highest, preferred_element_type=f32)


def first_kernel(col_hbm, load, panel, border, owed, u, diag, coup, off, u1, g, cols, cross, sem):
    first = fetch_tables(col_hbm, cols, sem)
    base = lax.axis_index("group") * 128
    n = u.shape[2]
    cross[...] = jnp.zeros_like(cross)
    for s in range(coup.shape[0]):
        cross[s] = crossed(s, border, coup)
    g[...] = jnp.zeros_like(g)

    def row(s, _):
        tiles, rest = own_products(s, panel, border, u, diag, coup, off, cols, load, first, base)
        w = tiles + rest + cross[s] + jnp.concatenate([owed[0, s], owed[1, s]], axis=0)
        u1[0, s] = w[:n]
        u1[1, s] = w[n:]
        x = jnp.concatenate([u[0, s], u[1, s], w], axis=0)
        g[...] += gram(x, x)
        return 0

    lax.fori_loop(0, off.shape[0], row, 0)


def second_kernel(col_hbm, load, moved, panel, border, u, diag, coup, off, buf, g, cols, cross, sem):
    first = fetch_tables(col_hbm, cols, sem)
    base = lax.axis_index("group") * 128
    n = u.shape[2]
    returned_products(u, off, cols, load, first, base, buf, lambda a: moved[a])
    cross[...] = jnp.zeros_like(cross)
    for s in range(coup.shape[0]):
        cross[s] = crossed(s, border, coup)

    def row(s, total):
        tiles, rest = own_products(s, panel, border, u, diag, coup, off, cols, load, first, base)
        rest = rest + cross[s]
        w = tiles + rest
        c, i = place(moved[first + s] - base)
        buf[c, 0, i] = buf[c, 0, i] + w[:n]
        buf[c, 1, i] = buf[c, 1, i] + w[n:]
        return total + gram(jnp.concatenate([u[0, s], u[1, s]], axis=0), w + tiles)

    total = lax.fori_loop(0, off.shape[0], row, jnp.zeros((2 * n, 2 * n), f32))
    g[...] = jnp.concatenate([total[:n], total[n:]], axis=1)


def last_kernel(moved, p0, p1, owed, weights, sol, res):
    first = (lax.axis_index("group") * 32 + lax.axis_index("bulk")) * 4
    base = lax.axis_index("group") * 128
    half = sol.shape[1]
    for s in range(sol.shape[0]):
        c, i = place(moved[first + s] - base)
        x = jnp.concatenate([joined(p0, c, i), joined(p1, c, i), owed[0, s], owed[1, s]], axis=0)
        out = lax.dot_general(
            weights[...], x, (COLS, ((), ())), precision=highest, preferred_element_type=f32
        )
        sol[s] = out[:half]
        res[s] = out[half:]


def chol_apply(matrix, right):
    factor = jnp.linalg.cholesky(matrix)
    middle = lax.linalg.triangular_solve(factor, right, left_side=True, lower=True)
    return lax.linalg.triangular_solve(factor, middle, left_side=True, lower=True, transpose_a=True)


def sym(m):
    return 0.5 * (m + m.T)


def mm(a, b):
    return jnp.dot(a, b, precision=highest)


def coefficients(n0, n1, n2, n3):
    n = n0.shape[0]
    eye = jnp.eye(n, dtype=n0.dtype)
    n0, n1, n2, n3 = sym(n0), sym(n1), sym(n2), sym(n3)
    delta = chol_apply(shift * n0 + n1, n1)
    alpha = (eye - delta) / shift
    b = -alpha
    cross = mm(delta.T, mm(n1, b))
    gram_new = sym(mm(delta.T, mm(n0, delta)) + cross + cross.T + mm(b.T, mm(n2, b)))
    beta = chol_apply(n0, gram_new)
    a = delta + beta
    c1 = mm(a.T, mm(n1, b))
    c2 = mm(a.T, mm(n2, b))
    pp = mm(a.T, mm(n0, a)) + c1 + c1.T + mm(b.T, mm(n2, b))
    pep = mm(a.T, mm(n1, a)) + c2 + c2.T + mm(b.T, mm(n3, b))
    alpha2 = chol_apply(sym(shift * pp + pep), gram_new)
    ba = mm(b, alpha2)
    aa = mm(a, alpha2)
    sol = (alpha + aa, ba, jnp.zeros_like(ba))
    res = (delta - shift * aa, b - shift * ba - aa, -ba)
    return jnp.concatenate(
        [jnp.concatenate(sol, axis=0), jnp.concatenate(res, axis=0)], axis=1
    ).T


def local(rhs, diag, off, coup, col_index, load, new_slot):
    rows, n2, w = rhs.shape
    n = n2 // 2
    offs = off.shape[1]
    vm = pl.BlockSpec(memory_space=pltpu.VMEM)
    sm = pl.BlockSpec(memory_space=pltpu.SMEM)
    anys = pl.BlockSpec(memory_space=pl.ANY)
    params = pltpu.CompilerParams(vmem_limit_bytes=40 << 20)
    tables = [pltpu.SMEM((rows, offs), jnp.int32)]
    cross = [pltpu.VMEM((rows, n2, w), f32)]
    sem = [pltpu.SemaphoreType.DMA(())]
    panel_shape = (2, 2, RING, RING, 4, n, w)
    flat = (2, 2, RING * RING * 4, n, w)
    row_shape = jax.ShapeDtypeStruct((2, rows, n, w), f32)
    u0 = rhs.reshape(rows, 2, n, w).transpose(1, 0, 2, 3)

    buf = pl.pallas_call(
        returned_kernel,
        out_shape=jax.ShapeDtypeStruct(flat, f32),
        in_specs=[anys, sm, vm, vm],
        out_specs=vm,
        scratch_shapes=tables + sem,
        compiler_params=params,
        name="returned",
    )(col_index, load, u0, off)
    p0, border0, owed = exchange(u0, buf.reshape(panel_shape), None, 0)
    u1, g01 = pl.pallas_call(
        first_kernel,
        out_shape=[row_shape, jax.ShapeDtypeStruct((2 * n2, 2 * n2), f32)],
        in_specs=[anys, sm] + [vm] * 7,
        out_specs=[vm, vm],
        scratch_shapes=tables + cross + sem,
        compiler_params=params,
        name="first",
    )(col_index, load, p0.reshape(flat), border0, owed, u0, diag, coup, off)
    p1, border1, g01 = exchange(u1, None, g01, 1)
    buf, g3 = pl.pallas_call(
        second_kernel,
        out_shape=[
            jax.ShapeDtypeStruct(flat, f32),
            jax.ShapeDtypeStruct((n, 2 * n2), f32),
        ],
        in_specs=[anys, sm, sm] + [vm] * 6,
        out_specs=[vm, vm],
        scratch_shapes=tables + cross + sem,
        compiler_params=params,
        name="second",
    )(col_index, load, new_slot, p1.reshape(flat), border1, u1, diag, coup, off)
    owed, g3 = exchange(None, buf.reshape(panel_shape), g3, 2)
    n3 = jnp.concatenate([g3[:, :n2], g3[:, n2:]], axis=0)
    weights = coefficients(g01[:n2, :n2], g01[:n2, n2:], g01[n2:, n2:], n3)
    sol, res = pl.pallas_call(
        last_kernel,
        out_shape=[jax.ShapeDtypeStruct(rhs.shape, f32)] * 2,
        in_specs=[sm] + [vm] * 4,
        out_specs=[vm, vm],
        compiler_params=params,
        name="last",
    )(new_slot, p0.reshape(flat), p1.reshape(flat), owed, weights)
    return sol, res


def solution(mesh):
    return jax.shard_map(
        local,
        mesh=mesh,
        in_specs=(
            P(("group", "bulk"), None, None),
            P(("group", "bulk"), None, None),
            P(("group", "bulk"), None, None, None),
            P(("group", "bulk"), None, None, None),
            P(),
            P(),
            P(),
        ),
        out_specs=(P(("group", "bulk"), None, None), P(("group", "bulk"), None, None)),
        check_vma=False,
    )
```

```python
import functools

import jax
import jax.numpy as jnp
from jax import lax
from jax.experimental import pallas as pl
from jax.experimental.pallas import tpu as pltpu
from jax.sharding import PartitionSpec as P

highest = lax.Precision.HIGHEST
shift = 4.0
f32 = jnp.float32
bf16 = jnp.bfloat16
RING = 4
MESH = pl.DeviceIdType.MESH


class Net:
    def __init__(self, send, recv):
        self.g = lax.axis_index("group")
        b = lax.axis_index("bulk")
        self.c = lax.rem(b, 2)
        self.y = lax.rem(b // 2, RING)
        self.z = b // (2 * RING)
        self.send, self.recv = send, recv
        self.count = 0
        self.pending = []

    def device(self, dx=0, dy=0, dz=0, partner=False):
        c = 1 - self.c if partner else self.c
        y = lax.rem(self.y + dy, RING)
        z = lax.rem(self.z + dz, RING)
        return (lax.rem(self.g + dx, RING), (z * RING + y) * 2 + c)

    def copy(self, src, dst, device):
        i = self.count
        self.count += 1
        d = pltpu.make_async_remote_copy(
            src_ref=src,
            dst_ref=dst,
            send_sem=self.send.at[i],
            recv_sem=self.recv.at[i],
            device_id=device,
            device_id_type=MESH,
        )
        d.start()
        self.pending.append(d)
        return d

    def drain(self):
        for d in self.pending:
            d.wait_send()


def plus(a, k):
    return lax.rem(a + k, RING)


def greet(net, devices):
    barrier = pltpu.get_barrier_semaphore()
    for d in devices:
        pl.semaphore_signal(barrier, inc=1, device_id=d, device_id_type=MESH)
    pl.semaphore_wait(barrier, len(devices))


def gather_steps(net, j, u, panel, local_sem):
    c, y, z = net.c, net.y, net.z
    f0, s0 = (y, z) if j == 0 else (z, y)

    def unit(fi, si):
        return panel.at[c, j, si, fi] if j == 0 else panel.at[c, j, fi, si]

    def column(si):
        return panel.at[c, j, si] if j == 0 else panel.at[c, j, :, si]

    def to(df, ds):
        return net.device(dy=df, dz=ds) if j == 0 else net.device(dy=ds, dz=df)

    partner = net.device(partner=True)
    mine = unit(f0, s0)
    own = pltpu.make_async_copy(u.at[j], mine, local_sem)
    own.start()
    near = [net.copy(u.at[j], mine, to(k, 0)) for k in (1, 3)]
    ups = [net.copy(u.at[j], mine, to(0, 1))]
    downs = [net.copy(u.at[j], mine, to(0, 3))]
    far = net.copy(u.at[j], mine, to(2, 0))
    lo, hi = pl.ds(0, 2), pl.ds(2, 2)
    order = [f0, plus(f0, 3), plus(f0, 1), plus(f0, 2)]
    halves = []

    def pass_on(p):
        piece = unit(order[p], s0)
        ups.append(net.copy(piece, piece, to(0, 1)))
        downs.append(net.copy(piece, piece, to(0, 3)))

    def forward(p):
        ups[p].wait_recv()
        piece = unit(order[p], plus(s0, 3)).at[lo]
        halves.append(net.copy(piece, piece, to(0, 1)))
        downs[p].wait_recv()
        piece = unit(order[p], plus(s0, 1)).at[hi]
        halves.append(net.copy(piece, piece, to(0, 3)))

    def swap(k):
        return net.copy(column(plus(s0, k)), column(plus(s0, k)), partner)

    for p in (1, 2):
        yield
        near[p - 1].wait_recv()
        pass_on(p)
    yield
    forward(0)
    yield
    far.wait_recv()
    pass_on(3)
    piece = unit(order[3], s0)
    last = net.copy(piece, piece, to(0, 2))
    own.wait()
    swapped = [swap(0)]
    for p in (1, 2):
        yield
        forward(p)
    yield
    ups[3].wait_recv()
    swapped.append(swap(3))
    yield
    downs[3].wait_recv()
    swapped.append(swap(1))
    yield
    for d in halves:
        d.wait_recv()
    last.wait_recv()
    swapped.append(swap(2))
    for d in swapped:
        yield
        d.wait_recv()


def scatter_steps(net, j, buf, owed, r, t0, t1, t2, t3):
    c, y, z = net.c, net.y, net.z
    f0, s0 = (y, z) if j == 0 else (z, y)

    def column(ref, k):
        si = plus(s0, k)
        return ref.at[j, si] if j == 0 else ref.at[j, :, si]

    def to(df, ds):
        return net.device(dy=df, dz=ds) if j == 0 else net.device(dy=ds, dz=df)

    partner = net.device(partner=True)
    lo, hi = pl.ds(0, 2), pl.ds(2, 2)
    order = [2, 1, 3, 0]
    rows = {k: plus(f0, k) for k in range(RING)}
    first = {}
    for k in order:
        first[k] = net.copy(column(buf.at[1 - c], k), column(t0, k), partner)
    cols = {k: column(r, k) for k in range(RING)}

    def start(k):
        a, b = column(buf.at[c], k), column(t0, k)
        for i in order:
            cols[k][rows[i]] = a[rows[i]] + b[rows[i]]

    yield
    first[2].wait_recv()
    start(2)
    ups = {i: net.copy(cols[2].at[rows[i], lo], t1.at[j, 0, rows[i]], to(0, 1)) for i in order}
    downs = {i: net.copy(cols[2].at[rows[i], hi], t1.at[j, 1, rows[i]], to(0, 3)) for i in order}
    yield
    first[1].wait_recv()
    start(1)
    yield
    first[3].wait_recv()
    start(3)
    yield
    first[0].wait_recv()
    start(0)
    ups2, downs2 = {}, {}
    for i in order:
        q = rows[i]
        yield
        ups[i].wait_recv()
        cols[1][q, lo] = cols[1][q, lo] + t1[j, 0, q]
        ups2[i] = net.copy(cols[1].at[q], t2.at[j, 0, q], to(0, 1))
        downs[i].wait_recv()
        cols[3][q, hi] = cols[3][q, hi] + t1[j, 1, q]
        downs2[i] = net.copy(cols[3].at[q], t2.at[j, 1, q], to(0, 3))
    sent = []
    for i in order:
        q = rows[i]
        yield
        ups2[i].wait_recv()
        downs2[i].wait_recv()
        cols[0][q] = cols[0][q] + (t2[j, 0, q] + t2[j, 1, q])
        if i:
            sent.append(net.copy(cols[0].at[q], t3.at[j, i - 1], to(i, 0)))
    for d in sent:
        yield
        d.wait_recv()
    owed[j] = (cols[0][rows[0]] + t3[j, 0]) + (t3[j, 1] + t3[j, 2])


def border_steps(net, u, border, local_sem):
    src = u.at[:, pl.ds(0, 2)]
    own = pltpu.make_async_copy(src, border.at[net.g], local_sem)
    own.start()
    sent = [net.copy(src, border.at[net.g], net.device(dx=k)) for k in (1, 3, 2)]
    yield
    own.wait()
    for d in sent:
        d.wait_recv()


def reduce_steps(net, m, out, acc, slots, halves):
    c = net.c
    rows = acc.shape[1]
    partner = net.device(partner=True)
    d = net.copy(m.at[pl.ds((1 - c) * rows, rows)], halves, partner)
    yield
    d.wait_recv()
    acc[0] = m[pl.ds(c * rows, rows)] + halves[...]
    for t in range(3):
        sent = []
        for k in (1, 3, 2):
            step = [0, 0, 0]
            step[t] = k * (1 - c)
            step[(t + 1) % 3] = step[(t + 1) % 3] + k * c
            sent.append(
                net.copy(acc.at[t], slots.at[t, k - 1], net.device(step[0], step[1], step[2]))
            )
        yield
        for d in sent:
            d.wait_recv()
        acc[t + 1] = (acc[t] + slots[t, 0]) + (slots[t, 1] + slots[t, 2])
    out[pl.ds(c * rows, rows)] = acc[3]
    d = net.copy(acc.at[3], out.at[pl.ds(c * rows, rows)], partner)
    yield
    d.wait_recv()


def run(steps):
    steps = list(steps)
    while steps:
        left = []
        for s in steps:
            try:
                next(s)
                left.append(s)
            except StopIteration:
                pass
        steps = left


def exchange_kernel(gather, scatter, reduce, *refs):
    refs = list(refs)
    u = refs.pop(0) if gather else None
    buf = refs.pop(0) if scatter else None
    m = refs.pop(0) if reduce else None
    panel = refs.pop(0) if gather else None
    border = refs.pop(0) if gather else None
    owed = refs.pop(0) if scatter else None
    total = refs.pop(0) if reduce else None
    parts = [refs.pop(0) for _ in range(5)] if scatter else None
    work = [refs.pop(0) for _ in range(3)] if reduce else None
    send, recv, local_sems = refs
    net = Net(send, recv)
    devices = [net.device(partner=True)]
    devices += [net.device(dy=k) for k in (2, 1, 3)] + [net.device(dz=k) for k in (2, 1, 3)]
    if gather or reduce:
        devices += [net.device(dx=k) for k in (2, 1, 3)]
    greet(net, devices)
    steps = []
    if reduce:
        steps.append(reduce_steps(net, m, total, *work))
    if scatter:
        steps += [scatter_steps(net, j, buf, owed, *parts) for j in range(2)]
    if gather:
        steps += [gather_steps(net, j, u, panel, local_sems.at[j]) for j in range(2)]
        steps.append(border_steps(net, u, border, local_sems.at[2]))
    run(steps)
    net.drain()


def exchange(u, buf, m, ident):
    gather, scatter, reduce = u is not None, buf is not None, m is not None
    n, w = (u if gather else buf if scatter else m).shape[-2:]
    ins = [a for a in (u, buf, m) if a is not None]
    outs, scratch = [], []
    copies = 0
    if gather:
        outs.append(jax.ShapeDtypeStruct((2, 2, RING, RING, 4, n, w), f32))
        outs.append(jax.ShapeDtypeStruct((RING, 2, 2, n, w), f32))
        copies += 2 * 24 + 3
    if scatter:
        outs.append(jax.ShapeDtypeStruct((2, 4, n, w), f32))
        scratch += [
            pltpu.VMEM((2, RING, RING, 4, n, w), f32),
            pltpu.VMEM((2, RING, RING, 4, n, w), f32),
            pltpu.VMEM((2, 2, RING, 2, n, w), f32),
            pltpu.VMEM((2, 2, RING, 4, n, w), f32),
            pltpu.VMEM((2, 3, 4, n, w), f32),
        ]
        copies += 2 * 23
    if reduce:
        half = (m.shape[0] // 2, m.shape[1])
        outs.append(jax.ShapeDtypeStruct(m.shape, f32))
        scratch += [pltpu.VMEM((4,) + half, f32), pltpu.VMEM((3, 3) + half, f32), pltpu.VMEM(half, f32)]
        copies += 11
    scratch += [pltpu.SemaphoreType.DMA((copies,))] * 2 + [pltpu.SemaphoreType.DMA((3,))]
    vm = pl.BlockSpec(memory_space=pltpu.VMEM)
    return pl.pallas_call(
        functools.partial(exchange_kernel, gather, scatter, reduce),
        out_shape=outs,
        in_specs=[vm] * len(ins),
        out_specs=[vm] * len(outs),
        scratch_shapes=scratch,
        compiler_params=pltpu.CompilerParams(
            collective_id=ident, has_side_effects=True, vmem_limit_bytes=40 << 20
        ),
        name=f"exchange{ident}",
    )(*ins)


def split(a):
    top = a.astype(bf16)
    return top, (a - top.astype(f32)).astype(bf16)


def dot3(a, b, dims):
    dot = functools.partial(
        lax.dot_general, dimension_numbers=(dims, ((), ())), preferred_element_type=f32
    )
    return dot(a[0], b[0]) + (dot(a[0], b[1]) + dot(a[1], b[0]))


ROWS = ((1,), (1,))
COLS = ((1,), (0,))


def joined(ref, *idx):
    return jnp.concatenate([ref[idx[0], 0, idx[1]], ref[idx[0], 1, idx[1]]], axis=0)


def place(slot):
    return lax.rem(slot // 4, 2), (slot // 8) * 4 + lax.rem(slot, 4)


def fetch_tables(col_hbm, cols, sem):
    first = (lax.axis_index("group") * 32 + lax.axis_index("bulk")) * 4
    d = pltpu.make_async_copy(col_hbm.at[pl.ds(first, 4)], cols, sem)
    d.start()
    d.wait()
    return first


def returned_products(u, off, cols, load, first, base, buf, target):
    def zero(i, _):
        buf[0, 0, i] = jnp.zeros(buf.shape[3:], f32)
        buf[0, 1, i] = jnp.zeros(buf.shape[3:], f32)
        buf[1, 0, i] = jnp.zeros(buf.shape[3:], f32)
        buf[1, 1, i] = jnp.zeros(buf.shape[3:], f32)
        return 0

    lax.fori_loop(0, buf.shape[2], zero, 0)
    n = u.shape[2]

    def row(s, _):
        v = split(jnp.concatenate([u[0, s], u[1, s]], axis=0))
        for t in range(off.shape[1]):
            live = (t < load[first + s]).astype(f32)
            p = dot3(v, split(off[s, t]), COLS) * live
            c, i = place(target(cols[s, t]) - base)
            buf[c, 0, i] = buf[c, 0, i] + p[:n]
            buf[c, 1, i] = buf[c, 1, i] + p[n:]
        return 0

    lax.fori_loop(0, off.shape[0], row, 0)


def returned_kernel(col_hbm, load, u, off, buf, cols, sem):
    first = fetch_tables(col_hbm, cols, sem)
    base = lax.axis_index("group") * 128
    returned_products(u, off, cols, load, first, base, buf, lambda a: a)


def own_products(s, panel, border, u, diag, coup, off, cols, load, first, base):
    v = split(jnp.concatenate([u[0, s], u[1, s]], axis=0))
    rest = dot3(v, split(diag[s]), ROWS)
    tiles = jnp.zeros_like(rest)
    for t in range(off.shape[1]):
        live = (t < load[first + s]).astype(f32)
        c, i = place(cols[s, t] - base)
        tiles = tiles + dot3(split(joined(panel, c, i)), split(off[s, t]), ROWS) * live
    return tiles, rest


def crossed(s, border, coup):
    out = None
    for h in range(coup.shape[1]):
        v = split(jnp.concatenate([border[h, 0, s], border[h, 1, s]], axis=0))
        p = dot3(v, split(coup[s, h]), ROWS)
        out = p if out is None else out + p
    return out


def gram(a, b):
    return lax.dot_general(a, b, (ROWS, ((), ())), precision=highest, preferred_element_type=f32)


def first_kernel(col_hbm, load, panel, border, owed, u, diag, coup, off, u1, g, cols, cross, sem):
    first = fetch_tables(col_hbm, cols, sem)
    base = lax.axis_index("group") * 128
    n = u.shape[2]
    cross[...] = jnp.zeros_like(cross)
    for s in range(coup.shape[0]):
        cross[s] = crossed(s, border, coup)
    g[...] = jnp.zeros_like(g)

    def row(s, _):
        tiles, rest = own_products(s, panel, border, u, diag, coup, off, cols, load, first, base)
        w = tiles + rest + cross[s] + jnp.concatenate([owed[0, s], owed[1, s]], axis=0)
        u1[0, s] = w[:n]
        u1[1, s] = w[n:]
        x = jnp.concatenate([u[0, s], u[1, s], w], axis=0)
        g[...] += gram(x, x)
        return 0

    lax.fori_loop(0, off.shape[0], row, 0)


def second_kernel(col_hbm, load, moved, panel, border, u, diag, coup, off, buf, g, cols, cross, sem):
    first = fetch_tables(col_hbm, cols, sem)
    base = lax.axis_index("group") * 128
    n = u.shape[2]
    returned_products(u, off, cols, load, first, base, buf, lambda a: moved[a])
    cross[...] = jnp.zeros_like(cross)
    for s in range(coup.shape[0]):
        cross[s] = crossed(s, border, coup)

    def row(s, total):
        tiles, rest = own_products(s, panel, border, u, diag, coup, off, cols, load, first, base)
        rest = rest + cross[s]
        w = tiles + rest
        c, i = place(moved[first + s] - base)
        buf[c, 0, i] = buf[c, 0, i] + w[:n]
        buf[c, 1, i] = buf[c, 1, i] + w[n:]
        return total + gram(jnp.concatenate([u[0, s], u[1, s]], axis=0), w + tiles)

    total = lax.fori_loop(0, off.shape[0], row, jnp.zeros((2 * n, 2 * n), f32))
    g[...] = jnp.concatenate([total[:n], total[n:]], axis=1)


def solve(m, r):
    n = m.shape[0]
    t = jnp.concatenate([m, r], axis=1)
    blocks = [t[8 * i : 8 * i + 8] for i in range(n // 8)]
    shape = blocks[0].shape
    row_id = lax.broadcasted_iota(jnp.int32, shape, 0)
    for b in range(n // 8):
        piv = blocks[b]
        rows = [jnp.broadcast_to(piv[i : i + 1], shape) for i in range(8)]
        lanes = [jnp.broadcast_to(piv[:, 8 * b + i : 8 * b + i + 1], shape) for i in range(8)]
        d = [[jnp.broadcast_to(lanes[q][i : i + 1], shape) for q in range(8)] for i in range(8)]
        for i in range(8):
            inv = 1.0 / d[i][i]
            rows[i] = rows[i] * inv
            for q in range(i + 1, 8):
                d[i][q] = d[i][q] * inv
            for k in range(8):
                if k != i:
                    factor = d[k][i]
                    rows[k] = rows[k] - factor * rows[i]
                    for q in range(i + 1, 8):
                        d[k][q] = d[k][q] - factor * d[i][q]
        new = rows[0]
        for i in range(1, 8):
            new = jnp.where(row_id == i, rows[i], new)
        for k in range(n // 8):
            if k != b:
                acc = blocks[k]
                for i in range(8):
                    column = blocks[k][:, 8 * b + i : 8 * b + i + 1]
                    acc = acc - jnp.broadcast_to(column, shape) * rows[i]
                blocks[k] = acc
        blocks[b] = new
        yield
    return jnp.concatenate(blocks, axis=0)[:, n:]


def both(*solves):
    out = [None] * len(solves)
    left = list(range(len(solves)))
    while left:
        for i in list(left):
            try:
                next(solves[i])
            except StopIteration as e:
                out[i] = e.value
                left.remove(i)
        yield
    return out


def finish(steps):
    while True:
        try:
            next(steps)
        except StopIteration as e:
            return e.value


def mm(a, b):
    return lax.dot_general(a, b, (COLS, ((), ())), precision=highest, preferred_element_type=f32)


def tmm(a, b):
    return lax.dot_general(
        a, b, (((0,), (0,)), ((), ())), precision=highest, preferred_element_type=f32
    )


def first_coefficients(g):
    n = g.shape[0] // 2
    g = 0.5 * (g + g.T)
    n0, n1, n2 = g[:n, :n], 0.5 * (g[:n, n:] + g[n:, :n]), g[n:, n:]
    eye = (
        lax.broadcasted_iota(jnp.int32, (n, n), 0) == lax.broadcasted_iota(jnp.int32, (n, n), 1)
    ).astype(f32)
    delta, inverse = yield from both(solve(shift * n0 + n1, n1), solve(n0, eye))
    b = (delta - eye) * (1.0 / shift)
    yield
    n1b, n2b, n0d = mm(n1, b), mm(n2, b), mm(n0, delta)
    yield
    bb = tmm(b, n2b)
    fresh = tmm(delta, n0d) + (tmm(delta, n1b) + tmm(n1b, delta)) + bb
    yield
    a = delta + mm(inverse, fresh)
    yield
    pp = tmm(a, mm(n0, a)) + (tmm(a, n1b) + tmm(n1b, a)) + bb
    pep = tmm(a, mm(n1, a)) + (tmm(a, n2b) + tmm(n2b, a))
    yield
    return delta, a, fresh, shift * pp + pep


def coefficient_kernel(g, g3, w):
    n = g.shape[0] // 2
    delta, a, fresh, known = finish(first_coefficients(g[...]))
    n3 = jnp.concatenate([g3[:, :n], g3[:, n:]], axis=0)
    eye = (
        lax.broadcasted_iota(jnp.int32, (n, n), 0) == lax.broadcasted_iota(jnp.int32, (n, n), 1)
    ).astype(f32)
    b = (delta - eye) * (1.0 / shift)
    n3b = mm(n3, b)
    pq = known + 0.5 * (tmm(b, n3b) + tmm(n3b, b))
    alpha2 = finish(solve(pq, fresh))
    ba, aa = mm(b, alpha2), mm(a, alpha2)
    w[0:n] = jnp.concatenate([aa - b, delta - shift * aa], axis=1)
    w[n : 2 * n] = jnp.concatenate([ba, b - shift * ba - aa], axis=1)
    w[2 * n :] = jnp.concatenate([jnp.zeros_like(ba), -ba], axis=1)


def last_kernel(moved, p0, p1, owed, weights, sol, res, basis, sems):
    first = (lax.axis_index("group") * 32 + lax.axis_index("bulk")) * 4
    base = lax.axis_index("group") * 128
    half = sol.shape[1]
    n = half // 2
    copies = []
    for s in range(sol.shape[0]):
        c, i = place(moved[first + s] - base)
        for k, p in enumerate((p0, p1)):
            for j in range(2):
                dst = basis.at[s, pl.ds((2 * k + j) * n, n)]
                d = pltpu.make_async_copy(p.at[c, j, i], dst, sems.at[s, 2 * k + j])
                d.start()
                copies.append(d)
    for d in copies:
        d.wait()
    for s in range(sol.shape[0]):
        x = jnp.concatenate([basis[s], owed[0, s], owed[1, s]], axis=0)
        out = tmm(weights[...], x)
        sol[s] = out[:half]
        res[s] = out[half:]


def local(rhs, diag, off, coup, col_index, load, new_slot):
    rows, n2, w = rhs.shape
    n = n2 // 2
    offs = off.shape[1]
    vm = pl.BlockSpec(memory_space=pltpu.VMEM)
    sm = pl.BlockSpec(memory_space=pltpu.SMEM)
    anys = pl.BlockSpec(memory_space=pl.ANY)
    params = pltpu.CompilerParams(vmem_limit_bytes=40 << 20)
    tables = [pltpu.SMEM((rows, offs), jnp.int32)]
    cross = [pltpu.VMEM((rows, n2, w), f32)]
    sem = [pltpu.SemaphoreType.DMA(())]
    panel_shape = (2, 2, RING, RING, 4, n, w)
    flat = (2, 2, RING * RING * 4, n, w)
    row_shape = jax.ShapeDtypeStruct((2, rows, n, w), f32)
    u0 = rhs.reshape(rows, 2, n, w).transpose(1, 0, 2, 3)

    buf = pl.pallas_call(
        returned_kernel,
        out_shape=jax.ShapeDtypeStruct(flat, f32),
        in_specs=[anys, sm, vm, vm],
        out_specs=vm,
        scratch_shapes=tables + sem,
        compiler_params=params,
        name="returned",
    )(col_index, load, u0, off)
    p0, border0, owed = exchange(u0, buf.reshape(panel_shape), None, 0)
    u1, g01 = pl.pallas_call(
        first_kernel,
        out_shape=[row_shape, jax.ShapeDtypeStruct((2 * n2, 2 * n2), f32)],
        in_specs=[anys, sm] + [vm] * 7,
        out_specs=[vm, vm],
        scratch_shapes=tables + cross + sem,
        compiler_params=params,
        name="first",
    )(col_index, load, p0.reshape(flat), border0, owed, u0, diag, coup, off)
    p1, border1, g01 = exchange(u1, None, g01, 1)
    buf, g3 = pl.pallas_call(
        second_kernel,
        out_shape=[
            jax.ShapeDtypeStruct(flat, f32),
            jax.ShapeDtypeStruct((n, 2 * n2), f32),
        ],
        in_specs=[anys, sm, sm] + [vm] * 6,
        out_specs=[vm, vm],
        scratch_shapes=tables + cross + sem,
        compiler_params=params,
        name="second",
    )(col_index, load, new_slot, p1.reshape(flat), border1, u1, diag, coup, off)
    owed, g3 = exchange(None, buf.reshape(panel_shape), g3, 2)
    weights = pl.pallas_call(
        coefficient_kernel,
        out_shape=jax.ShapeDtypeStruct((3 * n2, 2 * n2), f32),
        in_specs=[vm, vm],
        out_specs=vm,
        name="coefficients",
    )(g01, g3)
    sol, res = pl.pallas_call(
        last_kernel,
        out_shape=[jax.ShapeDtypeStruct(rhs.shape, f32)] * 2,
        in_specs=[sm, anys, anys, vm, vm],
        out_specs=[vm, vm],
        scratch_shapes=[
            pltpu.VMEM((rows, 2 * n2, w), f32),
            pltpu.SemaphoreType.DMA((rows, 4)),
        ],
        compiler_params=params,
        name="last",
    )(new_slot, p0.reshape(flat), p1.reshape(flat), owed, weights)
    return sol, res


def solution(mesh):
    return jax.shard_map(
        local,
        mesh=mesh,
        in_specs=(
            P(("group", "bulk"), None, None),
            P(("group", "bulk"), None, None),
            P(("group", "bulk"), None, None, None),
            P(("group", "bulk"), None, None, None),
            P(),
            P(),
            P(),
        ),
        out_specs=(P(("group", "bulk"), None, None), P(("group", "bulk"), None, None)),
        check_vma=False,
    )
```

```python
import functools

import jax
import jax.numpy as jnp
from jax import lax
from jax.experimental import pallas as pl
from jax.experimental.pallas import tpu as pltpu
from jax.sharding import PartitionSpec as P

highest = lax.Precision.HIGHEST
shift = 4.0
f32 = jnp.float32
bf16 = jnp.bfloat16
RING = 4
MESH = pl.DeviceIdType.MESH


class Net:
    def __init__(self, send, recv):
        self.g = lax.axis_index("group")
        b = lax.axis_index("bulk")
        self.c = lax.rem(b, 2)
        self.y = lax.rem(b // 2, RING)
        self.z = b // (2 * RING)
        self.send, self.recv = send, recv
        self.count = 0
        self.pending = []

    def device(self, dx=0, dy=0, dz=0, partner=False):
        c = 1 - self.c if partner else self.c
        y = lax.rem(self.y + dy, RING)
        z = lax.rem(self.z + dz, RING)
        return (lax.rem(self.g + dx, RING), (z * RING + y) * 2 + c)

    def copy(self, src, dst, device):
        i = self.count
        self.count += 1
        d = pltpu.make_async_remote_copy(
            src_ref=src,
            dst_ref=dst,
            send_sem=self.send.at[i],
            recv_sem=self.recv.at[i],
            device_id=device,
            device_id_type=MESH,
        )
        d.start()
        self.pending.append(d)
        return d

    def drain(self):
        for d in self.pending:
            d.wait_send()


def plus(a, k):
    return lax.rem(a + k, RING)


def greet(net, devices):
    barrier = pltpu.get_barrier_semaphore()
    for d in devices:
        pl.semaphore_signal(barrier, inc=1, device_id=d, device_id_type=MESH)
    pl.semaphore_wait(barrier, len(devices))


def gather_steps(net, j, u, panel, local_sem):
    c, y, z = net.c, net.y, net.z
    f0, s0 = (y, z) if j == 0 else (z, y)

    def unit(fi, si):
        return panel.at[c, j, si, fi] if j == 0 else panel.at[c, j, fi, si]

    def column(si):
        return panel.at[c, j, si] if j == 0 else panel.at[c, j, :, si]

    def to(df, ds):
        return net.device(dy=df, dz=ds) if j == 0 else net.device(dy=ds, dz=df)

    partner = net.device(partner=True)
    mine = unit(f0, s0)
    own = pltpu.make_async_copy(u.at[j], mine, local_sem)
    own.start()
    near = [net.copy(u.at[j], mine, to(k, 0)) for k in (1, 3)]
    ups = [net.copy(u.at[j], mine, to(0, 1))]
    downs = [net.copy(u.at[j], mine, to(0, 3))]
    far = net.copy(u.at[j], mine, to(2, 0))
    lo, hi = pl.ds(0, 2), pl.ds(2, 2)
    order = [f0, plus(f0, 3), plus(f0, 1), plus(f0, 2)]
    halves = []

    def pass_on(p):
        piece = unit(order[p], s0)
        ups.append(net.copy(piece, piece, to(0, 1)))
        downs.append(net.copy(piece, piece, to(0, 3)))

    def forward(p):
        ups[p].wait_recv()
        piece = unit(order[p], plus(s0, 3)).at[lo]
        halves.append(net.copy(piece, piece, to(0, 1)))
        downs[p].wait_recv()
        piece = unit(order[p], plus(s0, 1)).at[hi]
        halves.append(net.copy(piece, piece, to(0, 3)))

    def swap(k):
        return net.copy(column(plus(s0, k)), column(plus(s0, k)), partner)

    for p in (1, 2):
        yield
        near[p - 1].wait_recv()
        pass_on(p)
    yield
    forward(0)
    yield
    far.wait_recv()
    pass_on(3)
    piece = unit(order[3], s0)
    last = net.copy(piece, piece, to(0, 2))
    own.wait()
    swapped = [swap(0)]
    for p in (1, 2):
        yield
        forward(p)
    yield
    ups[3].wait_recv()
    swapped.append(swap(3))
    yield
    downs[3].wait_recv()
    swapped.append(swap(1))
    yield
    for d in halves:
        d.wait_recv()
    last.wait_recv()
    swapped.append(swap(2))
    for d in swapped:
        yield
        d.wait_recv()


def scatter_steps(net, j, owed, stage, r, t0, t1, t2, t3):
    y, z = net.y, net.z
    f0, s0 = (y, z) if j == 0 else (z, y)

    def column(ref, k):
        si = plus(s0, k)
        return ref.at[j, si] if j == 0 else ref.at[j, :, si]

    def to(df, ds):
        return net.device(dy=df, dz=ds) if j == 0 else net.device(dy=ds, dz=df)

    partner = net.device(partner=True)
    lo, hi = pl.ds(0, 2), pl.ds(2, 2)
    order = [2, 1, 3, 0]
    rows = {k: plus(f0, k) for k in range(RING)}
    first = {}
    for k in order:
        first[k] = net.copy(column(stage, k), column(t0, k), partner)
    cols = {k: column(r, k) for k in range(RING)}

    def start(k):
        b = column(t0, k)
        for i in order:
            cols[k][rows[i]] = cols[k][rows[i]] + b[rows[i]]

    yield
    first[2].wait_recv()
    start(2)
    ups = {i: net.copy(cols[2].at[rows[i], lo], t1.at[j, 0, rows[i]], to(0, 1)) for i in order}
    downs = {i: net.copy(cols[2].at[rows[i], hi], t1.at[j, 1, rows[i]], to(0, 3)) for i in order}
    yield
    first[1].wait_recv()
    start(1)
    yield
    first[3].wait_recv()
    start(3)
    yield
    first[0].wait_recv()
    start(0)
    ups2, downs2 = {}, {}
    for i in order:
        q = rows[i]
        yield
        ups[i].wait_recv()
        cols[1][q, lo] = cols[1][q, lo] + t1[j, 0, q]
        ups2[i] = net.copy(cols[1].at[q], t2.at[j, 0, q], to(0, 1))
        downs[i].wait_recv()
        cols[3][q, hi] = cols[3][q, hi] + t1[j, 1, q]
        downs2[i] = net.copy(cols[3].at[q], t2.at[j, 1, q], to(0, 3))
    sent = []
    for i in order:
        q = rows[i]
        yield
        ups2[i].wait_recv()
        downs2[i].wait_recv()
        cols[0][q] = cols[0][q] + (t2[j, 0, q] + t2[j, 1, q])
        if i:
            sent.append(net.copy(cols[0].at[q], t3.at[j, i - 1], to(i, 0)))
    for d in sent:
        yield
        d.wait_recv()
    owed[j] = (cols[0][rows[0]] + t3[j, 0]) + (t3[j, 1] + t3[j, 2])


def border_steps(net, u, border, local_sem):
    src = u.at[:, pl.ds(0, 2)]
    own = pltpu.make_async_copy(src, border.at[net.g], local_sem)
    own.start()
    sent = [net.copy(src, border.at[net.g], net.device(dx=k)) for k in (1, 3, 2)]
    yield
    own.wait()
    for d in sent:
        d.wait_recv()


def reduce_steps(net, m, out, acc, slots, halves):
    c = net.c
    rows = acc.shape[1]
    partner = net.device(partner=True)
    d = net.copy(m.at[pl.ds((1 - c) * rows, rows)], halves, partner)
    yield
    d.wait_recv()
    acc[0] = m[pl.ds(c * rows, rows)] + halves[...]
    for t in range(3):
        sent = []
        for k in (1, 3, 2):
            step = [0, 0, 0]
            step[t] = k * (1 - c)
            step[(t + 1) % 3] = step[(t + 1) % 3] + k * c
            sent.append(
                net.copy(acc.at[t], slots.at[t, k - 1], net.device(step[0], step[1], step[2]))
            )
        yield
        for d in sent:
            d.wait_recv()
        acc[t + 1] = (acc[t] + slots[t, 0]) + (slots[t, 1] + slots[t, 2])
    out[pl.ds(c * rows, rows)] = acc[3]
    d = net.copy(acc.at[3], out.at[pl.ds(c * rows, rows)], partner)
    yield
    d.wait_recv()


def run(steps):
    steps = list(steps)
    while steps:
        left = []
        for s in steps:
            try:
                next(s)
                left.append(s)
            except StopIteration:
                pass
        steps = left


def split(a):
    top = a.astype(bf16)
    return top, (a - top.astype(f32)).astype(bf16)


def dot3(a, b, dims):
    dot = functools.partial(
        lax.dot_general, dimension_numbers=(dims, ((), ())), preferred_element_type=f32
    )
    return dot(a[0], b[0]) + (dot(a[0], b[1]) + dot(a[1], b[0]))


ROWS = ((1,), (1,))
COLS = ((1,), (0,))


ROW_COUNT = 4
OFFS = 11
ENTRIES = ROW_COUNT * OFFS
PART_ROWS = 128
NONE = ENTRIES
OWN = ENTRIES + 1
FIRST = 0
SECOND = 2 * PART_ROWS
PLACE = SECOND + 3 * PART_ROWS
LIVE = PLACE + ENTRIES
MINE = LIVE + ENTRIES
SPARE = MINE + ROW_COUNT
TABLE = SPARE + 4


def position(slot):
    return lax.rem(slot // 4, 2) * 64 + (slot // 8) * 4 + lax.rem(slot, 4)


def table_kernel(col_hbm, load, moved, table, cols, sem):
    first = (lax.axis_index("group") * 32 + lax.axis_index("bulk")) * ROW_COUNT
    base = lax.axis_index("group") * PART_ROWS
    d = pltpu.make_async_copy(col_hbm.at[pl.ds(first, ROW_COUNT)], cols, sem)
    d.start()

    def clear(i, _):
        for k in range(5):
            table[k * PART_ROWS + i] = NONE
        return 0

    lax.fori_loop(0, PART_ROWS, clear, 0)
    for i in range(SPARE, TABLE):
        table[i] = NONE
    d.wait()
    for s in range(ROW_COUNT):
        live_count = load[first + s]
        target = position(moved[first + s] - base)
        table[SECOND + 2 * PART_ROWS + target] = OWN + s
        table[MINE + s] = target

        def entry(t, _):
            e = s * OFFS + t
            slot = cols[s, t]
            live = t < live_count
            p = position(slot - base)
            q = position(moved[slot] - base)
            table[PLACE + e] = p
            table[LIVE + e] = live.astype(jnp.int32)
            i = FIRST + p + jnp.where(table[FIRST + p] == NONE, 0, PART_ROWS)
            table[jnp.where(live, i, SPARE)] = e
            i = SECOND + q + jnp.where(table[SECOND + q] == NONE, 0, PART_ROWS)
            table[jnp.where(live, i, SPARE)] = e
            return 0

        lax.fori_loop(0, OFFS, entry, 0)


def gram(a, b):
    return lax.dot_general(a, b, (ROWS, ((), ())), precision=highest, preferred_element_type=f32)


def whole(ref, *idx):
    return jnp.concatenate([ref[(0,) + idx], ref[(1,) + idx]], axis=0)


def panel_row(panel, p):
    c, z = p // 64, lax.rem(p // 16, RING)
    y, k = lax.rem(p // 4, RING), lax.rem(p, 4)
    return jnp.concatenate([panel[c, 0, z, y, k], panel[c, 1, z, y, k]], axis=0)


def solve(m, r):
    n = m.shape[0]
    t = jnp.concatenate([m, r], axis=1)
    blocks = [t[8 * i : 8 * i + 8] for i in range(n // 8)]
    shape = blocks[0].shape
    row_id = lax.broadcasted_iota(jnp.int32, shape, 0)
    for b in range(n // 8):
        piv = blocks[b]
        rows = [jnp.broadcast_to(piv[i : i + 1], shape) for i in range(8)]
        lanes = [jnp.broadcast_to(piv[:, 8 * b + i : 8 * b + i + 1], shape) for i in range(8)]
        d = [[jnp.broadcast_to(lanes[q][i : i + 1], shape) for q in range(8)] for i in range(8)]
        for i in range(8):
            inv = 1.0 / d[i][i]
            rows[i] = rows[i] * inv
            for q in range(i + 1, 8):
                d[i][q] = d[i][q] * inv
            for k in range(8):
                if k != i:
                    factor = d[k][i]
                    rows[k] = rows[k] - factor * rows[i]
                    for q in range(i + 1, 8):
                        d[k][q] = d[k][q] - factor * d[i][q]
        new = rows[0]
        for i in range(1, 8):
            new = jnp.where(row_id == i, rows[i], new)
        for k in range(n // 8):
            if k != b:
                acc = blocks[k]
                for i in range(8):
                    column = blocks[k][:, 8 * b + i : 8 * b + i + 1]
                    acc = acc - jnp.broadcast_to(column, shape) * rows[i]
                blocks[k] = acc
        blocks[b] = new
        yield
    return jnp.concatenate(blocks, axis=0)[:, n:]


def both(*solves):
    out = [None] * len(solves)
    left = list(range(len(solves)))
    while left:
        for i in list(left):
            try:
                next(solves[i])
            except StopIteration as e:
                out[i] = e.value
                left.remove(i)
        yield
    return out


def finish(steps):
    while True:
        try:
            next(steps)
        except StopIteration as e:
            return e.value


def mm(a, b):
    return lax.dot_general(a, b, (COLS, ((), ())), precision=highest, preferred_element_type=f32)


def tmm(a, b):
    return lax.dot_general(
        a, b, (((0,), (0,)), ((), ())), precision=highest, preferred_element_type=f32
    )


def first_coefficients(g):
    n = g.shape[0] // 2
    g = 0.5 * (g + g.T)
    n0, n1, n2 = g[:n, :n], 0.5 * (g[:n, n:] + g[n:, :n]), g[n:, n:]
    eye = (
        lax.broadcasted_iota(jnp.int32, (n, n), 0) == lax.broadcasted_iota(jnp.int32, (n, n), 1)
    ).astype(f32)
    delta, inverse = yield from both(solve(shift * n0 + n1, n1), solve(n0, eye))
    b = (delta - eye) * (1.0 / shift)
    yield
    n1b, n2b, n0d = mm(n1, b), mm(n2, b), mm(n0, delta)
    yield
    bb = tmm(b, n2b)
    fresh = tmm(delta, n0d) + (tmm(delta, n1b) + tmm(n1b, delta)) + bb
    yield
    a = delta + mm(inverse, fresh)
    yield
    pp = tmm(a, mm(n0, a)) + (tmm(a, n1b) + tmm(n1b, a)) + bb
    pep = tmm(a, mm(n1, a)) + (tmm(a, n2b) + tmm(n2b, a))
    yield
    return delta, a, fresh, shift * pp + pep


def last_coefficients(first, n3):
    delta, a, fresh, known = first
    n = delta.shape[0]
    eye = (
        lax.broadcasted_iota(jnp.int32, (n, n), 0) == lax.broadcasted_iota(jnp.int32, (n, n), 1)
    ).astype(f32)
    b = (delta - eye) * (1.0 / shift)
    n3b = mm(n3, b)
    pq = known + 0.5 * (tmm(b, n3b) + tmm(n3b, b))
    yield
    alpha2 = yield from solve(pq, fresh)
    ba, aa = mm(b, alpha2), mm(a, alpha2)
    return (
        jnp.concatenate([aa - b, delta - shift * aa], axis=1),
        jnp.concatenate([ba, b - shift * ba - aa], axis=1),
        jnp.concatenate([jnp.zeros_like(ba), -ba], axis=1),
    )


def fused_kernel(table, rhs, diag_in, off_in, coup_in, sol, res, *refs):
    refs = iter(refs)

    def take(count):
        return [next(refs) for _ in range(count)]

    u0, u1, diag, off, coup, products, part = take(7)
    panel0, border0, panel1, border1 = take(4)
    owed0, stage0, r0 = take(3)
    parts0 = take(4)
    owed1, stage1, r1 = take(3)
    parts1 = take(4)
    g01, total01 = take(2)
    work01 = take(3)
    g3, total3 = take(2)
    work3 = take(3)
    send, recv, local_sems, in_sems = take(4)
    n = u0.shape[2]
    net = Net(send, recv)
    c = net.c
    loads = [
        pltpu.make_async_copy(rhs.at[:, pl.ds(j * n, n)], u0.at[j], in_sems.at[j]) for j in range(2)
    ] + [
        pltpu.make_async_copy(a, b, in_sems.at[2 + i])
        for i, (a, b) in enumerate(((off_in, off), (diag_in, diag), (coup_in, coup)))
    ]
    for d in loads:
        d.start()
    greet(
        net,
        [net.device(partner=True)]
        + [net.device(dy=k) for k in (2, 1, 3)]
        + [net.device(dz=k) for k in (2, 1, 3)]
        + [net.device(dx=k) for k in (2, 1, 3)],
    )
    for k in range(NONE, products.shape[0]):
        products[k] = jnp.zeros(products.shape[1:], f32)

    def returned(u):
        def row(s, _):
            v = split(whole(u, s))
            for t in range(OFFS):
                p = dot3(v, split(off[s, t]), COLS)
                products[s * OFFS + t, 0] = p[:n]
                products[s * OFFS + t, 1] = p[n:]
            return 0

        lax.fori_loop(0, ROW_COUNT, row, 0)

    def fill(dst, core, start, count):
        def plane(z, _):
            for y in range(RING):
                for k in range(4):
                    p = core * 64 + (z * RING + y) * 4 + k
                    es = [table[start + i * PART_ROWS + p] for i in range(count)]
                    for j in range(2):
                        v = products[es[0], j]
                        for e in es[1:]:
                            v = v + products[e, j]
                        dst[j, z, y, k] = v
            return 0

        lax.fori_loop(0, RING, plane, 0)

    def crossed(border, s):
        out = None
        for h in range(RING):
            p = dot3(split(jnp.concatenate([border[h, 0, s], border[h, 1, s]], axis=0)), split(coup[s, h]), ROWS)
            out = p if out is None else out + p
        return out

    def tiles_of(panel, s):
        out = None
        for t in range(OFFS):
            e = s * OFFS + t
            live = table[LIVE + e].astype(f32)
            v = panel_row(panel, table[PLACE + e]) * live
            p = dot3(split(v), split(off[s, t]), ROWS)
            out = p if out is None else out + p
        return out

    def rest_steps(u, border, border_done):
        for s in range(ROW_COUNT):
            part[s] = dot3(split(whole(u, s)), split(diag[s]), ROWS)
        while not border_done:
            yield
        for s in range(coup.shape[0]):
            part[s] = part[s] + crossed(border, s)
            yield

    def marked(steps, mark):
        out = yield from steps
        mark.append(out)

    def started(steps):
        next(steps)
        return steps

    loads[0].wait()
    loads[1].wait()
    got_panel, got_border = [], []
    going = [
        started(marked(gather_steps(net, j, u0, panel0, local_sems.at[j]), got_panel))
        for j in range(2)
    ]
    going.append(started(marked(border_steps(net, u0, border0, local_sems.at[2]), got_border)))
    for d in loads[2:]:
        d.wait()
    returned(u0)
    fill(stage0, 1 - c, FIRST, 2)
    scatters = [scatter_steps(net, j, owed0, stage0, r0, *parts0) for j in range(2)]
    fill(r0, c, FIRST, 2)
    scatters = [started(s) for s in scatters]

    def forward_steps():
        yield from rest_steps(u0, border0, got_border)
        while len(got_panel) < 2:
            yield
        for s in range(ROW_COUNT):
            part[s] = part[s] + tiles_of(panel0, s)
            yield

    run(scatters + going + [forward_steps()])
    for s in range(ROW_COUNT):
        for j in range(2):
            u1[j, s] = part[s, j * n : (j + 1) * n] + owed0[j, s]

    got_panel, got_border = [], []
    going = [
        started(marked(gather_steps(net, j, u1, panel1, local_sems.at[3 + j]), got_panel))
        for j in range(2)
    ]
    going.append(started(marked(border_steps(net, u1, border1, local_sems.at[5]), got_border)))
    total = None
    for s in range(ROW_COUNT):
        x = jnp.concatenate([whole(u0, s), whole(u1, s)], axis=0)
        total = gram(x, x) if total is None else total + gram(x, x)
    g01[...] = total
    going.append(started(reduce_steps(net, g01, total01, *work01)))
    returned(u1)
    run(going + [rest_steps(u1, border1, got_border)])

    def second_row(s, total):
        tiles = tiles_of(panel1, s)
        w = tiles + part[s]
        products[OWN + s, 0] = w[:n]
        products[OWN + s, 1] = w[n:]
        return total + gram(whole(u1, s), w + tiles)

    total = lax.fori_loop(0, ROW_COUNT, second_row, jnp.zeros((2 * n, 2 * n), f32))
    g3[...] = jnp.concatenate([total[:n], total[n:]], axis=1)
    known, reduced, weights, scattered = [], [], [], []
    going = [started(marked(reduce_steps(net, g3, total3, *work3), reduced))]
    fill(stage1, 1 - c, SECOND, 3)
    scatters = [marked(scatter_steps(net, j, owed1, stage1, r1, *parts1), scattered) for j in range(2)]
    fill(r1, c, SECOND, 3)
    going += [started(s) for s in scatters]

    def weight_steps():
        first = yield from first_coefficients(total01[...])
        while not reduced:
            yield
        n3 = jnp.concatenate([total3[:, : 2 * n], total3[:, 2 * n :]], axis=0)
        return (yield from last_coefficients(first, n3))

    run(going + [marked(weight_steps(), weights)])
    w0, w1, w2 = weights[0]
    for s in range(ROW_COUNT):
        p = table[MINE + s]
        out = (
            tmm(w0, panel_row(panel0, p)) + tmm(w1, panel_row(panel1, p))
        ) + tmm(w2, whole(owed1, s))
        sol[s] = out[: 2 * n]
        res[s] = out[2 * n :]
    net.drain()


def local(rhs, diag, off, coup, col_index, load, new_slot):
    rows, n2, w = rhs.shape
    n = n2 // 2
    vm = pl.BlockSpec(memory_space=pltpu.VMEM)
    sm = pl.BlockSpec(memory_space=pltpu.SMEM)
    anys = pl.BlockSpec(memory_space=pl.ANY)
    table = pl.pallas_call(
        table_kernel,
        out_shape=jax.ShapeDtypeStruct((TABLE,), jnp.int32),
        in_specs=[anys, sm, sm],
        out_specs=sm,
        scratch_shapes=[pltpu.SMEM((rows, off.shape[1]), jnp.int32), pltpu.SemaphoreType.DMA(())],
        name="tables",
    )(col_index, load, new_slot)

    def vmem(*shape):
        return pltpu.VMEM(shape, f32)

    panels = [vmem(2, 2, RING, RING, 4, n, w), vmem(RING, 2, 2, n, w)]
    scatter = [
        vmem(2, rows, n, w),
        vmem(2, RING, RING, 4, n, w),
        vmem(2, RING, RING, 4, n, w),
        vmem(2, RING, RING, 4, n, w),
        vmem(2, 2, RING, 2, n, w),
        vmem(2, 2, RING, 4, n, w),
        vmem(2, 3, 4, n, w),
    ]

    def reduction(m, k):
        return [vmem(m, k), vmem(m, k), vmem(4, m // 2, k), vmem(3, 3, m // 2, k), vmem(m // 2, k)]

    copies = 2 * (2 * 22 + 3 + 2 * 23 + 11)
    scratch = (
        [vmem(2, rows, n, w), vmem(2, rows, n, w), vmem(*diag.shape), vmem(*off.shape), vmem(*coup.shape)]
        + [vmem(OWN + rows, 2, n, w), vmem(rows, n2, w)]
        + panels
        + panels
        + scatter
        + scatter
        + reduction(2 * n2, 2 * n2)
        + reduction(n, 2 * n2)
        + [pltpu.SemaphoreType.DMA((copies,))] * 2
        + [pltpu.SemaphoreType.DMA((6,)), pltpu.SemaphoreType.DMA((5,))]
    )
    return pl.pallas_call(
        fused_kernel,
        out_shape=[jax.ShapeDtypeStruct(rhs.shape, f32)] * 2,
        in_specs=[sm] + [anys] * 4,
        out_specs=[vm, vm],
        scratch_shapes=scratch,
        compiler_params=pltpu.CompilerParams(
            collective_id=0, has_side_effects=True, vmem_limit_bytes=56 << 20
        ),
        name="fused",
    )(table, rhs, diag, off, coup)


def solution(mesh):
    return jax.shard_map(
        local,
        mesh=mesh,
        in_specs=(
            P(("group", "bulk"), None, None),
            P(("group", "bulk"), None, None),
            P(("group", "bulk"), None, None, None),
            P(("group", "bulk"), None, None, None),
            P(),
            P(),
            P(),
        ),
        out_specs=(P(("group", "bulk"), None, None), P(("group", "bulk"), None, None)),
        check_vma=False,
    )
```

```python
import functools

import jax
import jax.numpy as jnp
from jax import lax
from jax.experimental import pallas as pl
from jax.experimental.pallas import tpu as pltpu
from jax.sharding import PartitionSpec as P

highest = lax.Precision.HIGHEST
shift = 4.0
f32 = jnp.float32
bf16 = jnp.bfloat16
RING = 4
MESH = pl.DeviceIdType.MESH


class Net:
    def __init__(self, send, recv):
        self.g = lax.axis_index("group")
        b = lax.axis_index("bulk")
        self.c = lax.rem(b, 2)
        self.y = lax.rem(b // 2, RING)
        self.z = b // (2 * RING)
        self.send, self.recv = send, recv
        self.count = 0
        self.pending = []

    def device(self, dx=0, dy=0, dz=0, partner=False):
        c = 1 - self.c if partner else self.c
        y = lax.rem(self.y + dy, RING)
        z = lax.rem(self.z + dz, RING)
        return (lax.rem(self.g + dx, RING), (z * RING + y) * 2 + c)

    def copy(self, src, dst, device):
        i = self.count
        self.count += 1
        d = pltpu.make_async_remote_copy(
            src_ref=src,
            dst_ref=dst,
            send_sem=self.send.at[i],
            recv_sem=self.recv.at[i],
            device_id=device,
            device_id_type=MESH,
        )
        d.start()
        self.pending.append(d)
        return d

    def drain(self):
        for d in self.pending:
            d.wait_send()


def plus(a, k):
    return lax.rem(a + k, RING)


def greet(net, devices):
    barrier = pltpu.get_barrier_semaphore()
    for d in devices:
        pl.semaphore_signal(barrier, inc=1, device_id=d, device_id_type=MESH)
    pl.semaphore_wait(barrier, len(devices))


def gather_steps(net, j, u, panel, local_sem):
    c, y, z = net.c, net.y, net.z
    f0, s0 = (y, z) if j == 0 else (z, y)

    def unit(fi, si):
        return panel.at[c, j, si, fi] if j == 0 else panel.at[c, j, fi, si]

    def column(si):
        return panel.at[c, j, si] if j == 0 else panel.at[c, j, :, si]

    def to(df, ds):
        return net.device(dy=df, dz=ds) if j == 0 else net.device(dy=ds, dz=df)

    partner = net.device(partner=True)
    mine = unit(f0, s0)
    own = pltpu.make_async_copy(u.at[j], mine, local_sem)
    own.start()
    near = [net.copy(u.at[j], mine, to(k, 0)) for k in (1, 3)]
    ups = [net.copy(u.at[j], mine, to(0, 1))]
    downs = [net.copy(u.at[j], mine, to(0, 3))]
    far = net.copy(u.at[j], mine, to(2, 0))
    lo, hi = pl.ds(0, 2), pl.ds(2, 2)
    order = [f0, plus(f0, 3), plus(f0, 1), plus(f0, 2)]
    halves = []

    def pass_on(p):
        piece = unit(order[p], s0)
        ups.append(net.copy(piece, piece, to(0, 1)))
        downs.append(net.copy(piece, piece, to(0, 3)))

    def forward(p):
        ups[p].wait_recv()
        piece = unit(order[p], plus(s0, 3)).at[lo]
        halves.append(net.copy(piece, piece, to(0, 1)))
        downs[p].wait_recv()
        piece = unit(order[p], plus(s0, 1)).at[hi]
        halves.append(net.copy(piece, piece, to(0, 3)))

    def swap(k):
        return net.copy(column(plus(s0, k)), column(plus(s0, k)), partner)

    for p in (1, 2):
        yield
        near[p - 1].wait_recv()
        pass_on(p)
    yield
    forward(0)
    yield
    far.wait_recv()
    pass_on(3)
    piece = unit(order[3], s0)
    last = net.copy(piece, piece, to(0, 2))
    own.wait()
    swapped = [swap(0)]
    for p in (1, 2):
        yield
        forward(p)
    yield
    ups[3].wait_recv()
    swapped.append(swap(3))
    yield
    downs[3].wait_recv()
    swapped.append(swap(1))
    yield
    for d in halves:
        d.wait_recv()
    last.wait_recv()
    swapped.append(swap(2))
    for d in swapped:
        yield
        d.wait_recv()


def scatter_steps(net, j, owed, stage, r, t0, t1, t2, t3):
    y, z = net.y, net.z
    f0, s0 = (y, z) if j == 0 else (z, y)

    def column(ref, k):
        si = plus(s0, k)
        return ref.at[j, si] if j == 0 else ref.at[j, :, si]

    def to(df, ds):
        return net.device(dy=df, dz=ds) if j == 0 else net.device(dy=ds, dz=df)

    partner = net.device(partner=True)
    lo, hi = pl.ds(0, 2), pl.ds(2, 2)
    order = [2, 1, 3, 0]
    rows = {k: plus(f0, k) for k in range(RING)}
    first = {}
    for k in order:
        first[k] = net.copy(column(stage, k), column(t0, k), partner)
    cols = {k: column(r, k) for k in range(RING)}

    def start(k):
        b = column(t0, k)
        for i in order:
            cols[k][rows[i]] = cols[k][rows[i]] + b[rows[i]]

    yield
    first[2].wait_recv()
    start(2)
    ups = {i: net.copy(cols[2].at[rows[i], lo], t1.at[j, 0, rows[i]], to(0, 1)) for i in order}
    downs = {i: net.copy(cols[2].at[rows[i], hi], t1.at[j, 1, rows[i]], to(0, 3)) for i in order}
    yield
    first[1].wait_recv()
    start(1)
    yield
    first[3].wait_recv()
    start(3)
    yield
    first[0].wait_recv()
    start(0)
    ups2, downs2 = {}, {}
    for i in order:
        q = rows[i]
        yield
        ups[i].wait_recv()
        cols[1][q, lo] = cols[1][q, lo] + t1[j, 0, q]
        ups2[i] = net.copy(cols[1].at[q], t2.at[j, 0, q], to(0, 1))
        downs[i].wait_recv()
        cols[3][q, hi] = cols[3][q, hi] + t1[j, 1, q]
        downs2[i] = net.copy(cols[3].at[q], t2.at[j, 1, q], to(0, 3))
    sent = []
    for i in order:
        q = rows[i]
        yield
        ups2[i].wait_recv()
        downs2[i].wait_recv()
        cols[0][q] = cols[0][q] + (t2[j, 0, q] + t2[j, 1, q])
        if i:
            sent.append(net.copy(cols[0].at[q], t3.at[j, i - 1], to(i, 0)))
    for d in sent:
        yield
        d.wait_recv()
    owed[j] = (cols[0][rows[0]] + t3[j, 0]) + (t3[j, 1] + t3[j, 2])


def border_steps(net, u, border, local_sem):
    src = u.at[:, pl.ds(0, 2)]
    own = pltpu.make_async_copy(src, border.at[net.g], local_sem)
    own.start()
    sent = [net.copy(src, border.at[net.g], net.device(dx=k)) for k in (1, 3, 2)]
    yield
    own.wait()
    for d in sent:
        d.wait_recv()


def reduce_steps(net, m, out, acc, slots, plane_slots, halves):
    c = net.c
    rows = acc.shape[1]
    partner = net.device(partner=True)
    d = net.copy(m.at[pl.ds((1 - c) * rows, rows)], halves, partner)
    yield
    d.wait_recv()
    acc[0] = m[pl.ds(c * rows, rows)] + halves[...]
    sent = [net.copy(acc.at[0], slots.at[k - 1], net.device(dx=k)) for k in (1, 3, 2)]
    yield
    for d in sent:
        d.wait_recv()
    acc[1] = (acc[0] + slots[0]) + (slots[1] + slots[2])
    sent = [
        net.copy(acc.at[1], plane_slots.at[k - 1], net.device(dy=k % RING, dz=k // RING))
        for k in FAR_FIRST
    ]
    yield
    for d in sent:
        d.wait_recv()
    terms = [acc[1]] + [plane_slots[k] for k in range(RING * RING - 1)]
    while len(terms) > 1:
        terms = [a + b for a, b in zip(terms[::2], terms[1::2])]
    acc[2] = terms[0]
    out[pl.ds(c * rows, rows)] = terms[0]
    d = net.copy(acc.at[2], out.at[pl.ds(c * rows, rows)], partner)
    yield
    d.wait_recv()


def hops(k):
    return min(k % RING, RING - k % RING) + min(k // RING, RING - k // RING)


FAR_FIRST = sorted(range(1, RING * RING), key=lambda k: -hops(k))


def advance(steps, count=1):
    for _ in range(count):
        for s in steps:
            next(s, None)


def run(*steps):
    for s in steps:
        for _ in s:
            pass


def split(a):
    top = a.astype(bf16)
    return top, (a - top.astype(f32)).astype(bf16)


def dot3(a, b, dims):
    dot = functools.partial(
        lax.dot_general, dimension_numbers=(dims, ((), ())), preferred_element_type=f32
    )
    return dot(a[0], b[0]) + (dot(a[0], b[1]) + dot(a[1], b[0]))


ROWS = ((1,), (1,))
COLS = ((1,), (0,))


ROW_COUNT = 4
OFFS = 11
ENTRIES = ROW_COUNT * OFFS
PART_ROWS = 128
NONE = ENTRIES
OWN = ENTRIES + 1
def position(slot):
    return lax.rem(slot // 4, 2) * 64 + (slot // 8) * 4 + lax.rem(slot, 4)


def gram(a, b):
    return lax.dot_general(a, b, (ROWS, ((), ())), precision=highest, preferred_element_type=f32)


def whole(ref, *idx):
    return jnp.concatenate([ref[(0,) + idx], ref[(1,) + idx]], axis=0)


def panel_row(panel, p):
    c, z = p // 64, lax.rem(p // 16, RING)
    y, k = lax.rem(p // 4, RING), lax.rem(p, 4)
    return jnp.concatenate([panel[c, 0, z, y, k], panel[c, 1, z, y, k]], axis=0)


def solve(m, r):
    n = m.shape[0]
    t = jnp.concatenate([m, r], axis=1)
    blocks = [t[8 * i : 8 * i + 8] for i in range(n // 8)]
    shape = blocks[0].shape
    row_id = lax.broadcasted_iota(jnp.int32, shape, 0)
    for b in range(n // 8):
        piv = blocks[b]
        rows = [jnp.broadcast_to(piv[i : i + 1], shape) for i in range(8)]
        lanes = [jnp.broadcast_to(piv[:, 8 * b + i : 8 * b + i + 1], shape) for i in range(8)]
        d = [[jnp.broadcast_to(lanes[q][i : i + 1], shape) for q in range(8)] for i in range(8)]
        for i in range(8):
            inv = 1.0 / d[i][i]
            rows[i] = rows[i] * inv
            for q in range(i + 1, 8):
                d[i][q] = d[i][q] * inv
            for k in range(8):
                if k != i:
                    factor = d[k][i]
                    rows[k] = rows[k] - factor * rows[i]
                    for q in range(i + 1, 8):
                        d[k][q] = d[k][q] - factor * d[i][q]
        new = rows[0]
        for i in range(1, 8):
            new = jnp.where(row_id == i, rows[i], new)
        for k in range(n // 8):
            if k != b:
                acc = blocks[k]
                for i in range(8):
                    column = blocks[k][:, 8 * b + i : 8 * b + i + 1]
                    acc = acc - jnp.broadcast_to(column, shape) * rows[i]
                blocks[k] = acc
        blocks[b] = new
        yield
    return jnp.concatenate(blocks, axis=0)[:, n:]


def both(*solves):
    out = [None] * len(solves)
    left = list(range(len(solves)))
    while left:
        for i in list(left):
            try:
                next(solves[i])
            except StopIteration as e:
                out[i] = e.value
                left.remove(i)
        yield
    return out


def finish(steps):
    while True:
        try:
            next(steps)
        except StopIteration as e:
            return e.value


def mm(a, b):
    return lax.dot_general(a, b, (COLS, ((), ())), precision=highest, preferred_element_type=f32)


def tmm(a, b):
    return lax.dot_general(
        a, b, (((0,), (0,)), ((), ())), precision=highest, preferred_element_type=f32
    )


def first_coefficients(g):
    n = g.shape[0] // 2
    g = 0.5 * (g + g.T)
    n0, n1, n2 = g[:n, :n], 0.5 * (g[:n, n:] + g[n:, :n]), g[n:, n:]
    eye = (
        lax.broadcasted_iota(jnp.int32, (n, n), 0) == lax.broadcasted_iota(jnp.int32, (n, n), 1)
    ).astype(f32)
    delta, inverse = yield from both(solve(shift * n0 + n1, n1), solve(n0, eye))
    b = (delta - eye) * (1.0 / shift)
    yield
    n1b, n2b, n0d = mm(n1, b), mm(n2, b), mm(n0, delta)
    yield
    bb = tmm(b, n2b)
    fresh = tmm(delta, n0d) + (tmm(delta, n1b) + tmm(n1b, delta)) + bb
    yield
    a = delta + mm(inverse, fresh)
    yield
    pp = tmm(a, mm(n0, a)) + (tmm(a, n1b) + tmm(n1b, a)) + bb
    pep = tmm(a, mm(n1, a)) + (tmm(a, n2b) + tmm(n2b, a))
    yield
    return delta, a, fresh, shift * pp + pep


def last_coefficients(first, n3):
    delta, a, fresh, known = first
    n = delta.shape[0]
    eye = (
        lax.broadcasted_iota(jnp.int32, (n, n), 0) == lax.broadcasted_iota(jnp.int32, (n, n), 1)
    ).astype(f32)
    b = (delta - eye) * (1.0 / shift)
    n3b = mm(n3, b)
    pq = known + 0.5 * (tmm(b, n3b) + tmm(n3b, b))
    yield
    alpha2 = yield from solve(pq, fresh)
    ba, aa = mm(b, alpha2), mm(a, alpha2)
    return (
        jnp.concatenate([aa - b, delta - shift * aa], axis=1),
        jnp.concatenate([ba, b - shift * ba - aa], axis=1),
        jnp.concatenate([jnp.zeros_like(ba), -ba], axis=1),
    )


def fused_kernel(cols, load, moved, rhs, diag_in, off_in, coup_in, weights_out, basis, *refs):
    refs = iter(refs)

    def take(count):
        return [next(refs) for _ in range(count)]

    u0, u1, diag, off, coup, products, part = take(7)
    panel0, border0, panel1, border1 = take(4)
    owed0, stage0, r0 = take(3)
    parts0 = take(4)
    owed1, stage1, r1 = take(3)
    parts1 = take(4)
    g01, total01 = take(2)
    work01 = take(4)
    g3, total3 = take(2)
    work3 = take(4)
    index, table, send, recv, local_sems, in_sems = take(6)
    n, w = u0.shape[2:]
    net = Net(send, recv)
    c = net.c
    loads = [
        pltpu.make_async_copy(rhs.at[:, pl.ds(j * n, n)], u0.at[j], in_sems.at[j]) for j in range(2)
    ] + [
        pltpu.make_async_copy(a, b, in_sems.at[2 + i])
        for i, (a, b) in enumerate(((off_in, off), (diag_in, diag), (coup_in, coup)))
    ]
    for d in loads:
        d.start()
    barrier = pltpu.get_barrier_semaphore()
    greeted = [net.device(partner=True)] + [net.device(dx=k) for k in (2, 1, 3)]
    greeted += [net.device(dy=k % RING, dz=k // RING) for k in FAR_FIRST]
    for d in greeted:
        pl.semaphore_signal(barrier, inc=1, device_id=d, device_id_type=MESH)
    first = (net.g * 32 + lax.axis_index("bulk")) * ROW_COUNT

    lane = lax.broadcasted_iota(jnp.int32, (1, PART_ROWS), 1)
    tops = [jnp.full((1, PART_ROWS), -1, jnp.int32)] * 2
    lows = [jnp.full((1, PART_ROWS), NONE + 1, jnp.int32)] * 2
    own_row = jnp.full((1, PART_ROWS), NONE, jnp.int32)
    mine = []
    for s in range(ROW_COUNT):
        count = load[first + s]
        mine.append(position(lax.rem(moved[first + s], PART_ROWS)))
        own_row = jnp.where(lane == mine[s], OWN + s, own_row)
        for t in range(OFFS):
            e = s * OFFS + t
            slot = cols[t, first + s]
            for i, p in enumerate((position(lax.rem(slot, PART_ROWS)), position(lax.rem(moved[slot], PART_ROWS)))):
                hit = lane == jnp.where(t < count, p, -1)
                tops[i] = jnp.where(hit, e, tops[i])
                lows[i] = jnp.where(hit, jnp.minimum(lows[i], e), lows[i])
    for i in range(2):
        index[2 * i : 2 * i + 1] = jnp.where(tops[i] < 0, NONE, tops[i])
        index[2 * i + 1 : 2 * i + 2] = jnp.where(lows[i] == tops[i], NONE, jnp.minimum(lows[i], NONE))
    index[4:5] = own_row
    index[5:8] = jnp.full((3, PART_ROWS), NONE, jnp.int32)
    indexed = pltpu.make_async_copy(index, table, in_sems.at[5])
    indexed.start()
    for k in range(NONE, products.shape[0]):
        products[k] = jnp.zeros(products.shape[1:], f32)

    def returned(u, begin, end):
        def row(s, _):
            v = split(whole(u, s))
            for t in range(OFFS):
                p = dot3(v, split(off[s, t]), COLS)
                products[s * OFFS + t, 0] = p[:n]
                products[s * OFFS + t, 1] = p[n:]
            return 0

        lax.fori_loop(begin, end, row, 0)

    def fill(dst, core, start, count):
        def plane(z, _):
            for y in range(RING):
                for k in range(4):
                    p = core * 64 + (z * RING + y) * 4 + k
                    es = [table[start + i, p] for i in range(count)]
                    for j in range(2):
                        v = products[es[0], j]
                        for e in es[1:]:
                            v = v + products[e, j]
                        dst[j, z, y, k] = v
            return 0

        lax.fori_loop(0, RING, plane, 0)

    def crossed(border, s):
        out = None
        for h in range(RING):
            p = dot3(split(jnp.concatenate([border[h, 0, s], border[h, 1, s]], axis=0)), split(coup[s, h]), ROWS)
            out = p if out is None else out + p
        return out

    def tiles_of(panel, s):
        out = None
        for t in range(OFFS):
            live = (t < load[first + s]).astype(f32)
            v = panel_row(panel, position(lax.rem(cols[t, first + s], PART_ROWS))) * live
            p = dot3(split(v), split(off[s, t]), ROWS)
            out = p if out is None else out + p
        return out

    def set_rest(u):
        for s in range(ROW_COUNT):
            part[s] = dot3(split(whole(u, s)), split(diag[s]), ROWS)

    def add_crossed(border):
        for s in range(coup.shape[0]):
            part[s] = part[s] + crossed(border, s)

    loads[2].wait()
    loads[0].wait()
    loads[1].wait()
    returned(u0, 0, ROW_COUNT // 2)
    pl.semaphore_wait(barrier, len(greeted))
    gathers = [gather_steps(net, j, u0, panel0, local_sems.at[j]) for j in range(2)]
    borders = border_steps(net, u0, border0, local_sems.at[2])
    advance(gathers)
    advance([borders])
    returned(u0, ROW_COUNT // 2, ROW_COUNT)
    indexed.wait()
    fill(stage0, 1 - c, 0, 2)
    scatters = [scatter_steps(net, j, owed0, stage0, r0, *parts0) for j in range(2)]
    fill(r0, c, 0, 2)
    advance(scatters)
    advance(gathers, 2)
    advance(scatters)
    advance(gathers, 2)
    advance(scatters, 3)
    run(borders)
    loads[3].wait()
    loads[4].wait()
    advance(gathers, 2)
    advance(scatters, 4)
    set_rest(u0)
    add_crossed(border0)
    advance(gathers, 2)
    advance(scatters, 2)
    run(*gathers)
    for s in range(ROW_COUNT):
        part[s] = part[s] + tiles_of(panel0, s)
        if s % 2 == 0:
            advance(scatters)
    run(*scatters)
    for s in range(ROW_COUNT):
        for j in range(2):
            u1[j, s] = part[s, j * n : (j + 1) * n] + owed0[j, s]

    gathers = [gather_steps(net, j, u1, panel1, local_sems.at[3 + j]) for j in range(2)]
    borders = border_steps(net, u1, border1, local_sems.at[5])
    advance(gathers)
    advance([borders])
    x = [jnp.concatenate([whole(u0, s), whole(u1, s)], axis=0) for s in range(ROW_COUNT)]
    x = jnp.concatenate(x, axis=1)
    g01[...] = gram(x, x)
    sums = reduce_steps(net, g01, total01, *work01)
    advance([sums])
    returned(u1, 0, ROW_COUNT)
    advance(gathers, 2)
    advance([sums])
    advance(gathers, 2)
    run(borders)
    set_rest(u1)
    add_crossed(border1)
    advance(gathers, 1)
    advance([sums])
    advance(gathers, 3)
    for s in range(ROW_COUNT):
        basis[0 : 2 * n, s * w : (s + 1) * w] = panel_row(panel0, mine[s])
    advance([sums])
    run(*gathers)
    run(sums)

    def second_row(s, total):
        tiles = tiles_of(panel1, s)
        v = tiles + part[s]
        products[OWN + s, 0] = v[:n]
        products[OWN + s, 1] = v[n:]
        return total + gram(whole(u1, s), v + tiles)

    total = lax.fori_loop(0, ROW_COUNT, second_row, jnp.zeros((2 * n, 2 * n), f32))
    g3[...] = jnp.concatenate([total[:n], total[n:]], axis=1)
    sums = reduce_steps(net, g3, total3, *work3)
    advance([sums])
    fill(stage1, 1 - c, 2, 3)
    scatters = [scatter_steps(net, j, owed1, stage1, r1, *parts1) for j in range(2)]
    fill(r1, c, 2, 3)
    advance(scatters)
    advance([sums])
    advance(scatters)
    solving = both(first_coefficients(total01[...]))
    advance([solving], 5)
    advance([sums])
    advance(scatters, 3)
    advance([solving], 2)
    advance(scatters, 4)
    for s in range(ROW_COUNT):
        basis[2 * n : 4 * n, s * w : (s + 1) * w] = panel_row(panel1, mine[s])
    known = finish(solving)[0]
    advance(scatters, 1)
    run(sums)
    n3 = jnp.concatenate([total3[:, : 2 * n], total3[:, 2 * n :]], axis=0)
    solving = both(last_coefficients(known, n3))
    for _ in range(3):
        advance([solving], 3)
        advance(scatters)
    weights = finish(solving)[0]
    for i in range(3):
        weights_out[2 * n * i : 2 * n * (i + 1)] = weights[i]
    run(*scatters)
    for s in range(ROW_COUNT):
        basis[4 * n :, s * w : (s + 1) * w] = whole(owed1, s)
    net.drain()


def last_kernel(weights, basis, sol, res):
    n = sol.shape[1]
    w = sol.shape[2]
    out = tmm(weights[...], basis[...])
    for s in range(sol.shape[0]):
        sol[s] = out[:n, s * w : (s + 1) * w]
        res[s] = out[n:, s * w : (s + 1) * w]


def local(rhs, diag, off, coup, col_index, load, new_slot):
    rows, n2, w = rhs.shape
    n = n2 // 2
    vm = pl.BlockSpec(memory_space=pltpu.VMEM)
    sm = pl.BlockSpec(memory_space=pltpu.SMEM)
    anys = pl.BlockSpec(memory_space=pl.ANY)
    def vmem(*shape):
        return pltpu.VMEM(shape, f32)

    panels = [vmem(2, 2, RING, RING, 4, n, w), vmem(RING, 2, 2, n, w)]
    scatter = [
        vmem(2, rows, n, w),
        vmem(2, RING, RING, 4, n, w),
        vmem(2, RING, RING, 4, n, w),
        vmem(2, RING, RING, 4, n, w),
        vmem(2, 2, RING, 2, n, w),
        vmem(2, 2, RING, 4, n, w),
        vmem(2, 3, 4, n, w),
    ]

    def reduction(m, k):
        half = m // 2
        return [vmem(m, k), vmem(m, k), vmem(3, half, k), vmem(3, half, k)] + [
            vmem(RING * RING - 1, half, k),
            vmem(half, k),
        ]

    copies = 2 * (2 * 22 + 3 + 2 * 23 + 20)
    scratch = (
        [vmem(2, rows, n, w), vmem(2, rows, n, w), vmem(*diag.shape), vmem(*off.shape), vmem(*coup.shape)]
        + [vmem(OWN + rows, 2, n, w), vmem(rows, n2, w)]
        + panels
        + panels
        + scatter
        + scatter
        + reduction(2 * n2, 2 * n2)
        + reduction(n, 2 * n2)
        + [pltpu.VMEM((8, PART_ROWS), jnp.int32), pltpu.SMEM((8, PART_ROWS), jnp.int32)]
        + [pltpu.SemaphoreType.DMA((copies,))] * 2
        + [pltpu.SemaphoreType.DMA((6,)), pltpu.SemaphoreType.DMA((6,))]
    )
    weights, basis = pl.pallas_call(
        fused_kernel,
        out_shape=[
            jax.ShapeDtypeStruct((3 * n2, 2 * n2), f32),
            jax.ShapeDtypeStruct((3 * n2, rows * w), f32),
        ],
        in_specs=[sm] * 3 + [anys] * 4,
        out_specs=[vm, vm],
        scratch_shapes=scratch,
        compiler_params=pltpu.CompilerParams(
            collective_id=0, has_side_effects=True, vmem_limit_bytes=56 << 20
        ),
        name="fused",
    )(col_index.T, load, new_slot, rhs, diag, off, coup)
    return pl.pallas_call(
        last_kernel,
        out_shape=[jax.ShapeDtypeStruct(rhs.shape, f32)] * 2,
        in_specs=[vm, vm],
        out_specs=[vm, vm],
        name="last",
    )(weights, basis)


def solution(mesh):
    return jax.shard_map(
        local,
        mesh=mesh,
        in_specs=(
            P(("group", "bulk"), None, None),
            P(("group", "bulk"), None, None),
            P(("group", "bulk"), None, None, None),
            P(("group", "bulk"), None, None, None),
            P(),
            P(),
            P(),
        ),
        out_specs=(P(("group", "bulk"), None, None), P(("group", "bulk"), None, None)),
        check_vma=False,
    )
```

```python
import functools

import jax
import jax.numpy as jnp
from jax import lax
from jax.experimental import pallas as pl
from jax.experimental.pallas import tpu as pltpu
from jax.sharding import PartitionSpec as P

highest = lax.Precision.HIGHEST
shift = 4.0
f32 = jnp.float32
bf16 = jnp.bfloat16
RING = 4
MESH = pl.DeviceIdType.MESH


class Net:
    def __init__(self, send, recv):
        self.g = lax.axis_index("group")
        b = lax.axis_index("bulk")
        self.c = lax.rem(b, 2)
        self.y = lax.rem(b // 2, RING)
        self.z = b // (2 * RING)
        self.send, self.recv = send, recv
        self.count = 0
        self.pending = []

    def device(self, dx=0, dy=0, dz=0, partner=False):
        c = 1 - self.c if partner else self.c
        y = lax.rem(self.y + dy, RING)
        z = lax.rem(self.z + dz, RING)
        return (lax.rem(self.g + dx, RING), (z * RING + y) * 2 + c)

    def copy(self, src, dst, device):
        i = self.count
        self.count += 1
        d = pltpu.make_async_remote_copy(
            src_ref=src,
            dst_ref=dst,
            send_sem=self.send.at[i],
            recv_sem=self.recv.at[i],
            device_id=device,
            device_id_type=MESH,
        )
        d.start()
        self.pending.append(d)
        return d

    def drain(self):
        for d in self.pending:
            d.wait_send()


def plus(a, k):
    return lax.rem(a + k, RING)


def greet(net, devices):
    barrier = pltpu.get_barrier_semaphore()
    for d in devices:
        pl.semaphore_signal(barrier, inc=1, device_id=d, device_id_type=MESH)
    pl.semaphore_wait(barrier, len(devices))


def gather_steps(net, j, u, panel, local_sem):
    c, y, z = net.c, net.y, net.z
    f0, s0 = (y, z) if j == 0 else (z, y)

    def unit(fi, si):
        return panel.at[c, j, si, fi] if j == 0 else panel.at[c, j, fi, si]

    def column(si):
        return panel.at[c, j, si] if j == 0 else panel.at[c, j, :, si]

    def to(df, ds):
        return net.device(dy=df, dz=ds) if j == 0 else net.device(dy=ds, dz=df)

    partner = net.device(partner=True)
    mine = unit(f0, s0)
    own = pltpu.make_async_copy(u.at[j], mine, local_sem)
    own.start()
    near = [net.copy(u.at[j], mine, to(k, 0)) for k in (1, 3)]
    ups = [net.copy(u.at[j], mine, to(0, 1))]
    downs = [net.copy(u.at[j], mine, to(0, 3))]
    far = net.copy(u.at[j], mine, to(2, 0))
    lo, hi = pl.ds(0, 2), pl.ds(2, 2)
    order = [f0, plus(f0, 3), plus(f0, 1), plus(f0, 2)]
    halves = []

    def pass_on(p):
        piece = unit(order[p], s0)
        ups.append(net.copy(piece, piece, to(0, 1)))
        downs.append(net.copy(piece, piece, to(0, 3)))

    def forward(p):
        ups[p].wait_recv()
        piece = unit(order[p], plus(s0, 3)).at[lo]
        halves.append(net.copy(piece, piece, to(0, 1)))
        downs[p].wait_recv()
        piece = unit(order[p], plus(s0, 1)).at[hi]
        halves.append(net.copy(piece, piece, to(0, 3)))

    def swap(k):
        return net.copy(column(plus(s0, k)), column(plus(s0, k)), partner)

    for p in (1, 2):
        yield
        near[p - 1].wait_recv()
        pass_on(p)
    yield
    forward(0)
    yield
    far.wait_recv()
    pass_on(3)
    piece = unit(order[3], s0)
    last = net.copy(piece, piece, to(0, 2))
    own.wait()
    swapped = [swap(0)]
    for p in (1, 2):
        yield
        forward(p)
    yield
    ups[3].wait_recv()
    swapped.append(swap(3))
    yield
    downs[3].wait_recv()
    swapped.append(swap(1))
    yield
    for d in halves:
        d.wait_recv()
    last.wait_recv()
    swapped.append(swap(2))
    for d in swapped:
        yield
        d.wait_recv()


def scatter_steps(net, j, owed, stage, r, t0, t1, t2, t3):
    y, z = net.y, net.z
    f0, s0 = (y, z) if j == 0 else (z, y)

    def column(ref, k):
        si = plus(s0, k)
        return ref.at[j, si] if j == 0 else ref.at[j, :, si]

    def to(df, ds):
        return net.device(dy=df, dz=ds) if j == 0 else net.device(dy=ds, dz=df)

    partner = net.device(partner=True)
    lo, hi = pl.ds(0, 2), pl.ds(2, 2)
    order = [2, 1, 3, 0]
    rows = {k: plus(f0, k) for k in range(RING)}
    first = {}
    for k in order:
        first[k] = net.copy(column(stage, k), column(t0, k), partner)
        if k == 2:
            yield
    cols = {k: column(r, k) for k in range(RING)}

    def start(k):
        b = column(t0, k)
        for i in order:
            cols[k][rows[i]] = cols[k][rows[i]] + b[rows[i]]

    yield
    first[2].wait_recv()
    start(2)
    ups = {i: net.copy(cols[2].at[rows[i], lo], t1.at[j, 0, rows[i]], to(0, 1)) for i in order}
    downs = {i: net.copy(cols[2].at[rows[i], hi], t1.at[j, 1, rows[i]], to(0, 3)) for i in order}
    yield
    first[1].wait_recv()
    start(1)
    yield
    first[3].wait_recv()
    start(3)
    yield
    first[0].wait_recv()
    start(0)
    ups2, downs2 = {}, {}
    for i in order:
        q = rows[i]
        yield
        ups[i].wait_recv()
        cols[1][q, lo] = cols[1][q, lo] + t1[j, 0, q]
        ups2[i] = net.copy(cols[1].at[q], t2.at[j, 0, q], to(0, 1))
        downs[i].wait_recv()
        cols[3][q, hi] = cols[3][q, hi] + t1[j, 1, q]
        downs2[i] = net.copy(cols[3].at[q], t2.at[j, 1, q], to(0, 3))
    sent = []
    for i in order:
        q = rows[i]
        yield
        ups2[i].wait_recv()
        downs2[i].wait_recv()
        cols[0][q] = cols[0][q] + (t2[j, 0, q] + t2[j, 1, q])
        if i:
            sent.append(net.copy(cols[0].at[q], t3.at[j, i - 1], to(i, 0)))
    for d in sent:
        yield
        d.wait_recv()
    owed[j] = (cols[0][rows[0]] + t3[j, 0]) + (t3[j, 1] + t3[j, 2])


def border_steps(net, u, border, local_sem):
    src = u.at[:, pl.ds(0, 2)]
    own = pltpu.make_async_copy(src, border.at[net.g], local_sem)
    own.start()
    sent = [net.copy(src, border.at[net.g], net.device(dx=k)) for k in (1, 3, 2)]
    yield
    own.wait()
    for d in sent:
        d.wait_recv()


def axis_reduce_steps(net, m, out, acc, slots, halves):
    c = net.c
    rows = acc.shape[1]
    partner = net.device(partner=True)
    d = net.copy(m.at[pl.ds((1 - c) * rows, rows)], halves, partner)
    yield
    d.wait_recv()
    acc[0] = m[pl.ds(c * rows, rows)] + halves[...]
    for t in range(3):
        sent = []
        for k in (1, 3, 2):
            step = [0, 0, 0]
            step[t] = k * (1 - c)
            step[(t + 1) % 3] = step[(t + 1) % 3] + k * c
            sent.append(
                net.copy(acc.at[t], slots.at[t, k - 1], net.device(step[0], step[1], step[2]))
            )
        yield
        for d in sent:
            d.wait_recv()
        acc[t + 1] = (acc[t] + slots[t, 0]) + (slots[t, 1] + slots[t, 2])
    out[pl.ds(c * rows, rows)] = acc[3]
    d = net.copy(acc.at[3], out.at[pl.ds(c * rows, rows)], partner)
    yield
    d.wait_recv()


def reduce_steps(net, m, out, acc, slots, plane_slots, halves):
    c = net.c
    rows = acc.shape[1]
    partner = net.device(partner=True)
    d = net.copy(m.at[pl.ds((1 - c) * rows, rows)], halves, partner)
    yield
    d.wait_recv()
    acc[0] = m[pl.ds(c * rows, rows)] + halves[...]
    sent = [net.copy(acc.at[0], slots.at[k - 1], net.device(dx=k)) for k in (1, 3, 2)]
    yield
    for d in sent:
        d.wait_recv()
    acc[1] = (acc[0] + slots[0]) + (slots[1] + slots[2])
    sent = [
        net.copy(acc.at[1], plane_slots.at[k - 1], net.device(dy=k % RING, dz=k // RING))
        for k in FAR_FIRST
    ]
    yield
    for d in sent:
        d.wait_recv()
    terms = [acc[1]] + [plane_slots[k] for k in range(RING * RING - 1)]
    while len(terms) > 1:
        terms = [a + b for a, b in zip(terms[::2], terms[1::2])]
    acc[2] = terms[0]
    out[pl.ds(c * rows, rows)] = terms[0]
    d = net.copy(acc.at[2], out.at[pl.ds(c * rows, rows)], partner)
    yield
    d.wait_recv()


def hops(k):
    return min(k % RING, RING - k % RING) + min(k // RING, RING - k // RING)


FAR_FIRST = sorted(range(1, RING * RING), key=lambda k: -hops(k))


def advance(steps, count=1):
    for _ in range(count):
        for s in steps:
            next(s, None)


def run(*steps):
    for s in steps:
        for _ in s:
            pass


def split(a):
    top = a.astype(bf16)
    return top, (a - top.astype(f32)).astype(bf16)


def dot3(a, b, dims):
    axis = dims[1][0]
    left = [x[i] for i in (0, 1, 0) for x in a]
    right = [x[i] for i in (0, 0, 1) for x in b]
    return lax.dot_general(
        jnp.concatenate(left, axis=1),
        jnp.concatenate(right, axis=axis),
        (dims, ((), ())),
        preferred_element_type=f32,
    )


ROWS = ((1,), (1,))
COLS = ((1,), (0,))


ROW_COUNT = 4
OFFS = 11
ENTRIES = ROW_COUNT * OFFS
PART_ROWS = 128
NONE = ENTRIES
OWN = ENTRIES + 1
def gram(a, b):
    return lax.dot_general(a, b, (ROWS, ((), ())), precision=highest, preferred_element_type=f32)


def whole(ref, *idx):
    return jnp.concatenate([ref[(0,) + idx], ref[(1,) + idx]], axis=0)


def bits(a, low, mask):
    return jnp.bitwise_and(lax.shift_right_logical(a, low), mask)


def panel_row(panel, slot):
    c, z, y, k = bits(slot, 2, 1), bits(slot, 5, 3), bits(slot, 3, 3), bits(slot, 0, 3)
    return jnp.concatenate([panel[c, 0, z, y, k], panel[c, 1, z, y, k]], axis=0)


def solve(m, r):
    n = m.shape[0]
    t = jnp.concatenate([m, r], axis=1)
    blocks = [t[8 * i : 8 * i + 8] for i in range(n // 8)]
    shape = blocks[0].shape
    row_id = lax.broadcasted_iota(jnp.int32, shape, 0)
    for b in range(n // 8):
        piv = blocks[b]
        rows = [jnp.broadcast_to(piv[i : i + 1], shape) for i in range(8)]
        lanes = [jnp.broadcast_to(piv[:, 8 * b + i : 8 * b + i + 1], shape) for i in range(8)]
        d = [[jnp.broadcast_to(lanes[q][i : i + 1], shape) for q in range(8)] for i in range(8)]
        for i in range(8):
            inv = 1.0 / d[i][i]
            rows[i] = rows[i] * inv
            for q in range(i + 1, 8):
                d[i][q] = d[i][q] * inv
            for k in range(8):
                if k != i:
                    factor = d[k][i]
                    rows[k] = rows[k] - factor * rows[i]
                    for q in range(i + 1, 8):
                        d[k][q] = d[k][q] - factor * d[i][q]
        new = rows[0]
        for i in range(1, 8):
            new = jnp.where(row_id == i, rows[i], new)
        for k in range(n // 8):
            if k != b:
                acc = blocks[k]
                for i in range(8):
                    column = blocks[k][:, 8 * b + i : 8 * b + i + 1]
                    acc = acc - jnp.broadcast_to(column, shape) * rows[i]
                blocks[k] = acc
        blocks[b] = new
        yield
    return jnp.concatenate(blocks, axis=0)[:, n:]


def both(*solves):
    out = [None] * len(solves)
    left = list(range(len(solves)))
    while left:
        for i in list(left):
            try:
                next(solves[i])
            except StopIteration as e:
                out[i] = e.value
                left.remove(i)
        yield
    return out


def finish(steps):
    while True:
        try:
            next(steps)
        except StopIteration as e:
            return e.value


def mm(a, b):
    return lax.dot_general(a, b, (COLS, ((), ())), precision=highest, preferred_element_type=f32)


def tmm(a, b):
    return lax.dot_general(
        a, b, (((0,), (0,)), ((), ())), precision=highest, preferred_element_type=f32
    )


def first_coefficients(g):
    n = g.shape[0] // 2
    g = 0.5 * (g + g.T)
    n0, n1, n2 = g[:n, :n], 0.5 * (g[:n, n:] + g[n:, :n]), g[n:, n:]
    eye = (
        lax.broadcasted_iota(jnp.int32, (n, n), 0) == lax.broadcasted_iota(jnp.int32, (n, n), 1)
    ).astype(f32)
    delta, inverse = yield from both(solve(shift * n0 + n1, n1), solve(n0, eye))
    b = (delta - eye) * (1.0 / shift)
    yield
    n1b, n2b, n0d = mm(n1, b), mm(n2, b), mm(n0, delta)
    yield
    bb = tmm(b, n2b)
    fresh = tmm(delta, n0d) + (tmm(delta, n1b) + tmm(n1b, delta)) + bb
    yield
    a = delta + mm(inverse, fresh)
    yield
    pp = tmm(a, mm(n0, a)) + (tmm(a, n1b) + tmm(n1b, a)) + bb
    pep = tmm(a, mm(n1, a)) + (tmm(a, n2b) + tmm(n2b, a))
    yield
    return delta, a, fresh, shift * pp + pep


def last_coefficients(first, n3):
    delta, a, fresh, known = first
    n = delta.shape[0]
    eye = (
        lax.broadcasted_iota(jnp.int32, (n, n), 0) == lax.broadcasted_iota(jnp.int32, (n, n), 1)
    ).astype(f32)
    b = (delta - eye) * (1.0 / shift)
    n3b = mm(n3, b)
    pq = known + 0.5 * (tmm(b, n3b) + tmm(n3b, b))
    yield
    alpha2 = yield from solve(pq, fresh)
    ba, aa = mm(b, alpha2), mm(a, alpha2)
    return (
        jnp.concatenate([aa - b, delta - shift * aa], axis=1),
        jnp.concatenate([ba, b - shift * ba - aa], axis=1),
        jnp.concatenate([jnp.zeros_like(ba), -ba], axis=1),
    )


def fused_kernel(cols, load, moved, rhs, diag_in, off_in, coup_in, weights_out, basis, *refs):
    refs = iter(refs)

    def take(count):
        return [next(refs) for _ in range(count)]

    u0, u1, diag, off, coup, products, part = take(7)
    panel0, border0, panel1, border1 = take(4)
    owed0, stage0, r0 = take(3)
    parts0 = take(4)
    owed1, stage1, r1 = take(3)
    parts1 = take(4)
    g01, total01 = take(2)
    work01 = take(3)
    g3, total3 = take(2)
    work3 = take(4)
    index, table, send, recv, local_sems, in_sems = take(6)
    n, w = u0.shape[2:]
    net = Net(send, recv)
    c = net.c
    loads = [
        pltpu.make_async_copy(rhs.at[:, pl.ds(j * n, n)], u0.at[j], in_sems.at[j]) for j in range(2)
    ] + [
        pltpu.make_async_copy(a, b, in_sems.at[2 + i])
        for i, (a, b) in enumerate(((off_in, off), (diag_in, diag), (coup_in, coup)))
    ]
    for d in loads:
        d.start()
    barrier = pltpu.get_barrier_semaphore()
    greeted = [net.device(partner=True)] + [net.device(dx=k) for k in (2, 1, 3)]
    greeted += [net.device(dy=k % RING, dz=k // RING) for k in FAR_FIRST]
    for d in greeted:
        pl.semaphore_signal(barrier, inc=1, device_id=d, device_id_type=MESH)
    first = (net.g * 32 + lax.axis_index("bulk")) * ROW_COUNT

    lane = lax.broadcasted_iota(jnp.int32, (1, PART_ROWS), 1)
    lane = bits(lane, 6, 1) * 4 + bits(lane, 2, 15) * 8 + bits(lane, 0, 3)
    tops = [jnp.full((1, PART_ROWS), -1, jnp.int32)] * 2
    lows = [jnp.full((1, PART_ROWS), NONE + 1, jnp.int32)] * 2
    own_row = jnp.full((1, PART_ROWS), NONE, jnp.int32)
    mine = []
    for s in range(ROW_COUNT):
        count = load[first + s]
        mine.append(moved[first + s])
        own_row = jnp.where(lane == bits(mine[s], 0, PART_ROWS - 1), OWN + s, own_row)
        for t in range(OFFS):
            e = s * OFFS + t
            slot = cols[t, first + s]
            for i, p in enumerate((slot, moved[slot])):
                hit = lane == jnp.where(t < count, bits(p, 0, PART_ROWS - 1), -1)
                tops[i] = jnp.where(hit, e, tops[i])
                lows[i] = jnp.where(hit, jnp.minimum(lows[i], e), lows[i])
    for i in range(2):
        index[2 * i : 2 * i + 1] = jnp.where(tops[i] < 0, NONE, tops[i])
        index[2 * i + 1 : 2 * i + 2] = jnp.where(lows[i] == tops[i], NONE, jnp.minimum(lows[i], NONE))
    index[4:5] = own_row
    index[5:8] = jnp.full((3, PART_ROWS), NONE, jnp.int32)
    indexed = pltpu.make_async_copy(index, table, in_sems.at[5])
    indexed.start()
    for k in range(NONE, products.shape[0]):
        products[k] = jnp.zeros(products.shape[1:], f32)

    def returned(u, begin, end):
        def row(s, _):
            v = split(whole(u, s))
            for t in range(OFFS):
                p = dot3([v], [split(off[s, t])], COLS)
                products[s * OFFS + t, 0] = p[:n]
                products[s * OFFS + t, 1] = p[n:]
            return 0

        lax.fori_loop(begin, end, row, 0)

    def fill(dst, core, start, count):
        def plane(z, _):
            for y in range(RING):
                for k in range(4):
                    p = core * 64 + (z * RING + y) * 4 + k
                    es = [table[start + i, p] for i in range(count)]
                    for j in range(2):
                        v = products[es[0], j]
                        for e in es[1:]:
                            v = v + products[e, j]
                        dst[j, z, y, k] = v
            return 0

        lax.fori_loop(0, RING, plane, 0)

    def crossed(border, s):
        v = [split(jnp.concatenate([border[h, 0, s], border[h, 1, s]], axis=0)) for h in range(RING)]
        return dot3(v, [split(coup[s, h]) for h in range(RING)], ROWS)

    def tiles_of(panel, s):
        v = []
        for t in range(OFFS):
            live = (t < load[first + s]).astype(f32)
            v.append(split(panel_row(panel, cols[t, first + s]) * live))
        return dot3(v, [split(off[s, t]) for t in range(OFFS)], ROWS)

    def set_rest(u):
        for s in range(ROW_COUNT):
            part[s] = dot3([split(whole(u, s))], [split(diag[s])], ROWS)

    def add_crossed(border):
        for s in range(coup.shape[0]):
            part[s] = part[s] + crossed(border, s)

    loads[0].wait()
    loads[1].wait()
    pl.semaphore_wait(barrier, len(greeted))
    gathers = [gather_steps(net, j, u0, panel0, local_sems.at[j]) for j in range(2)]
    borders = border_steps(net, u0, border0, local_sems.at[2])
    advance(gathers)
    advance([borders])
    loads[2].wait()
    returned(u0, 0, ROW_COUNT)
    indexed.wait()
    fill(stage0, 1 - c, 0, 2)
    scatters = [scatter_steps(net, j, owed0, stage0, r0, *parts0) for j in range(2)]
    advance(scatters, 2)
    advance(gathers, 2)
    fill(r0, c, 0, 2)
    advance(gathers)
    advance(scatters)
    advance(gathers)
    advance(scatters, 3)
    run(borders)
    loads[3].wait()
    loads[4].wait()
    advance(gathers, 2)
    advance(scatters, 4)
    set_rest(u0)
    add_crossed(border0)
    advance(gathers, 2)
    advance(scatters, 1)
    run(*gathers)
    for s in range(ROW_COUNT):
        part[s] = part[s] + tiles_of(panel0, s)
        if s < 3:
            advance(scatters)
    run(*scatters)
    for s in range(ROW_COUNT):
        for j in range(2):
            u1[j, s] = part[s, j * n : (j + 1) * n] + owed0[j, s]

    gathers = [gather_steps(net, j, u1, panel1, local_sems.at[3 + j]) for j in range(2)]
    borders = border_steps(net, u1, border1, local_sems.at[5])
    advance(gathers)
    advance([borders])
    x = [jnp.concatenate([whole(u0, s), whole(u1, s)], axis=0) for s in range(ROW_COUNT)]
    x = jnp.concatenate(x, axis=1)
    g01[...] = gram(x, x)
    sums = axis_reduce_steps(net, g01, total01, *work01)
    advance([sums])
    returned(u1, 0, 2)
    advance(gathers, 2)
    advance([sums])
    advance(gathers, 1)
    returned(u1, 2, 3)
    advance(gathers, 1)
    returned(u1, 3, 4)
    advance(gathers, 1)
    run(borders)
    advance(gathers, 1)
    advance([sums])
    set_rest(u1)
    add_crossed(border1)
    for s in range(ROW_COUNT):
        basis[0 : 2 * n, s * w : (s + 1) * w] = panel_row(panel0, mine[s])
    advance(gathers, 2)
    advance([sums])
    advance(gathers, 1)
    run(*gathers)

    def second_row(s, total):
        tiles = tiles_of(panel1, s)
        v = tiles + part[s]
        products[OWN + s, 0] = v[:n]
        products[OWN + s, 1] = v[n:]
        return total + gram(whole(u1, s), v + tiles)

    total = lax.fori_loop(0, ROW_COUNT, second_row, jnp.zeros((2 * n, 2 * n), f32))
    g3[...] = jnp.concatenate([total[:n], total[n:]], axis=1)
    early = sums
    sums = reduce_steps(net, g3, total3, *work3)
    advance([sums])
    advance([early])
    fill(stage1, 1 - c, 2, 3)
    scatters = [scatter_steps(net, j, owed1, stage1, r1, *parts1) for j in range(2)]
    advance(scatters, 2)
    advance([sums])
    fill(r1, c, 2, 3)
    advance(scatters)
    run(early)
    solving = both(first_coefficients(total01[...]))
    advance([solving], 5)
    advance([sums])
    advance(scatters, 3)
    advance([solving], 2)
    advance(scatters, 4)
    for s in range(ROW_COUNT):
        basis[2 * n : 4 * n, s * w : (s + 1) * w] = panel_row(panel1, mine[s])
    known = finish(solving)[0]
    advance(scatters, 1)
    run(sums)
    n3 = jnp.concatenate([total3[:, : 2 * n], total3[:, 2 * n :]], axis=0)
    solving = both(last_coefficients(known, n3))
    for _ in range(3):
        advance([solving], 3)
        advance(scatters)
    weights = finish(solving)[0]
    for i in range(3):
        weights_out[2 * n * i : 2 * n * (i + 1)] = weights[i]
    run(*scatters)
    for s in range(ROW_COUNT):
        basis[4 * n :, s * w : (s + 1) * w] = whole(owed1, s)
    net.drain()


def last_kernel(weights, basis, sol, res):
    n = sol.shape[1]
    w = sol.shape[2]
    out = tmm(weights[...], basis[...])
    for s in range(sol.shape[0]):
        sol[s] = out[:n, s * w : (s + 1) * w]
        res[s] = out[n:, s * w : (s + 1) * w]


def local(rhs, diag, off, coup, col_index, load, new_slot):
    rows, n2, w = rhs.shape
    n = n2 // 2
    vm = pl.BlockSpec(memory_space=pltpu.VMEM)
    sm = pl.BlockSpec(memory_space=pltpu.SMEM)
    anys = pl.BlockSpec(memory_space=pl.ANY)
    def vmem(*shape):
        return pltpu.VMEM(shape, f32)

    panels = [vmem(2, 2, RING, RING, 4, n, w), vmem(RING, 2, 2, n, w)]
    scatter = [
        vmem(2, rows, n, w),
        vmem(2, RING, RING, 4, n, w),
        vmem(2, RING, RING, 4, n, w),
        vmem(2, RING, RING, 4, n, w),
        vmem(2, 2, RING, 2, n, w),
        vmem(2, 2, RING, 4, n, w),
        vmem(2, 3, 4, n, w),
    ]

    def axis_reduction(m, k):
        half = m // 2
        return [vmem(m, k), vmem(m, k), vmem(4, half, k), vmem(3, 3, half, k), vmem(half, k)]

    def reduction(m, k):
        half = m // 2
        return [vmem(m, k), vmem(m, k), vmem(3, half, k), vmem(3, half, k)] + [
            vmem(RING * RING - 1, half, k),
            vmem(half, k),
        ]

    copies = 2 * (2 * 22 + 3 + 2 * 23 + 20)
    scratch = (
        [vmem(2, rows, n, w), vmem(2, rows, n, w), vmem(*diag.shape), vmem(*off.shape), vmem(*coup.shape)]
        + [vmem(OWN + rows, 2, n, w), vmem(rows, n2, w)]
        + panels
        + panels
        + scatter
        + scatter
        + axis_reduction(2 * n2, 2 * n2)
        + reduction(n, 2 * n2)
        + [pltpu.VMEM((8, PART_ROWS), jnp.int32), pltpu.SMEM((8, PART_ROWS), jnp.int32)]
        + [pltpu.SemaphoreType.DMA((copies,))] * 2
        + [pltpu.SemaphoreType.DMA((6,)), pltpu.SemaphoreType.DMA((6,))]
    )
    weights, basis = pl.pallas_call(
        fused_kernel,
        out_shape=[
            jax.ShapeDtypeStruct((3 * n2, 2 * n2), f32),
            jax.ShapeDtypeStruct((3 * n2, rows * w), f32),
        ],
        in_specs=[sm] * 3 + [anys] * 4,
        out_specs=[vm, vm],
        scratch_shapes=scratch,
        compiler_params=pltpu.CompilerParams(
            collective_id=0, has_side_effects=True, vmem_limit_bytes=56 << 20
        ),
        name="fused",
    )(col_index.T, load, new_slot, rhs, diag, off, coup)
    return pl.pallas_call(
        last_kernel,
        out_shape=[jax.ShapeDtypeStruct(rhs.shape, f32)] * 2,
        in_specs=[vm, vm],
        out_specs=[vm, vm],
        name="last",
    )(weights, basis)


def solution(mesh):
    return jax.shard_map(
        local,
        mesh=mesh,
        in_specs=(
            P(("group", "bulk"), None, None),
            P(("group", "bulk"), None, None),
            P(("group", "bulk"), None, None, None),
            P(("group", "bulk"), None, None, None),
            P(),
            P(),
            P(),
        ),
        out_specs=(P(("group", "bulk"), None, None), P(("group", "bulk"), None, None)),
        check_vma=False,
    )
```

```python
import functools

import jax
import jax.numpy as jnp
from jax import lax
from jax.experimental import pallas as pl
from jax.experimental.pallas import tpu as pltpu
from jax.sharding import PartitionSpec as P

highest = lax.Precision.HIGHEST
shift = 4.0
f32 = jnp.float32
bf16 = jnp.bfloat16
RING = 4
MESH = pl.DeviceIdType.MESH


class Net:
    def __init__(self, send, recv):
        self.g = lax.axis_index("group")
        b = lax.axis_index("bulk")
        self.c = lax.rem(b, 2)
        self.y = lax.rem(b // 2, RING)
        self.z = b // (2 * RING)
        self.send, self.recv = send, recv
        self.count = 0
        self.pending = []

    def device(self, dx=0, dy=0, dz=0, partner=False):
        c = 1 - self.c if partner else self.c
        y = lax.rem(self.y + dy, RING)
        z = lax.rem(self.z + dz, RING)
        return (lax.rem(self.g + dx, RING), (z * RING + y) * 2 + c)

    def copy(self, src, dst, device):
        i = self.count
        self.count += 1
        d = pltpu.make_async_remote_copy(
            src_ref=src,
            dst_ref=dst,
            send_sem=self.send.at[i],
            recv_sem=self.recv.at[i],
            device_id=device,
            device_id_type=MESH,
        )
        d.start()
        self.pending.append(d)
        return d

    def drain(self):
        for d in self.pending:
            d.wait_send()


def plus(a, k):
    return lax.rem(a + k, RING)


def greet(net, devices):
    barrier = pltpu.get_barrier_semaphore()
    for d in devices:
        pl.semaphore_signal(barrier, inc=1, device_id=d, device_id_type=MESH)
    pl.semaphore_wait(barrier, len(devices))


def gather_steps(net, j, u, panel, local_sem):
    c, y, z = net.c, net.y, net.z
    f0, s0 = (y, z) if j == 0 else (z, y)

    def unit(fi, si):
        return panel.at[c, j, si, fi] if j == 0 else panel.at[c, j, fi, si]

    def column(si):
        return panel.at[c, j, si] if j == 0 else panel.at[c, j, :, si]

    def to(df, ds):
        return net.device(dy=df, dz=ds) if j == 0 else net.device(dy=ds, dz=df)

    partner = net.device(partner=True)
    mine = unit(f0, s0)
    own = pltpu.make_async_copy(u.at[j], mine, local_sem)
    own.start()
    near = [net.copy(u.at[j], mine, to(k, 0)) for k in (1, 3)]
    ups = [net.copy(u.at[j], mine, to(0, 1))]
    downs = [net.copy(u.at[j], mine, to(0, 3))]
    far = net.copy(u.at[j], mine, to(2, 0))
    lo, hi = pl.ds(0, 2), pl.ds(2, 2)
    order = [f0, plus(f0, 3), plus(f0, 1), plus(f0, 2)]
    halves = []

    def pass_on(p):
        piece = unit(order[p], s0)
        ups.append(net.copy(piece, piece, to(0, 1)))
        downs.append(net.copy(piece, piece, to(0, 3)))

    def forward(p):
        ups[p].wait_recv()
        piece = unit(order[p], plus(s0, 3)).at[lo]
        halves.append(net.copy(piece, piece, to(0, 1)))
        downs[p].wait_recv()
        piece = unit(order[p], plus(s0, 1)).at[hi]
        halves.append(net.copy(piece, piece, to(0, 3)))

    def swap(k):
        return net.copy(column(plus(s0, k)), column(plus(s0, k)), partner)

    for p in (1, 2):
        yield
        near[p - 1].wait_recv()
        pass_on(p)
    yield
    forward(0)
    yield
    far.wait_recv()
    pass_on(3)
    piece = unit(order[3], s0)
    last = net.copy(piece, piece, to(0, 2))
    own.wait()
    swapped = [swap(0)]
    for p in (1, 2):
        yield
        forward(p)
    yield
    ups[3].wait_recv()
    swapped.append(swap(3))
    yield
    downs[3].wait_recv()
    swapped.append(swap(1))
    yield
    for d in halves:
        d.wait_recv()
    last.wait_recv()
    swapped.append(swap(2))
    for d in swapped:
        yield
        d.wait_recv()


def scatter_steps(net, j, owed, stage, r, t0, t1, t2, t3):
    y, z = net.y, net.z
    f0, s0 = (y, z) if j == 0 else (z, y)

    def column(ref, k):
        si = plus(s0, k)
        return ref.at[j, si] if j == 0 else ref.at[j, :, si]

    def to(df, ds):
        return net.device(dy=df, dz=ds) if j == 0 else net.device(dy=ds, dz=df)

    partner = net.device(partner=True)
    lo, hi = pl.ds(0, 2), pl.ds(2, 2)
    order = [2, 1, 3, 0]
    rows = {k: plus(f0, k) for k in range(RING)}
    first = {}
    for k in order:
        first[k] = net.copy(column(stage, k), column(t0, k), partner)
        if k == 2:
            yield
    cols = {k: column(r, k) for k in range(RING)}

    def start(k):
        b = column(t0, k)
        for i in order:
            cols[k][rows[i]] = cols[k][rows[i]] + b[rows[i]]

    yield
    first[2].wait_recv()
    start(2)
    ups = {i: net.copy(cols[2].at[rows[i], lo], t1.at[j, 0, rows[i]], to(0, 1)) for i in order}
    downs = {i: net.copy(cols[2].at[rows[i], hi], t1.at[j, 1, rows[i]], to(0, 3)) for i in order}
    yield
    first[1].wait_recv()
    start(1)
    yield
    first[3].wait_recv()
    start(3)
    yield
    first[0].wait_recv()
    start(0)
    ups2, downs2 = {}, {}
    for i in order:
        q = rows[i]
        yield
        ups[i].wait_recv()
        cols[1][q, lo] = cols[1][q, lo] + t1[j, 0, q]
        ups2[i] = net.copy(cols[1].at[q], t2.at[j, 0, q], to(0, 1))
        downs[i].wait_recv()
        cols[3][q, hi] = cols[3][q, hi] + t1[j, 1, q]
        downs2[i] = net.copy(cols[3].at[q], t2.at[j, 1, q], to(0, 3))
    sent = []
    for i in order:
        q = rows[i]
        yield
        ups2[i].wait_recv()
        downs2[i].wait_recv()
        cols[0][q] = cols[0][q] + (t2[j, 0, q] + t2[j, 1, q])
        if i:
            sent.append(net.copy(cols[0].at[q], t3.at[j, i - 1], to(i, 0)))
    for d in sent:
        yield
        d.wait_recv()
    owed[j] = (cols[0][rows[0]] + t3[j, 0]) + (t3[j, 1] + t3[j, 2])


def border_steps(net, u, border, local_sem):
    src = u.at[:, pl.ds(0, 2)]
    own = pltpu.make_async_copy(src, border.at[net.g], local_sem)
    own.start()
    sent = [net.copy(src, border.at[net.g], net.device(dx=k)) for k in (1, 3, 2)]
    yield
    own.wait()
    for d in sent:
        d.wait_recv()


def axis_reduce_steps(net, m, out, acc, slots, halves):
    c = net.c
    rows = acc.shape[1]
    partner = net.device(partner=True)
    d = net.copy(m.at[pl.ds((1 - c) * rows, rows)], halves, partner)
    yield
    d.wait_recv()
    acc[0] = m[pl.ds(c * rows, rows)] + halves[...]
    for t in range(3):
        sent = []
        for k in (1, 3, 2):
            step = [0, 0, 0]
            step[t] = k * (1 - c)
            step[(t + 1) % 3] = step[(t + 1) % 3] + k * c
            sent.append(
                net.copy(acc.at[t], slots.at[t, k - 1], net.device(step[0], step[1], step[2]))
            )
        yield
        for d in sent:
            d.wait_recv()
        acc[t + 1] = (acc[t] + slots[t, 0]) + (slots[t, 1] + slots[t, 2])
    out[pl.ds(c * rows, rows)] = acc[3]
    d = net.copy(acc.at[3], out.at[pl.ds(c * rows, rows)], partner)
    yield
    d.wait_recv()


def reduce_steps(net, m, out, acc, slots, plane_slots, halves):
    c = net.c
    rows = acc.shape[1]
    partner = net.device(partner=True)
    d = net.copy(m.at[pl.ds((1 - c) * rows, rows)], halves, partner)
    yield
    d.wait_recv()
    acc[0] = m[pl.ds(c * rows, rows)] + halves[...]
    sent = [net.copy(acc.at[0], slots.at[k - 1], net.device(dx=k)) for k in (1, 3, 2)]
    yield
    for d in sent:
        d.wait_recv()
    acc[1] = (acc[0] + slots[0]) + (slots[1] + slots[2])
    sent = [
        net.copy(acc.at[1], plane_slots.at[k - 1], net.device(dy=k % RING, dz=k // RING))
        for k in FAR_FIRST
    ]
    yield
    for d in sent:
        d.wait_recv()
    terms = [acc[1]] + [plane_slots[k] for k in range(RING * RING - 1)]
    while len(terms) > 1:
        terms = [a + b for a, b in zip(terms[::2], terms[1::2])]
    acc[2] = terms[0]
    out[pl.ds(c * rows, rows)] = terms[0]
    d = net.copy(acc.at[2], out.at[pl.ds(c * rows, rows)], partner)
    yield
    d.wait_recv()


def hops(k):
    return min(k % RING, RING - k % RING) + min(k // RING, RING - k // RING)


FAR_FIRST = sorted(range(1, RING * RING), key=lambda k: -hops(k))


def advance(steps, count=1):
    for _ in range(count):
        for s in steps:
            next(s, None)


def run(*steps):
    for s in steps:
        for _ in s:
            pass


def split(a):
    top = a.astype(bf16)
    return top, (a - top.astype(f32)).astype(bf16)


def dot3(a, b, dims):
    axis = dims[1][0]
    left = [x[i] for i in (0, 1, 0) for x in a]
    right = [x[i] for i in (0, 0, 1) for x in b]
    return lax.dot_general(
        jnp.concatenate(left, axis=1),
        jnp.concatenate(right, axis=axis),
        (dims, ((), ())),
        preferred_element_type=f32,
    )


ROWS = ((1,), (1,))
COLS = ((1,), (0,))


ROW_COUNT = 4
OFFS = 11
ENTRIES = ROW_COUNT * OFFS
PART_ROWS = 128
NONE = ENTRIES
OWN = ENTRIES + 1
def gram(a, b):
    return lax.dot_general(a, b, (ROWS, ((), ())), precision=highest, preferred_element_type=f32)


def whole(ref, *idx):
    return jnp.concatenate([ref[(0,) + idx], ref[(1,) + idx]], axis=0)


def bits(a, low, mask):
    return jnp.bitwise_and(lax.shift_right_logical(a, low), mask)


def panel_row(panel, slot):
    c, z, y, k = bits(slot, 2, 1), bits(slot, 5, 3), bits(slot, 3, 3), bits(slot, 0, 3)
    return jnp.concatenate([panel[c, 0, z, y, k], panel[c, 1, z, y, k]], axis=0)


def solve(m, r):
    n = m.shape[0]
    t = jnp.concatenate([m, r], axis=1)
    blocks = [t[8 * i : 8 * i + 8] for i in range(n // 8)]
    shape = blocks[0].shape
    row_id = lax.broadcasted_iota(jnp.int32, shape, 0)
    for b in range(n // 8):
        piv = blocks[b]
        rows = [jnp.broadcast_to(piv[i : i + 1], shape) for i in range(8)]
        lanes = [jnp.broadcast_to(piv[:, 8 * b + i : 8 * b + i + 1], shape) for i in range(8)]
        d = [[jnp.broadcast_to(lanes[q][i : i + 1], shape) for q in range(8)] for i in range(8)]
        for i in range(8):
            inv = 1.0 / d[i][i]
            rows[i] = rows[i] * inv
            for q in range(i + 1, 8):
                d[i][q] = d[i][q] * inv
            for k in range(8):
                if k != i:
                    factor = d[k][i]
                    rows[k] = rows[k] - factor * rows[i]
                    for q in range(i + 1, 8):
                        d[k][q] = d[k][q] - factor * d[i][q]
        new = rows[0]
        for i in range(1, 8):
            new = jnp.where(row_id == i, rows[i], new)
        for k in range(n // 8):
            if k != b:
                acc = blocks[k]
                for i in range(8):
                    column = blocks[k][:, 8 * b + i : 8 * b + i + 1]
                    acc = acc - jnp.broadcast_to(column, shape) * rows[i]
                blocks[k] = acc
        blocks[b] = new
        yield
    return jnp.concatenate(blocks, axis=0)[:, n:]


def both(*solves):
    out = [None] * len(solves)
    left = list(range(len(solves)))
    while left:
        for i in list(left):
            try:
                next(solves[i])
            except StopIteration as e:
                out[i] = e.value
                left.remove(i)
        yield
    return out


def finish(steps):
    while True:
        try:
            next(steps)
        except StopIteration as e:
            return e.value


def mm(a, b):
    return lax.dot_general(a, b, (COLS, ((), ())), precision=highest, preferred_element_type=f32)


def tmm(a, b):
    return lax.dot_general(
        a, b, (((0,), (0,)), ((), ())), precision=highest, preferred_element_type=f32
    )


def first_coefficients(g):
    n = g.shape[0] // 2
    g = 0.5 * (g + g.T)
    n0, n1, n2 = g[:n, :n], 0.5 * (g[:n, n:] + g[n:, :n]), g[n:, n:]
    eye = (
        lax.broadcasted_iota(jnp.int32, (n, n), 0) == lax.broadcasted_iota(jnp.int32, (n, n), 1)
    ).astype(f32)
    delta, inverse = yield from both(solve(shift * n0 + n1, n1), solve(n0, eye))
    b = (delta - eye) * (1.0 / shift)
    yield
    n1b, n2b, n0d = mm(n1, b), mm(n2, b), mm(n0, delta)
    yield
    bb = tmm(b, n2b)
    fresh = tmm(delta, n0d) + (tmm(delta, n1b) + tmm(n1b, delta)) + bb
    yield
    a = delta + mm(inverse, fresh)
    yield
    pp = tmm(a, mm(n0, a)) + (tmm(a, n1b) + tmm(n1b, a)) + bb
    pep = tmm(a, mm(n1, a)) + (tmm(a, n2b) + tmm(n2b, a))
    yield
    return delta, a, fresh, shift * pp + pep


def last_coefficients(first, n3):
    delta, a, fresh, known = first
    n = delta.shape[0]
    eye = (
        lax.broadcasted_iota(jnp.int32, (n, n), 0) == lax.broadcasted_iota(jnp.int32, (n, n), 1)
    ).astype(f32)
    b = (delta - eye) * (1.0 / shift)
    n3b = mm(n3, b)
    pq = known + 0.5 * (tmm(b, n3b) + tmm(n3b, b))
    yield
    alpha2 = yield from solve(pq, fresh)
    ba, aa = mm(b, alpha2), mm(a, alpha2)
    return (
        jnp.concatenate([aa - b, delta - shift * aa], axis=1),
        jnp.concatenate([ba, b - shift * ba - aa], axis=1),
        jnp.concatenate([jnp.zeros_like(ba), -ba], axis=1),
    )


def fused_kernel(cols_in, load_in, moved_in, rhs, diag_in, off_in, coup_in, weights_out, basis, *refs):
    refs = iter(refs)

    def take(count):
        return [next(refs) for _ in range(count)]

    u0, u1, diag, off, coup, products, part = take(7)
    panel0, border0, panel1, border1 = take(4)
    owed0, stage0, r0 = take(3)
    parts0 = take(4)
    owed1, stage1, r1 = take(3)
    parts1 = take(4)
    g01, total01 = take(2)
    work01 = take(3)
    g3, total3 = take(2)
    work3 = take(4)
    cols, load, moved, index, table, send, recv, local_sems, in_sems = take(9)
    n, w = u0.shape[2:]
    net = Net(send, recv)
    c = net.c
    barrier = pltpu.get_barrier_semaphore()
    greeted = [net.device(partner=True)] + [net.device(dx=k) for k in (2, 1, 3)]
    greeted += [net.device(dy=k) for k in (2, 1, 3)] + [net.device(dz=k) for k in (2, 1, 3)]
    for d in greeted:
        pl.semaphore_signal(barrier, inc=1, device_id=d, device_id_type=MESH)
    small = [
        pltpu.make_async_copy(a, b, in_sems.at[6 + i])
        for i, (a, b) in enumerate(((cols_in, cols), (load_in, load), (moved_in, moved)))
    ]
    for d in small:
        d.start()
    loads = [
        pltpu.make_async_copy(rhs.at[:, pl.ds(j * n, n)], u0.at[j], in_sems.at[j]) for j in range(2)
    ] + [
        pltpu.make_async_copy(a, b, in_sems.at[2 + i])
        for i, (a, b) in enumerate(((off_in, off), (diag_in, diag), (coup_in, coup)))
    ]
    for d in loads:
        d.start()
    first = (net.g * 32 + lax.axis_index("bulk")) * ROW_COUNT

    for d in small:
        d.wait()
    lane = lax.broadcasted_iota(jnp.int32, (1, PART_ROWS), 1)
    lane = bits(lane, 6, 1) * 4 + bits(lane, 2, 15) * 8 + bits(lane, 0, 3)
    tops = [jnp.full((1, PART_ROWS), -1, jnp.int32)] * 2
    lows = [jnp.full((1, PART_ROWS), NONE + 1, jnp.int32)] * 2
    own_row = jnp.full((1, PART_ROWS), NONE, jnp.int32)
    mine = []
    for s in range(ROW_COUNT):
        count = load[first + s]
        mine.append(moved[first + s])
        own_row = jnp.where(lane == bits(mine[s], 0, PART_ROWS - 1), OWN + s, own_row)
        for t in range(OFFS):
            e = s * OFFS + t
            slot = cols[t, first + s]
            for i, p in enumerate((slot, moved[slot])):
                hit = lane == jnp.where(t < count, bits(p, 0, PART_ROWS - 1), -1)
                tops[i] = jnp.where(hit, e, tops[i])
                lows[i] = jnp.where(hit, jnp.minimum(lows[i], e), lows[i])
    for i in range(2):
        index[2 * i : 2 * i + 1] = jnp.where(tops[i] < 0, NONE, tops[i])
        index[2 * i + 1 : 2 * i + 2] = jnp.where(lows[i] == tops[i], NONE, jnp.minimum(lows[i], NONE))
    index[4:5] = own_row
    index[5:8] = jnp.full((3, PART_ROWS), NONE, jnp.int32)
    indexed = pltpu.make_async_copy(index, table, in_sems.at[5])
    indexed.start()
    for k in range(NONE, products.shape[0]):
        products[k] = jnp.zeros(products.shape[1:], f32)

    def returned(u, begin, end):
        def row(s, _):
            v = split(whole(u, s))
            for t in range(OFFS):
                p = dot3([v], [split(off[s, t])], COLS)
                products[s * OFFS + t, 0] = p[:n]
                products[s * OFFS + t, 1] = p[n:]
            return 0

        lax.fori_loop(begin, end, row, 0)

    def fill(dst, core, start, count):
        def plane(z, _):
            for y in range(RING):
                for k in range(4):
                    p = core * 64 + (z * RING + y) * 4 + k
                    es = [table[start + i, p] for i in range(count)]
                    for j in range(2):
                        v = products[es[0], j]
                        for e in es[1:]:
                            v = v + products[e, j]
                        dst[j, z, y, k] = v
            return 0

        lax.fori_loop(0, RING, plane, 0)

    def crossed(border, s):
        v = [split(jnp.concatenate([border[h, 0, s], border[h, 1, s]], axis=0)) for h in range(RING)]
        return dot3(v, [split(coup[s, h]) for h in range(RING)], ROWS)

    def tiles_of(panel, s):
        v = []
        for t in range(OFFS):
            live = (t < load[first + s]).astype(f32)
            v.append(split(panel_row(panel, cols[t, first + s]) * live))
        return dot3(v, [split(off[s, t]) for t in range(OFFS)], ROWS)

    def set_rest(u):
        for s in range(ROW_COUNT):
            part[s] = dot3([split(whole(u, s))], [split(diag[s])], ROWS)

    def add_crossed(border):
        for s in range(coup.shape[0]):
            part[s] = part[s] + crossed(border, s)

    loads[0].wait()
    loads[1].wait()
    pl.semaphore_wait(barrier, len(greeted))
    gathers = [gather_steps(net, j, u0, panel0, local_sems.at[j]) for j in range(2)]
    borders = border_steps(net, u0, border0, local_sems.at[2])
    advance(gathers)
    advance([borders])
    loads[2].wait()
    returned(u0, 0, ROW_COUNT)
    indexed.wait()
    fill(stage0, 1 - c, 0, 2)
    scatters = [scatter_steps(net, j, owed0, stage0, r0, *parts0) for j in range(2)]
    advance(scatters, 2)
    fill(r0, c, 0, 2)
    advance(scatters)
    advance(gathers, 3)
    advance(scatters, 3)
    advance(gathers)
    advance(scatters, 4)
    advance(gathers, 2)
    loads[3].wait()
    loads[4].wait()
    set_rest(u0)
    run(borders)
    add_crossed(border0)
    advance(scatters, 2)
    advance(gathers, 2)
    advance(scatters, 2)
    run(*gathers)
    for s in range(ROW_COUNT):
        part[s] = part[s] + tiles_of(panel0, s)
    run(*scatters)
    for s in range(ROW_COUNT):
        for j in range(2):
            u1[j, s] = part[s, j * n : (j + 1) * n] + owed0[j, s]

    gathers = [gather_steps(net, j, u1, panel1, local_sems.at[3 + j]) for j in range(2)]
    borders = border_steps(net, u1, border1, local_sems.at[5])
    advance(gathers)
    advance([borders])
    x = [jnp.concatenate([whole(u0, s), whole(u1, s)], axis=0) for s in range(ROW_COUNT)]
    x = jnp.concatenate(x, axis=1)
    g01[...] = gram(x, x)
    sums = axis_reduce_steps(net, g01, total01, *work01)
    advance([sums])
    returned(u1, 0, 2)
    advance(gathers, 2)
    advance([sums])
    advance(gathers, 1)
    returned(u1, 2, 3)
    advance(gathers, 1)
    returned(u1, 3, 4)
    advance(gathers, 1)
    run(borders)
    advance(gathers, 1)
    advance([sums])
    set_rest(u1)
    add_crossed(border1)
    for s in range(ROW_COUNT):
        basis[0 : 2 * n, s * w : (s + 1) * w] = panel_row(panel0, mine[s])
    advance(gathers, 2)
    advance([sums])
    advance(gathers, 1)
    run(*gathers)

    def second_row(s, total):
        tiles = tiles_of(panel1, s)
        v = tiles + part[s]
        products[OWN + s, 0] = v[:n]
        products[OWN + s, 1] = v[n:]
        return total + gram(whole(u1, s), v + tiles)

    total = lax.fori_loop(0, ROW_COUNT, second_row, jnp.zeros((2 * n, 2 * n), f32))
    g3[...] = jnp.concatenate([total[:n], total[n:]], axis=1)
    early = sums
    sums = reduce_steps(net, g3, total3, *work3)
    advance([sums])
    advance([early])
    fill(stage1, 1 - c, 2, 3)
    scatters = [scatter_steps(net, j, owed1, stage1, r1, *parts1) for j in range(2)]
    advance(scatters, 2)
    advance([sums])
    fill(r1, c, 2, 3)
    advance(scatters)
    run(early)
    solving = both(first_coefficients(total01[...]))
    advance([solving], 5)
    advance([sums])
    advance(scatters, 3)
    advance([solving], 2)
    advance(scatters, 4)
    for s in range(ROW_COUNT):
        basis[2 * n : 4 * n, s * w : (s + 1) * w] = panel_row(panel1, mine[s])
    known = finish(solving)[0]
    advance(scatters, 1)
    run(sums)
    n3 = jnp.concatenate([total3[:, : 2 * n], total3[:, 2 * n :]], axis=0)
    solving = both(last_coefficients(known, n3))
    for _ in range(3):
        advance([solving], 3)
        advance(scatters)
    weights = finish(solving)[0]
    for i in range(3):
        weights_out[2 * n * i : 2 * n * (i + 1)] = weights[i]
    run(*scatters)
    for s in range(ROW_COUNT):
        basis[4 * n :, s * w : (s + 1) * w] = whole(owed1, s)
    net.drain()


def last_kernel(weights, basis, sol, res):
    n = sol.shape[1]
    w = sol.shape[2]
    out = tmm(weights[...], basis[...])
    for s in range(sol.shape[0]):
        sol[s] = out[:n, s * w : (s + 1) * w]
        res[s] = out[n:, s * w : (s + 1) * w]


def local(rhs, diag, off, coup, col_index, load, new_slot):
    rows, n2, w = rhs.shape
    n = n2 // 2
    vm = pl.BlockSpec(memory_space=pltpu.VMEM)
    anys = pl.BlockSpec(memory_space=pl.ANY)
    def vmem(*shape):
        return pltpu.VMEM(shape, f32)

    panels = [vmem(2, 2, RING, RING, 4, n, w), vmem(RING, 2, 2, n, w)]
    scatter = [
        vmem(2, rows, n, w),
        vmem(2, RING, RING, 4, n, w),
        vmem(2, RING, RING, 4, n, w),
        vmem(2, RING, RING, 4, n, w),
        vmem(2, 2, RING, 2, n, w),
        vmem(2, 2, RING, 4, n, w),
        vmem(2, 3, 4, n, w),
    ]

    def axis_reduction(m, k):
        half = m // 2
        return [vmem(m, k), vmem(m, k), vmem(4, half, k), vmem(3, 3, half, k), vmem(half, k)]

    def reduction(m, k):
        half = m // 2
        return [vmem(m, k), vmem(m, k), vmem(3, half, k), vmem(3, half, k)] + [
            vmem(RING * RING - 1, half, k),
            vmem(half, k),
        ]

    copies = 2 * (2 * 22 + 3 + 2 * 23 + 20)
    scratch = (
        [vmem(2, rows, n, w), vmem(2, rows, n, w), vmem(*diag.shape), vmem(*off.shape), vmem(*coup.shape)]
        + [vmem(OWN + rows, 2, n, w), vmem(rows, n2, w)]
        + panels
        + panels
        + scatter
        + scatter
        + axis_reduction(2 * n2, 2 * n2)
        + reduction(n, 2 * n2)
        + [pltpu.SMEM(a.shape, jnp.int32) for a in (col_index.T, load, new_slot)]
        + [pltpu.VMEM((8, PART_ROWS), jnp.int32), pltpu.SMEM((8, PART_ROWS), jnp.int32)]
        + [pltpu.SemaphoreType.DMA((copies,))] * 2
        + [pltpu.SemaphoreType.DMA((6,)), pltpu.SemaphoreType.DMA((9,))]
    )
    weights, basis = pl.pallas_call(
        fused_kernel,
        out_shape=[
            jax.ShapeDtypeStruct((3 * n2, 2 * n2), f32),
            jax.ShapeDtypeStruct((3 * n2, rows * w), f32),
        ],
        in_specs=[anys] * 7,
        out_specs=[vm, vm],
        scratch_shapes=scratch,
        compiler_params=pltpu.CompilerParams(
            collective_id=0, has_side_effects=True, vmem_limit_bytes=56 << 20
        ),
        name="fused",
    )(col_index.T, load, new_slot, rhs, diag, off, coup)
    return pl.pallas_call(
        last_kernel,
        out_shape=[jax.ShapeDtypeStruct(rhs.shape, f32)] * 2,
        in_specs=[vm, vm],
        out_specs=[vm, vm],
        name="last",
    )(weights, basis)


def solution(mesh):
    return jax.shard_map(
        local,
        mesh=mesh,
        in_specs=(
            P(("group", "bulk"), None, None),
            P(("group", "bulk"), None, None),
            P(("group", "bulk"), None, None, None),
            P(("group", "bulk"), None, None, None),
            P(),
            P(),
            P(),
        ),
        out_specs=(P(("group", "bulk"), None, None), P(("group", "bulk"), None, None)),
        check_vma=False,
    )
```

```python
import functools

import jax
import jax.numpy as jnp
from jax import lax
from jax.experimental import pallas as pl
from jax.experimental.pallas import tpu as pltpu
from jax.sharding import PartitionSpec as P

highest = lax.Precision.HIGHEST
shift = 4.0
f32 = jnp.float32
bf16 = jnp.bfloat16
RING = 4
MESH = pl.DeviceIdType.MESH


class Net:
    def __init__(self, send, recv):
        self.g = lax.axis_index("group")
        b = lax.axis_index("bulk")
        self.c = lax.rem(b, 2)
        self.y = lax.rem(b // 2, RING)
        self.z = b // (2 * RING)
        self.send, self.recv = send, recv
        self.count = 0
        self.arrivals = 0
        self.pending = []

    def device(self, dx=0, dy=0, dz=0, partner=False):
        c = 1 - self.c if partner else self.c
        y = lax.rem(self.y + dy, RING)
        z = lax.rem(self.z + dz, RING)
        return (lax.rem(self.g + dx, RING), (z * RING + y) * 2 + c)

    def slot(self):
        self.count += 1
        return self.count - 1

    def sent(self, ref):
        i = self.slot()
        self.pending.append((i, ref))
        return i

    def copy(self, src, dst, device, out, into=None):
        d = pltpu.make_async_remote_copy(
            src_ref=src,
            dst_ref=dst,
            send_sem=self.send.at[out],
            recv_sem=self.recv.at[self.arrival() if into is None else into],
            device_id=device,
            device_id_type=MESH,
        )
        d.start()
        return d

    def arrival(self):
        self.arrivals += 1
        return self.arrivals - 1

    def arrived(self, ref, into):
        pltpu.make_async_copy(ref, ref, self.recv.at[into]).wait()

    def drain(self):
        for i, ref in self.pending:
            pltpu.make_async_copy(ref, ref, self.send.at[i]).wait()


def plus(a, k):
    return lax.rem(a + k, RING)


def gather_steps(net, j, u, panel, local_sem):
    c, y, z = net.c, net.y, net.z
    f0, s0 = (y, z) if j == 0 else (z, y)

    def unit(fi, si):
        return panel.at[c, j, si, fi] if j == 0 else panel.at[c, j, fi, si]

    def column(si):
        return panel.at[c, j, si] if j == 0 else panel.at[c, j, :, si]

    def to(df, ds):
        return net.device(dy=df, dz=ds) if j == 0 else net.device(dy=ds, dz=df)

    partner = net.device(partner=True)
    mine = unit(f0, s0)
    own = pltpu.make_async_copy(u.at[j], mine, local_sem)
    own.start()
    out = net.sent(panel.at[0, 0, pl.ds(0, 3)])
    out_half = net.sent(panel.at[0, 0, 0, pl.ds(0, 3)])
    out_swap = net.sent(panel.at[0, 0])
    into_half, into_swap = net.arrival(), net.arrival()
    near = [net.copy(u.at[j], mine, to(k, 0), out) for k in (1, 3)]
    ups = [net.copy(u.at[j], mine, to(0, 1), out)]
    downs = [net.copy(u.at[j], mine, to(0, 3), out)]
    far = net.copy(u.at[j], mine, to(2, 0), out)
    lo, hi = pl.ds(0, 2), pl.ds(2, 2)
    order = [f0, plus(f0, 3), plus(f0, 1), plus(f0, 2)]

    def pass_on(p):
        piece = unit(order[p], s0)
        ups.append(net.copy(piece, piece, to(0, 1), out))
        downs.append(net.copy(piece, piece, to(0, 3), out))

    def forward(p):
        ups[p].wait_recv()
        piece = unit(order[p], plus(s0, 3)).at[lo]
        net.copy(piece, piece, to(0, 1), out_half, into_half)
        downs[p].wait_recv()
        piece = unit(order[p], plus(s0, 1)).at[hi]
        net.copy(piece, piece, to(0, 3), out_half, into_half)

    def swap(k):
        net.copy(column(plus(s0, k)), column(plus(s0, k)), partner, out_swap, into_swap)

    for p in (1, 2):
        yield
        near[p - 1].wait_recv()
        pass_on(p)
    yield
    forward(0)
    yield
    far.wait_recv()
    pass_on(3)
    piece = unit(order[3], s0)
    last = net.copy(piece, piece, to(0, 2), out)
    own.wait()
    swap(0)
    for p in (1, 2):
        yield
        forward(p)
    yield
    ups[3].wait_recv()
    swap(3)
    yield
    downs[3].wait_recv()
    swap(1)
    yield
    net.arrived(panel.at[c, j, 0, pl.ds(0, 3)], into_half)
    last.wait_recv()
    swap(2)
    yield
    net.arrived(panel.at[1 - c, j], into_swap)


def scatter_steps(net, j, owed, stage, r, t0, t1, t2, t3):
    y, z = net.y, net.z
    f0, s0 = (y, z) if j == 0 else (z, y)

    def column(ref, k):
        si = plus(s0, k)
        return ref.at[j, si] if j == 0 else ref.at[j, :, si]

    def to(df, ds):
        return net.device(dy=df, dz=ds) if j == 0 else net.device(dy=ds, dz=df)

    partner = net.device(partner=True)
    lo, hi = pl.ds(0, 2), pl.ds(2, 2)
    order = [2, 1, 3, 0]
    rows = {k: plus(f0, k) for k in range(RING)}
    first = {}
    out_first = net.sent(stage.at[0])
    out = net.sent(stage.at[0, pl.ds(0, 3)])
    out_last = net.sent(t3.at[0])
    into = {i: net.arrival() for i in order}
    into2 = {i: net.arrival() for i in order}
    into3 = net.arrival()
    for k in order:
        first[k] = net.copy(column(stage, k), column(t0, k), partner, out_first)
        if k == 2:
            yield
    cols = {k: column(r, k) for k in range(RING)}

    def start(k):
        b = column(t0, k)
        for i in order:
            cols[k][rows[i]] = cols[k][rows[i]] + b[rows[i]]

    yield
    first[2].wait_recv()
    start(2)
    for i in order:
        q = rows[i]
        net.copy(cols[2].at[q, lo], t1.at[j, 0, q], to(0, 1), out, into[i])
        net.copy(cols[2].at[q, hi], t1.at[j, 1, q], to(0, 3), out, into[i])
    yield
    first[1].wait_recv()
    start(1)
    yield
    first[3].wait_recv()
    start(3)
    yield
    first[0].wait_recv()
    start(0)
    for i in order:
        q = rows[i]
        yield
        net.arrived(t1.at[j, :, q], into[i])
        cols[1][q, lo] = cols[1][q, lo] + t1[j, 0, q]
        net.copy(cols[1].at[q], t2.at[j, 0, q], to(0, 1), out, into2[i])
        cols[3][q, hi] = cols[3][q, hi] + t1[j, 1, q]
        net.copy(cols[3].at[q], t2.at[j, 1, q], to(0, 3), out, into2[i])
    for i in order:
        q = rows[i]
        yield
        net.arrived(t2.at[j, :, q], into2[i])
        cols[0][q] = cols[0][q] + (t2[j, 0, q] + t2[j, 1, q])
        if i:
            net.copy(cols[0].at[q], t3.at[j, i - 1], to(i, 0), out_last, into3)
    yield
    net.arrived(t3.at[j], into3)
    owed[j] = (cols[0][rows[0]] + t3[j, 0]) + (t3[j, 1] + t3[j, 2])


def border_steps(net, u, border, local_sem):
    src = u.at[:, pl.ds(0, 2)]
    own = pltpu.make_async_copy(src, border.at[net.g], local_sem)
    own.start()
    others = border.at[pl.ds(0, RING - 1)]
    out, into = net.sent(others), net.arrival()
    for k in (1, 3, 2):
        net.copy(src, border.at[net.g], net.device(dx=k), out, into)
    yield
    own.wait()
    net.arrived(others, into)


def axis_reduce_steps(net, m, out, acc, slots, halves):
    c = net.c
    rows = acc.shape[1]
    partner = net.device(partner=True)
    out_pair, out_axis = net.sent(acc.at[pl.ds(0, 2)]), net.sent(slots)
    d = net.copy(m.at[pl.ds((1 - c) * rows, rows)], halves, partner, out_pair)
    yield
    d.wait_recv()
    acc[0] = m[pl.ds(c * rows, rows)] + halves[...]
    for t in range(3):
        into = net.arrival()
        for k in (1, 3, 2):
            step = [0, 0, 0]
            step[t] = k * (1 - c)
            step[(t + 1) % 3] = step[(t + 1) % 3] + k * c
            to = net.device(step[0], step[1], step[2])
            net.copy(acc.at[t], slots.at[t, k - 1], to, out_axis, into)
        yield
        net.arrived(slots.at[t], into)
        acc[t + 1] = (acc[t] + slots[t, 0]) + (slots[t, 1] + slots[t, 2])
    out[pl.ds(c * rows, rows)] = acc[3]
    d = net.copy(acc.at[3], out.at[pl.ds(c * rows, rows)], partner, out_pair)
    yield
    d.wait_recv()


def reduce_steps(net, m, out, acc, slots, plane_slots, halves):
    c = net.c
    rows = acc.shape[1]
    partner = net.device(partner=True)
    out_pair = net.sent(acc.at[pl.ds(0, 2)])
    out_x, out_plane = net.sent(slots), net.sent(plane_slots)
    into_x, into_plane = net.arrival(), net.arrival()
    d = net.copy(m.at[pl.ds((1 - c) * rows, rows)], halves, partner, out_pair)
    yield
    d.wait_recv()
    acc[0] = m[pl.ds(c * rows, rows)] + halves[...]
    for k in (1, 3, 2):
        net.copy(acc.at[0], slots.at[k - 1], net.device(dx=k), out_x, into_x)
    yield
    net.arrived(slots, into_x)
    acc[1] = (acc[0] + slots[0]) + (slots[1] + slots[2])
    for k in FAR_FIRST:
        to = net.device(dy=k % RING, dz=k // RING)
        net.copy(acc.at[1], plane_slots.at[k - 1], to, out_plane, into_plane)
    yield
    net.arrived(plane_slots, into_plane)
    terms = [acc[1]] + [plane_slots[k] for k in range(RING * RING - 1)]
    while len(terms) > 1:
        terms = [a + b for a, b in zip(terms[::2], terms[1::2])]
    acc[2] = terms[0]
    out[pl.ds(c * rows, rows)] = terms[0]
    d = net.copy(acc.at[2], out.at[pl.ds(c * rows, rows)], partner, out_pair)
    yield
    d.wait_recv()


def hops(k):
    return min(k % RING, RING - k % RING) + min(k // RING, RING - k // RING)


FAR_FIRST = sorted(range(1, RING * RING), key=lambda k: -hops(k))


def advance(steps, count=1):
    for _ in range(count):
        for s in steps:
            next(s, None)


def run(*steps):
    for s in steps:
        for _ in s:
            pass


def split(a):
    top = a.astype(bf16)
    return top, (a - top.astype(f32)).astype(bf16)


def dot3(a, b, dims):
    axis = dims[1][0]
    left = [x[i] for i in (0, 1, 0) for x in a]
    right = [x[i] for i in (0, 0, 1) for x in b]
    return lax.dot_general(
        jnp.concatenate(left, axis=1),
        jnp.concatenate(right, axis=axis),
        (dims, ((), ())),
        preferred_element_type=f32,
    )


ROWS = ((1,), (1,))
COLS = ((1,), (0,))


ROW_COUNT = 4
OFFS = 11
ENTRIES = ROW_COUNT * OFFS
PART_ROWS = 128
NONE = ENTRIES
OWN = ENTRIES + 1
def gram(a, b):
    return lax.dot_general(a, b, (ROWS, ((), ())), precision=highest, preferred_element_type=f32)


def whole(ref, *idx):
    return jnp.concatenate([ref[(0,) + idx], ref[(1,) + idx]], axis=0)


def bits(a, low, mask):
    return jnp.bitwise_and(lax.shift_right_logical(a, low), mask)


def panel_row(panel, slot):
    c, z, y, k = bits(slot, 2, 1), bits(slot, 5, 3), bits(slot, 3, 3), bits(slot, 0, 3)
    return jnp.concatenate([panel[c, 0, z, y, k], panel[c, 1, z, y, k]], axis=0)


def solve(m, r):
    n = m.shape[0]
    t = jnp.concatenate([m, r], axis=1)
    blocks = [t[8 * i : 8 * i + 8] for i in range(n // 8)]
    shape = blocks[0].shape
    row_id = lax.broadcasted_iota(jnp.int32, shape, 0)
    for b in range(n // 8):
        piv = blocks[b]
        rows = [jnp.broadcast_to(piv[i : i + 1], shape) for i in range(8)]
        lanes = [jnp.broadcast_to(piv[:, 8 * b + i : 8 * b + i + 1], shape) for i in range(8)]
        d = [[jnp.broadcast_to(lanes[q][i : i + 1], shape) for q in range(8)] for i in range(8)]
        for i in range(8):
            inv = 1.0 / d[i][i]
            rows[i] = rows[i] * inv
            for q in range(i + 1, 8):
                d[i][q] = d[i][q] * inv
            for k in range(8):
                if k != i:
                    factor = d[k][i]
                    rows[k] = rows[k] - factor * rows[i]
                    for q in range(i + 1, 8):
                        d[k][q] = d[k][q] - factor * d[i][q]
        new = rows[0]
        for i in range(1, 8):
            new = jnp.where(row_id == i, rows[i], new)
        for k in range(n // 8):
            if k != b:
                acc = blocks[k]
                for i in range(8):
                    column = blocks[k][:, 8 * b + i : 8 * b + i + 1]
                    acc = acc - jnp.broadcast_to(column, shape) * rows[i]
                blocks[k] = acc
        blocks[b] = new
        yield
    return jnp.concatenate(blocks, axis=0)[:, n:]


def both(*solves):
    out = [None] * len(solves)
    left = list(range(len(solves)))
    while left:
        for i in list(left):
            try:
                next(solves[i])
            except StopIteration as e:
                out[i] = e.value
                left.remove(i)
        yield
    return out


def finish(steps):
    while True:
        try:
            next(steps)
        except StopIteration as e:
            return e.value


def mm(a, b):
    return lax.dot_general(a, b, (COLS, ((), ())), precision=highest, preferred_element_type=f32)


def tmm(a, b):
    return lax.dot_general(
        a, b, (((0,), (0,)), ((), ())), precision=highest, preferred_element_type=f32
    )


def first_coefficients(g):
    n = g.shape[0] // 2
    g = 0.5 * (g + g.T)
    n0, n1, n2 = g[:n, :n], 0.5 * (g[:n, n:] + g[n:, :n]), g[n:, n:]
    eye = (
        lax.broadcasted_iota(jnp.int32, (n, n), 0) == lax.broadcasted_iota(jnp.int32, (n, n), 1)
    ).astype(f32)
    delta, inverse = yield from both(solve(shift * n0 + n1, n1), solve(n0, eye))
    b = (delta - eye) * (1.0 / shift)
    yield
    n1b, n2b, n0d = mm(n1, b), mm(n2, b), mm(n0, delta)
    yield
    bb = tmm(b, n2b)
    fresh = tmm(delta, n0d) + (tmm(delta, n1b) + tmm(n1b, delta)) + bb
    yield
    a = delta + mm(inverse, fresh)
    yield
    pp = tmm(a, mm(n0, a)) + (tmm(a, n1b) + tmm(n1b, a)) + bb
    pep = tmm(a, mm(n1, a)) + (tmm(a, n2b) + tmm(n2b, a))
    yield
    return delta, a, fresh, shift * pp + pep


def last_coefficients(first, n3):
    delta, a, fresh, known = first
    n = delta.shape[0]
    eye = (
        lax.broadcasted_iota(jnp.int32, (n, n), 0) == lax.broadcasted_iota(jnp.int32, (n, n), 1)
    ).astype(f32)
    b = (delta - eye) * (1.0 / shift)
    n3b = mm(n3, b)
    pq = known + 0.5 * (tmm(b, n3b) + tmm(n3b, b))
    yield
    alpha2 = yield from solve(pq, fresh)
    ba, aa = mm(b, alpha2), mm(a, alpha2)
    return (
        jnp.concatenate([aa - b, delta - shift * aa], axis=1),
        jnp.concatenate([ba, b - shift * ba - aa], axis=1),
        jnp.concatenate([jnp.zeros_like(ba), -ba], axis=1),
    )


def fused_kernel(cols_in, load_in, moved_in, rhs, diag_in, off_in, coup_in, weights_out, basis, *refs):
    refs = iter(refs)

    def take(count):
        return [next(refs) for _ in range(count)]

    u0, u1, diag, off, coup, products, part = take(7)
    panel0, border0, panel1, border1 = take(4)
    owed0, stage0, r0 = take(3)
    parts0 = take(4)
    owed1, stage1, r1 = take(3)
    parts1 = take(4)
    g01, total01 = take(2)
    work01 = take(3)
    g3, total3 = take(2)
    work3 = take(4)
    cols, load, moved, index, table, send, recv, local_sems, in_sems = take(9)
    n, w = u0.shape[2:]
    net = Net(send, recv)
    c = net.c
    barrier = pltpu.get_barrier_semaphore()
    greeted = [net.device(partner=True)] + [net.device(dx=k) for k in (2, 1, 3)]
    greeted += [net.device(dy=k) for k in (2, 1, 3)] + [net.device(dz=k) for k in (2, 1, 3)]
    for d in greeted:
        pl.semaphore_signal(barrier, inc=1, device_id=d, device_id_type=MESH)
    small = [
        pltpu.make_async_copy(a, b, in_sems.at[6 + i])
        for i, (a, b) in enumerate(((cols_in, cols), (load_in, load), (moved_in, moved)))
    ]
    for d in small:
        d.start()
    loads = [
        pltpu.make_async_copy(rhs.at[:, pl.ds(j * n, n)], u0.at[j], in_sems.at[j]) for j in range(2)
    ] + [
        pltpu.make_async_copy(a, b, in_sems.at[2 + i])
        for i, (a, b) in enumerate(((off_in, off), (diag_in, diag), (coup_in, coup)))
    ]
    for d in loads:
        d.start()
    first = (net.g * 32 + lax.axis_index("bulk")) * ROW_COUNT

    for d in small:
        d.wait()
    lane = lax.broadcasted_iota(jnp.int32, (1, PART_ROWS), 1)
    lane = bits(lane, 6, 1) * 4 + bits(lane, 2, 15) * 8 + bits(lane, 0, 3)
    tops = [jnp.full((1, PART_ROWS), -1, jnp.int32)] * 2
    lows = [jnp.full((1, PART_ROWS), NONE + 1, jnp.int32)] * 2
    own_row = jnp.full((1, PART_ROWS), NONE, jnp.int32)
    mine = []
    for s in range(ROW_COUNT):
        count = load[first + s]
        mine.append(moved[first + s])
        own_row = jnp.where(lane == bits(mine[s], 0, PART_ROWS - 1), OWN + s, own_row)
        for t in range(OFFS):
            e = s * OFFS + t
            slot = cols[t, first + s]
            for i, p in enumerate((slot, moved[slot])):
                hit = lane == jnp.where(t < count, bits(p, 0, PART_ROWS - 1), -1)
                tops[i] = jnp.where(hit, e, tops[i])
                lows[i] = jnp.where(hit, jnp.minimum(lows[i], e), lows[i])
    for i in range(2):
        index[2 * i : 2 * i + 1] = jnp.where(tops[i] < 0, NONE, tops[i])
        index[2 * i + 1 : 2 * i + 2] = jnp.where(lows[i] == tops[i], NONE, jnp.minimum(lows[i], NONE))
    index[4:5] = own_row
    index[5:8] = jnp.full((3, PART_ROWS), NONE, jnp.int32)
    indexed = pltpu.make_async_copy(index, table, in_sems.at[5])
    indexed.start()
    for k in range(NONE, products.shape[0]):
        products[k] = jnp.zeros(products.shape[1:], f32)

    def returned(u, begin, end):
        def row(s, _):
            v = split(whole(u, s))
            for t in range(OFFS):
                p = dot3([v], [split(off[s, t])], COLS)
                products[s * OFFS + t, 0] = p[:n]
                products[s * OFFS + t, 1] = p[n:]
            return 0

        lax.fori_loop(begin, end, row, 0)

    def fill(dst, core, start, count):
        def plane(z, _):
            for y in range(RING):
                for k in range(4):
                    p = core * 64 + (z * RING + y) * 4 + k
                    es = [table[start + i, p] for i in range(count)]
                    for j in range(2):
                        v = products[es[0], j]
                        for e in es[1:]:
                            v = v + products[e, j]
                        dst[j, z, y, k] = v
            return 0

        lax.fori_loop(0, RING, plane, 0)

    def crossed(border, s):
        v = [split(jnp.concatenate([border[h, 0, s], border[h, 1, s]], axis=0)) for h in range(RING)]
        return dot3(v, [split(coup[s, h]) for h in range(RING)], ROWS)

    def tiles_of(panel, s):
        v = []
        for t in range(OFFS):
            live = (t < load[first + s]).astype(f32)
            v.append(split(panel_row(panel, cols[t, first + s]) * live))
        return dot3(v, [split(off[s, t]) for t in range(OFFS)], ROWS)

    def set_rest(u):
        for s in range(ROW_COUNT):
            part[s] = dot3([split(whole(u, s))], [split(diag[s])], ROWS)

    def add_crossed(border):
        for s in range(coup.shape[0]):
            part[s] = part[s] + crossed(border, s)

    loads[0].wait()
    loads[1].wait()
    pl.semaphore_wait(barrier, len(greeted))
    gathers = [gather_steps(net, j, u0, panel0, local_sems.at[j]) for j in range(2)]
    borders = border_steps(net, u0, border0, local_sems.at[2])
    advance(gathers)
    advance([borders])
    loads[2].wait()
    returned(u0, 0, ROW_COUNT)
    indexed.wait()
    fill(stage0, 1 - c, 0, 2)
    scatters = [scatter_steps(net, j, owed0, stage0, r0, *parts0) for j in range(2)]
    advance(scatters, 2)
    fill(r0, c, 0, 2)
    advance(scatters)
    advance(gathers, 3)
    advance(scatters, 3)
    advance(gathers)
    advance(scatters, 4)
    advance(gathers, 2)
    loads[3].wait()
    loads[4].wait()
    set_rest(u0)
    run(borders)
    add_crossed(border0)
    advance(scatters, 2)
    advance(gathers, 2)
    advance(scatters, 2)
    run(*gathers)
    for s in range(ROW_COUNT):
        part[s] = part[s] + tiles_of(panel0, s)
    run(*scatters)
    for s in range(ROW_COUNT):
        for j in range(2):
            u1[j, s] = part[s, j * n : (j + 1) * n] + owed0[j, s]

    gathers = [gather_steps(net, j, u1, panel1, local_sems.at[3 + j]) for j in range(2)]
    borders = border_steps(net, u1, border1, local_sems.at[5])
    advance(gathers)
    advance([borders])
    x = [jnp.concatenate([whole(u0, s), whole(u1, s)], axis=0) for s in range(ROW_COUNT)]
    x = jnp.concatenate(x, axis=1)
    g01[...] = gram(x, x)
    sums = axis_reduce_steps(net, g01, total01, *work01)
    advance([sums])
    returned(u1, 0, 2)
    advance(gathers, 2)
    advance([sums])
    advance(gathers, 1)
    returned(u1, 2, 3)
    advance(gathers, 1)
    returned(u1, 3, 4)
    advance(gathers, 1)
    run(borders)
    advance(gathers, 1)
    advance([sums])
    set_rest(u1)
    add_crossed(border1)
    for s in range(ROW_COUNT):
        basis[0 : 2 * n, s * w : (s + 1) * w] = panel_row(panel0, mine[s])
    advance(gathers, 2)
    advance([sums])
    advance(gathers, 1)
    run(*gathers)

    def second_row(s, total):
        tiles = tiles_of(panel1, s)
        v = tiles + part[s]
        products[OWN + s, 0] = v[:n]
        products[OWN + s, 1] = v[n:]
        return total + gram(whole(u1, s), v + tiles)

    total = lax.fori_loop(0, ROW_COUNT, second_row, jnp.zeros((2 * n, 2 * n), f32))
    g3[...] = jnp.concatenate([total[:n], total[n:]], axis=1)
    early = sums
    sums = reduce_steps(net, g3, total3, *work3)
    advance([sums])
    advance([early])
    fill(stage1, 1 - c, 2, 3)
    scatters = [scatter_steps(net, j, owed1, stage1, r1, *parts1) for j in range(2)]
    advance(scatters, 2)
    advance([sums])
    fill(r1, c, 2, 3)
    advance(scatters)
    run(early)
    solving = both(first_coefficients(total01[...]))
    advance([solving], 5)
    advance([sums])
    advance(scatters, 3)
    advance([solving], 2)
    advance(scatters, 4)
    for s in range(ROW_COUNT):
        basis[2 * n : 4 * n, s * w : (s + 1) * w] = panel_row(panel1, mine[s])
    known = finish(solving)[0]
    advance(scatters, 1)
    run(sums)
    n3 = jnp.concatenate([total3[:, : 2 * n], total3[:, 2 * n :]], axis=0)
    solving = both(last_coefficients(known, n3))
    for _ in range(3):
        advance([solving], 3)
        advance(scatters)
    weights = finish(solving)[0]
    for i in range(3):
        weights_out[2 * n * i : 2 * n * (i + 1)] = weights[i]
    run(*scatters)
    for s in range(ROW_COUNT):
        basis[4 * n :, s * w : (s + 1) * w] = whole(owed1, s)
    assert net.count == send.shape[0] and net.arrivals == recv.shape[0]
    net.drain()


def last_kernel(weights, basis, sol, res):
    n = sol.shape[1]
    w = sol.shape[2]
    out = tmm(weights[...], basis[...])
    for s in range(sol.shape[0]):
        sol[s] = out[:n, s * w : (s + 1) * w]
        res[s] = out[n:, s * w : (s + 1) * w]


def local(rhs, diag, off, coup, col_index, load, new_slot):
    rows, n2, w = rhs.shape
    n = n2 // 2
    vm = pl.BlockSpec(memory_space=pltpu.VMEM)
    anys = pl.BlockSpec(memory_space=pl.ANY)
    def vmem(*shape):
        return pltpu.VMEM(shape, f32)

    panels = [vmem(2, 2, RING, RING, 4, n, w), vmem(RING, 2, 2, n, w)]
    scatter = [
        vmem(2, rows, n, w),
        vmem(2, RING, RING, 4, n, w),
        vmem(2, RING, RING, 4, n, w),
        vmem(2, RING, RING, 4, n, w),
        vmem(2, 2, RING, 2, n, w),
        vmem(2, 2, RING, 4, n, w),
        vmem(2, 3, 4, n, w),
    ]

    def axis_reduction(m, k):
        half = m // 2
        return [vmem(m, k), vmem(m, k), vmem(4, half, k), vmem(3, 3, half, k), vmem(half, k)]

    def reduction(m, k):
        half = m // 2
        return [vmem(m, k), vmem(m, k), vmem(3, half, k), vmem(3, half, k)] + [
            vmem(RING * RING - 1, half, k),
            vmem(half, k),
        ]

    sends, arrivals = 2 * (2 * 3 + 1 + 2 * 3) + 5, 2 * (2 * 14 + 1 + 2 * 13) + 9
    scratch = (
        [vmem(2, rows, n, w), vmem(2, rows, n, w), vmem(*diag.shape), vmem(*off.shape), vmem(*coup.shape)]
        + [vmem(OWN + rows, 2, n, w), vmem(rows, n2, w)]
        + panels
        + panels
        + scatter
        + scatter
        + axis_reduction(2 * n2, 2 * n2)
        + reduction(n, 2 * n2)
        + [pltpu.SMEM(a.shape, jnp.int32) for a in (col_index.T, load, new_slot)]
        + [pltpu.VMEM((8, PART_ROWS), jnp.int32), pltpu.SMEM((8, PART_ROWS), jnp.int32)]
        + [pltpu.SemaphoreType.DMA((sends,)), pltpu.SemaphoreType.DMA((arrivals,))]
        + [pltpu.SemaphoreType.DMA((6,)), pltpu.SemaphoreType.DMA((9,))]
    )
    weights, basis = pl.pallas_call(
        fused_kernel,
        out_shape=[
            jax.ShapeDtypeStruct((3 * n2, 2 * n2), f32),
            jax.ShapeDtypeStruct((3 * n2, rows * w), f32),
        ],
        in_specs=[anys] * 7,
        out_specs=[vm, vm],
        scratch_shapes=scratch,
        compiler_params=pltpu.CompilerParams(
            collective_id=0, has_side_effects=True, vmem_limit_bytes=56 << 20
        ),
        name="fused",
    )(col_index.T, load, new_slot, rhs, diag, off, coup)
    return pl.pallas_call(
        last_kernel,
        out_shape=[jax.ShapeDtypeStruct(rhs.shape, f32)] * 2,
        in_specs=[vm, vm],
        out_specs=[vm, vm],
        name="last",
    )(weights, basis)


def solution(mesh):
    return jax.shard_map(
        local,
        mesh=mesh,
        in_specs=(
            P(("group", "bulk"), None, None),
            P(("group", "bulk"), None, None),
            P(("group", "bulk"), None, None, None),
            P(("group", "bulk"), None, None, None),
            P(),
            P(),
            P(),
        ),
        out_specs=(P(("group", "bulk"), None, None), P(("group", "bulk"), None, None)),
        check_vma=False,
    )
```

```python
import functools

import jax
import jax.numpy as jnp
from jax import lax
from jax.experimental import pallas as pl
from jax.experimental.pallas import tpu as pltpu
from jax.sharding import PartitionSpec as P

highest = lax.Precision.HIGHEST
shift = 4.0
f32 = jnp.float32
bf16 = jnp.bfloat16
RING = 4
MESH = pl.DeviceIdType.MESH


class Net:
    def __init__(self, send, recv):
        self.g = lax.axis_index("group")
        b = lax.axis_index("bulk")
        self.c = lax.rem(b, 2)
        self.y = lax.rem(b // 2, RING)
        self.z = b // (2 * RING)
        self.send, self.recv = send, recv
        self.count = 0
        self.arrivals = 0
        self.pending = []

    def device(self, dx=0, dy=0, dz=0, partner=False):
        c = 1 - self.c if partner else self.c
        y = lax.rem(self.y + dy, RING)
        z = lax.rem(self.z + dz, RING)
        return (lax.rem(self.g + dx, RING), (z * RING + y) * 2 + c)

    def slot(self):
        self.count += 1
        return self.count - 1

    def sent(self, ref):
        i = self.slot()
        self.pending.append((i, ref))
        return i

    def copy(self, src, dst, device, out, into=None):
        d = pltpu.make_async_remote_copy(
            src_ref=src,
            dst_ref=dst,
            send_sem=self.send.at[out],
            recv_sem=self.recv.at[self.arrival() if into is None else into],
            device_id=device,
            device_id_type=MESH,
        )
        d.start()
        return d

    def arrival(self):
        self.arrivals += 1
        return self.arrivals - 1

    def arrived(self, ref, into):
        pltpu.make_async_copy(ref, ref, self.recv.at[into]).wait()

    def drain(self):
        for i, ref in self.pending:
            pltpu.make_async_copy(ref, ref, self.send.at[i]).wait()


def plus(a, k):
    return lax.rem(a + k, RING)


def gather_steps(net, j, u, panel, local_sem):
    c, y, z = net.c, net.y, net.z
    f0, s0 = (y, z) if j == 0 else (z, y)

    def unit(fi, si):
        return panel.at[c, j, si, fi] if j == 0 else panel.at[c, j, fi, si]

    def column(si):
        return panel.at[c, j, si] if j == 0 else panel.at[c, j, :, si]

    def to(df, ds):
        return net.device(dy=df, dz=ds) if j == 0 else net.device(dy=ds, dz=df)

    partner = net.device(partner=True)
    mine = unit(f0, s0)
    own = pltpu.make_async_copy(u.at[j], mine, local_sem)
    own.start()
    out = net.sent(panel.at[0, 0, pl.ds(0, 3)])
    out_half = net.sent(panel.at[0, 0, 0, pl.ds(0, 3)])
    out_swap = net.sent(panel.at[0, 0])
    into_half, into_swap = net.arrival(), net.arrival()
    near = [net.copy(u.at[j], mine, to(k, 0), out) for k in (1, 3)]
    ups = [net.copy(u.at[j], mine, to(0, 1), out)]
    downs = [net.copy(u.at[j], mine, to(0, 3), out)]
    far = net.copy(u.at[j], mine, to(2, 0), out)
    lo, hi = pl.ds(0, 2), pl.ds(2, 2)
    order = [f0, plus(f0, 3), plus(f0, 1), plus(f0, 2)]

    def pass_on(p):
        piece = unit(order[p], s0)
        ups.append(net.copy(piece, piece, to(0, 1), out))
        downs.append(net.copy(piece, piece, to(0, 3), out))

    def forward(p):
        ups[p].wait_recv()
        piece = unit(order[p], plus(s0, 3)).at[lo]
        net.copy(piece, piece, to(0, 1), out_half, into_half)
        downs[p].wait_recv()
        piece = unit(order[p], plus(s0, 1)).at[hi]
        net.copy(piece, piece, to(0, 3), out_half, into_half)

    def swap(k):
        net.copy(column(plus(s0, k)), column(plus(s0, k)), partner, out_swap, into_swap)

    for p in (1, 2):
        yield
        near[p - 1].wait_recv()
        pass_on(p)
    yield
    forward(0)
    yield
    far.wait_recv()
    pass_on(3)
    piece = unit(order[3], s0)
    last = net.copy(piece, piece, to(0, 2), out)
    own.wait()
    swap(0)
    for p in (1, 2):
        yield
        forward(p)
    yield
    ups[3].wait_recv()
    swap(3)
    yield
    downs[3].wait_recv()
    swap(1)
    yield
    net.arrived(panel.at[c, j, 0, pl.ds(0, 3)], into_half)
    last.wait_recv()
    swap(2)
    yield
    net.arrived(panel.at[1 - c, j], into_swap)


def scatter_steps(net, j, owed, stage, r, t0, t1, t2, t3):
    y, z = net.y, net.z
    f0, s0 = (y, z) if j == 0 else (z, y)

    def column(ref, k):
        si = plus(s0, k)
        return ref.at[j, si] if j == 0 else ref.at[j, :, si]

    def to(df, ds):
        return net.device(dy=df, dz=ds) if j == 0 else net.device(dy=ds, dz=df)

    partner = net.device(partner=True)
    lo, hi = pl.ds(0, 2), pl.ds(2, 2)
    order = [2, 1, 3, 0]
    rows = {k: plus(f0, k) for k in range(RING)}
    first = {}
    out_first = net.sent(stage.at[0])
    out = net.sent(stage.at[0, pl.ds(0, 3)])
    out_last = net.sent(t3.at[0])
    into = {i: net.arrival() for i in order}
    into2 = {i: net.arrival() for i in order}
    into3 = net.arrival()
    for k in order:
        first[k] = net.copy(column(stage, k), column(t0, k), partner, out_first)
        if k == 2:
            yield
    cols = {k: column(r, k) for k in range(RING)}

    def start(k):
        b = column(t0, k)
        for i in order:
            cols[k][rows[i]] = cols[k][rows[i]] + b[rows[i]]

    yield
    first[2].wait_recv()
    start(2)
    for i in order:
        q = rows[i]
        net.copy(cols[2].at[q, lo], t1.at[j, 0, q], to(0, 1), out, into[i])
        net.copy(cols[2].at[q, hi], t1.at[j, 1, q], to(0, 3), out, into[i])
    yield
    first[1].wait_recv()
    start(1)
    yield
    first[3].wait_recv()
    start(3)
    yield
    first[0].wait_recv()
    start(0)
    for i in order:
        q = rows[i]
        yield
        net.arrived(t1.at[j, :, q], into[i])
        cols[1][q, lo] = cols[1][q, lo] + t1[j, 0, q]
        net.copy(cols[1].at[q], t2.at[j, 0, q], to(0, 1), out, into2[i])
        cols[3][q, hi] = cols[3][q, hi] + t1[j, 1, q]
        net.copy(cols[3].at[q], t2.at[j, 1, q], to(0, 3), out, into2[i])
    for i in order:
        q = rows[i]
        yield
        net.arrived(t2.at[j, :, q], into2[i])
        cols[0][q] = cols[0][q] + (t2[j, 0, q] + t2[j, 1, q])
        if i:
            net.copy(cols[0].at[q], t3.at[j, i - 1], to(i, 0), out_last, into3)
    yield
    net.arrived(t3.at[j], into3)
    owed[j] = (cols[0][rows[0]] + t3[j, 0]) + (t3[j, 1] + t3[j, 2])


def border_steps(net, u, border, local_sem):
    src = u.at[:, pl.ds(0, 2)]
    own = pltpu.make_async_copy(src, border.at[net.g], local_sem)
    own.start()
    others = border.at[pl.ds(0, RING - 1)]
    out, into = net.sent(others), net.arrival()
    for k in (1, 3, 2):
        net.copy(src, border.at[net.g], net.device(dx=k), out, into)
    yield
    own.wait()
    net.arrived(others, into)


def axis_reduce_steps(net, m, out, acc, slots, halves):
    c = net.c
    rows = acc.shape[1]
    partner = net.device(partner=True)
    out_pair, out_axis = net.sent(acc.at[pl.ds(0, 2)]), net.sent(slots)
    d = net.copy(m.at[pl.ds((1 - c) * rows, rows)], halves, partner, out_pair)
    yield
    d.wait_recv()
    acc[0] = m[pl.ds(c * rows, rows)] + halves[...]
    for t in range(3):
        into = net.arrival()
        for k in (1, 3, 2):
            step = [0, 0, 0]
            step[t] = k * (1 - c)
            step[(t + 1) % 3] = step[(t + 1) % 3] + k * c
            to = net.device(step[0], step[1], step[2])
            net.copy(acc.at[t], slots.at[t, k - 1], to, out_axis, into)
        yield
        net.arrived(slots.at[t], into)
        acc[t + 1] = (acc[t] + slots[t, 0]) + (slots[t, 1] + slots[t, 2])
    out[pl.ds(c * rows, rows)] = acc[3]
    d = net.copy(acc.at[3], out.at[pl.ds(c * rows, rows)], partner, out_pair)
    yield
    d.wait_recv()


def reduce_steps(net, m, out, acc, slots, plane_slots, halves):
    c = net.c
    rows = acc.shape[1]
    partner = net.device(partner=True)
    out_pair = net.sent(acc.at[pl.ds(0, 2)])
    out_x, out_plane = net.sent(slots), net.sent(plane_slots)
    into_x, into_plane = net.arrival(), net.arrival()
    d = net.copy(m.at[pl.ds((1 - c) * rows, rows)], halves, partner, out_pair)
    yield
    d.wait_recv()
    acc[0] = m[pl.ds(c * rows, rows)] + halves[...]
    for k in (1, 3, 2):
        net.copy(acc.at[0], slots.at[k - 1], net.device(dx=k), out_x, into_x)
    yield
    net.arrived(slots, into_x)
    acc[1] = (acc[0] + slots[0]) + (slots[1] + slots[2])
    for k in FAR_FIRST:
        to = net.device(dy=k % RING, dz=k // RING)
        net.copy(acc.at[1], plane_slots.at[k - 1], to, out_plane, into_plane)
    yield
    net.arrived(plane_slots, into_plane)
    terms = [acc[1]] + [plane_slots[k] for k in range(RING * RING - 1)]
    while len(terms) > 1:
        terms = [a + b for a, b in zip(terms[::2], terms[1::2])]
    acc[2] = terms[0]
    out[pl.ds(c * rows, rows)] = terms[0]
    d = net.copy(acc.at[2], out.at[pl.ds(c * rows, rows)], partner, out_pair)
    yield
    d.wait_recv()


def hops(k):
    return min(k % RING, RING - k % RING) + min(k // RING, RING - k // RING)


FAR_FIRST = sorted(range(1, RING * RING), key=lambda k: -hops(k))


def advance(steps, count=1):
    for _ in range(count):
        for s in steps:
            next(s, None)


def run(*steps):
    for s in steps:
        for _ in s:
            pass


def split(a):
    top = a.astype(bf16)
    return top, (a - top.astype(f32)).astype(bf16)


def dot3(a, b, dims):
    axis = dims[1][0]
    left = [x[i] for i in (0, 1, 0) for x in a]
    right = [x[i] for i in (0, 0, 1) for x in b]
    return lax.dot_general(
        jnp.concatenate(left, axis=1),
        jnp.concatenate(right, axis=axis),
        (dims, ((), ())),
        preferred_element_type=f32,
    )


ROWS = ((1,), (1,))
COLS = ((1,), (0,))


ROW_COUNT = 4
OFFS = 11
ENTRIES = ROW_COUNT * OFFS
PART_ROWS = 128
NONE = ENTRIES
OWN = ENTRIES + 1
def gram(a, b):
    return lax.dot_general(a, b, (ROWS, ((), ())), precision=highest, preferred_element_type=f32)


def whole(ref, *idx):
    return jnp.concatenate([ref[(0,) + idx], ref[(1,) + idx]], axis=0)


def bits(a, low, mask):
    return jnp.bitwise_and(lax.shift_right_logical(a, low), mask)


def panel_row(panel, slot):
    c, z, y, k = bits(slot, 2, 1), bits(slot, 5, 3), bits(slot, 3, 3), bits(slot, 0, 3)
    return jnp.concatenate([panel[c, 0, z, y, k], panel[c, 1, z, y, k]], axis=0)


def solve(m, r):
    n = m.shape[0]
    t = jnp.concatenate([m, r], axis=1)
    blocks = [t[8 * i : 8 * i + 8] for i in range(n // 8)]
    shape = blocks[0].shape
    row_id = lax.broadcasted_iota(jnp.int32, shape, 0)
    for b in range(n // 8):
        piv = blocks[b]
        rows = [jnp.broadcast_to(piv[i : i + 1], shape) for i in range(8)]
        lanes = [jnp.broadcast_to(piv[:, 8 * b + i : 8 * b + i + 1], shape) for i in range(8)]
        d = [[jnp.broadcast_to(lanes[q][i : i + 1], shape) for q in range(8)] for i in range(8)]
        for i in range(8):
            inv = 1.0 / d[i][i]
            rows[i] = rows[i] * inv
            for q in range(i + 1, 8):
                d[i][q] = d[i][q] * inv
            for k in range(8):
                if k != i:
                    factor = d[k][i]
                    rows[k] = rows[k] - factor * rows[i]
                    for q in range(i + 1, 8):
                        d[k][q] = d[k][q] - factor * d[i][q]
        new = rows[0]
        for i in range(1, 8):
            new = jnp.where(row_id == i, rows[i], new)
        for k in range(n // 8):
            if k != b:
                acc = blocks[k]
                for i in range(8):
                    column = blocks[k][:, 8 * b + i : 8 * b + i + 1]
                    acc = acc - jnp.broadcast_to(column, shape) * rows[i]
                blocks[k] = acc
        blocks[b] = new
        yield
    return jnp.concatenate(blocks, axis=0)[:, n:]


def both(*solves):
    out = [None] * len(solves)
    left = list(range(len(solves)))
    while left:
        for i in list(left):
            try:
                next(solves[i])
            except StopIteration as e:
                out[i] = e.value
                left.remove(i)
        yield
    return out


def finish(steps):
    while True:
        try:
            next(steps)
        except StopIteration as e:
            return e.value


def mm(a, b):
    return lax.dot_general(a, b, (COLS, ((), ())), precision=highest, preferred_element_type=f32)


def tmm(a, b):
    return lax.dot_general(
        a, b, (((0,), (0,)), ((), ())), precision=highest, preferred_element_type=f32
    )


def first_coefficients(g):
    n = g.shape[0] // 2
    g = 0.5 * (g + g.T)
    n0, n1, n2 = g[:n, :n], 0.5 * (g[:n, n:] + g[n:, :n]), g[n:, n:]
    eye = (
        lax.broadcasted_iota(jnp.int32, (n, n), 0) == lax.broadcasted_iota(jnp.int32, (n, n), 1)
    ).astype(f32)
    delta, inverse = yield from both(solve(shift * n0 + n1, n1), solve(n0, eye))
    b = (delta - eye) * (1.0 / shift)
    yield
    n1b, n2b, n0d = mm(n1, b), mm(n2, b), mm(n0, delta)
    yield
    bb = tmm(b, n2b)
    fresh = tmm(delta, n0d) + (tmm(delta, n1b) + tmm(n1b, delta)) + bb
    yield
    a = delta + mm(inverse, fresh)
    yield
    pp = tmm(a, mm(n0, a)) + (tmm(a, n1b) + tmm(n1b, a)) + bb
    pep = tmm(a, mm(n1, a)) + (tmm(a, n2b) + tmm(n2b, a))
    yield
    return delta, a, fresh, shift * pp + pep


def last_coefficients(first, n3):
    delta, a, fresh, known = first
    n = delta.shape[0]
    eye = (
        lax.broadcasted_iota(jnp.int32, (n, n), 0) == lax.broadcasted_iota(jnp.int32, (n, n), 1)
    ).astype(f32)
    b = (delta - eye) * (1.0 / shift)
    n3b = mm(n3, b)
    pq = known + 0.5 * (tmm(b, n3b) + tmm(n3b, b))
    yield
    alpha2 = yield from solve(pq, fresh)
    ba, aa = mm(b, alpha2), mm(a, alpha2)
    return (
        jnp.concatenate([aa - b, delta - shift * aa], axis=1),
        jnp.concatenate([ba, b - shift * ba - aa], axis=1),
        jnp.concatenate([jnp.zeros_like(ba), -ba], axis=1),
    )


def fused_kernel(cols_in, load_in, moved_in, rhs, diag_in, off_in, coup_in, weights_out, basis, *refs):
    refs = iter(refs)

    def take(count):
        return [next(refs) for _ in range(count)]

    u0, u1, diag, off, coup, products, part = take(7)
    panel0, border0, panel1, border1 = take(4)
    owed0, stage0, r0 = take(3)
    parts0 = take(4)
    owed1, stage1, r1 = take(3)
    parts1 = take(4)
    g01, total01 = take(2)
    work01 = take(3)
    g3, total3 = take(2)
    work3 = take(4)
    cols, load, moved, index, table, send, recv, local_sems, in_sems = take(9)
    n, w = u0.shape[2:]
    net = Net(send, recv)
    c = net.c
    barrier = pltpu.get_barrier_semaphore()
    greeted = [net.device(partner=True)] + [net.device(dx=k) for k in (2, 1, 3)]
    greeted += [net.device(dy=k) for k in (2, 1, 3)] + [net.device(dz=k) for k in (2, 1, 3)]
    for d in greeted:
        pl.semaphore_signal(barrier, inc=1, device_id=d, device_id_type=MESH)
    small = [
        pltpu.make_async_copy(a, b, in_sems.at[6 + i])
        for i, (a, b) in enumerate(((cols_in, cols), (load_in, load), (moved_in, moved)))
    ]
    for d in small:
        d.start()
    loads = [
        pltpu.make_async_copy(rhs.at[:, pl.ds(j * n, n)], u0.at[j], in_sems.at[j]) for j in range(2)
    ] + [
        pltpu.make_async_copy(a, b, in_sems.at[2 + i])
        for i, (a, b) in enumerate(((off_in, off), (diag_in, diag), (coup_in, coup)))
    ]
    for d in loads:
        d.start()
    first = (net.g * 32 + lax.axis_index("bulk")) * ROW_COUNT

    for d in small:
        d.wait()
    lane = lax.broadcasted_iota(jnp.int32, (1, PART_ROWS), 1)
    lane = bits(lane, 6, 1) * 4 + bits(lane, 2, 15) * 8 + bits(lane, 0, 3)
    tops = [jnp.full((1, PART_ROWS), -1, jnp.int32)] * 2
    lows = [jnp.full((1, PART_ROWS), NONE + 1, jnp.int32)] * 2
    own_row = jnp.full((1, PART_ROWS), NONE, jnp.int32)
    mine = []
    for s in range(ROW_COUNT):
        count = load[first + s]
        mine.append(moved[first + s])
        own_row = jnp.where(lane == bits(mine[s], 0, PART_ROWS - 1), OWN + s, own_row)
        for t in range(OFFS):
            e = s * OFFS + t
            slot = cols[t, first + s]
            for i, p in enumerate((slot, moved[slot])):
                hit = lane == jnp.where(t < count, bits(p, 0, PART_ROWS - 1), -1)
                tops[i] = jnp.where(hit, e, tops[i])
                lows[i] = jnp.where(hit, jnp.minimum(lows[i], e), lows[i])
    for i in range(2):
        index[2 * i : 2 * i + 1] = jnp.where(tops[i] < 0, NONE, tops[i])
        index[2 * i + 1 : 2 * i + 2] = jnp.where(lows[i] == tops[i], NONE, jnp.minimum(lows[i], NONE))
    index[4:5] = own_row
    index[5:8] = jnp.full((3, PART_ROWS), NONE, jnp.int32)
    indexed = pltpu.make_async_copy(index, table, in_sems.at[5])
    indexed.start()
    for k in range(NONE, products.shape[0]):
        products[k] = jnp.zeros(products.shape[1:], f32)

    def returned(u, begin, end):
        def row(s, _):
            v = split(whole(u, s))
            for t in range(OFFS):
                p = dot3([v], [split(off[s, t])], COLS)
                products[s * OFFS + t, 0] = p[:n]
                products[s * OFFS + t, 1] = p[n:]
            return 0

        lax.fori_loop(begin, end, row, 0)

    def fill(dst, core, start, count):
        def plane(z, _):
            for y in range(RING):
                for k in range(4):
                    p = core * 64 + (z * RING + y) * 4 + k
                    es = [table[start + i, p] for i in range(count)]
                    for j in range(2):
                        v = products[es[0], j]
                        for e in es[1:]:
                            v = v + products[e, j]
                        dst[j, z, y, k] = v
            return 0

        lax.fori_loop(0, RING, plane, 0)

    def crossed(border, s):
        v = [split(jnp.concatenate([border[h, 0, s], border[h, 1, s]], axis=0)) for h in range(RING)]
        return dot3(v, [split(coup[s, h]) for h in range(RING)], ROWS)

    def tiles_of(panel, s):
        v = []
        for t in range(OFFS):
            live = (t < load[first + s]).astype(f32)
            v.append(split(panel_row(panel, cols[t, first + s]) * live))
        return dot3(v, [split(off[s, t]) for t in range(OFFS)], ROWS)

    def set_rest(u):
        for s in range(ROW_COUNT):
            part[s] = dot3([split(whole(u, s))], [split(diag[s])], ROWS)

    def add_crossed(border):
        for s in range(coup.shape[0]):
            part[s] = part[s] + crossed(border, s)

    loads[0].wait()
    loads[1].wait()
    pl.semaphore_wait(barrier, len(greeted))
    gathers = [gather_steps(net, j, u0, panel0, local_sems.at[j]) for j in range(2)]
    borders = border_steps(net, u0, border0, local_sems.at[2])
    advance(gathers)
    advance([borders])
    loads[2].wait()
    returned(u0, 0, ROW_COUNT)
    indexed.wait()
    fill(stage0, 1 - c, 0, 2)
    scatters = [scatter_steps(net, j, owed0, stage0, r0, *parts0) for j in range(2)]
    advance(scatters, 2)
    fill(r0, c, 0, 2)
    advance(scatters)
    advance(gathers, 3)
    advance(scatters, 3)
    advance(gathers)
    advance(scatters, 4)
    advance(gathers, 2)
    loads[3].wait()
    loads[4].wait()
    set_rest(u0)
    run(borders)
    add_crossed(border0)
    advance(scatters, 2)
    advance(gathers, 2)
    advance(scatters, 2)
    run(*gathers)
    for s in range(ROW_COUNT):
        part[s] = part[s] + tiles_of(panel0, s)
    run(*scatters)
    for s in range(ROW_COUNT):
        for j in range(2):
            u1[j, s] = part[s, j * n : (j + 1) * n] + owed0[j, s]

    gathers = [gather_steps(net, j, u1, panel1, local_sems.at[3 + j]) for j in range(2)]
    borders = border_steps(net, u1, border1, local_sems.at[5])
    advance(gathers)
    advance([borders])
    x = [jnp.concatenate([whole(u0, s), whole(u1, s)], axis=0) for s in range(ROW_COUNT)]
    x = jnp.concatenate(x, axis=1)
    g01[...] = gram(x, x)
    sums = axis_reduce_steps(net, g01, total01, *work01)
    advance([sums])
    returned(u1, 0, 2)
    advance(gathers, 2)
    advance([sums])
    advance(gathers, 1)
    returned(u1, 2, 3)
    advance(gathers, 1)
    returned(u1, 3, 4)
    advance(gathers, 1)
    run(borders)
    advance(gathers, 1)
    advance([sums])
    set_rest(u1)
    add_crossed(border1)
    for s in range(ROW_COUNT):
        basis[0 : 2 * n, s * w : (s + 1) * w] = panel_row(panel0, mine[s])
    advance(gathers, 2)
    advance([sums])
    advance(gathers, 1)
    run(*gathers)

    def second_row(s, total):
        tiles = tiles_of(panel1, s)
        v = tiles + part[s]
        products[OWN + s, 0] = v[:n]
        products[OWN + s, 1] = v[n:]
        return total + gram(whole(u1, s), v + tiles)

    total = lax.fori_loop(0, ROW_COUNT, second_row, jnp.zeros((2 * n, 2 * n), f32))
    g3[...] = jnp.concatenate([total[:n], total[n:]], axis=1)
    early = sums
    sums = reduce_steps(net, g3, total3, *work3)
    advance([sums])
    advance([early])
    fill(stage1, 1 - c, 2, 3)
    scatters = [scatter_steps(net, j, owed1, stage1, r1, *parts1) for j in range(2)]
    advance(scatters, 2)
    advance([sums])
    fill(r1, c, 2, 3)
    advance(scatters)
    run(early)
    solving = both(first_coefficients(total01[...]))
    advance([solving], 5)
    advance([sums])
    advance(scatters, 3)
    advance([solving], 2)
    advance(scatters, 4)
    for s in range(ROW_COUNT):
        basis[2 * n : 4 * n, s * w : (s + 1) * w] = panel_row(panel1, mine[s])
    advance([sums])
    known = finish(solving)[0]
    advance(scatters, 2)
    run(sums)
    n3 = jnp.concatenate([total3[:, : 2 * n], total3[:, 2 * n :]], axis=0)
    solving = both(last_coefficients(known, n3))
    for _ in range(3):
        advance([solving], 3)
        advance(scatters)
    weights = finish(solving)[0]
    for i in range(3):
        weights_out[2 * n * i : 2 * n * (i + 1)] = weights[i]
    run(*scatters)
    for s in range(ROW_COUNT):
        basis[4 * n :, s * w : (s + 1) * w] = whole(owed1, s)
    assert net.count == send.shape[0] and net.arrivals == recv.shape[0]
    net.drain()


def last_kernel(weights, basis, sol, res):
    n = sol.shape[1]
    w = sol.shape[2]
    out = tmm(weights[...], basis[...])
    for s in range(sol.shape[0]):
        sol[s] = out[:n, s * w : (s + 1) * w]
        res[s] = out[n:, s * w : (s + 1) * w]


def local(rhs, diag, off, coup, col_index, load, new_slot):
    rows, n2, w = rhs.shape
    n = n2 // 2
    vm = pl.BlockSpec(memory_space=pltpu.VMEM)
    anys = pl.BlockSpec(memory_space=pl.ANY)
    def vmem(*shape):
        return pltpu.VMEM(shape, f32)

    panels = [vmem(2, 2, RING, RING, 4, n, w), vmem(RING, 2, 2, n, w)]
    scatter = [
        vmem(2, rows, n, w),
        vmem(2, RING, RING, 4, n, w),
        vmem(2, RING, RING, 4, n, w),
        vmem(2, RING, RING, 4, n, w),
        vmem(2, 2, RING, 2, n, w),
        vmem(2, 2, RING, 4, n, w),
        vmem(2, 3, 4, n, w),
    ]

    def axis_reduction(m, k):
        half = m // 2
        return [vmem(m, k), vmem(m, k), vmem(4, half, k), vmem(3, 3, half, k), vmem(half, k)]

    def reduction(m, k):
        half = m // 2
        return [vmem(m, k), vmem(m, k), vmem(3, half, k), vmem(3, half, k)] + [
            vmem(RING * RING - 1, half, k),
            vmem(half, k),
        ]

    sends, arrivals = 2 * (2 * 3 + 1 + 2 * 3) + 5, 2 * (2 * 14 + 1 + 2 * 13) + 9
    scratch = (
        [vmem(2, rows, n, w), vmem(2, rows, n, w), vmem(*diag.shape), vmem(*off.shape), vmem(*coup.shape)]
        + [vmem(OWN + rows, 2, n, w), vmem(rows, n2, w)]
        + panels
        + panels
        + scatter
        + scatter
        + axis_reduction(2 * n2, 2 * n2)
        + reduction(n, 2 * n2)
        + [pltpu.SMEM(a.shape, jnp.int32) for a in (col_index.T, load, new_slot)]
        + [pltpu.VMEM((8, PART_ROWS), jnp.int32), pltpu.SMEM((8, PART_ROWS), jnp.int32)]
        + [pltpu.SemaphoreType.DMA((sends,)), pltpu.SemaphoreType.DMA((arrivals,))]
        + [pltpu.SemaphoreType.DMA((6,)), pltpu.SemaphoreType.DMA((9,))]
    )
    weights, basis = pl.pallas_call(
        fused_kernel,
        out_shape=[
            jax.ShapeDtypeStruct((3 * n2, 2 * n2), f32),
            jax.ShapeDtypeStruct((3 * n2, rows * w), f32),
        ],
        in_specs=[anys] * 7,
        out_specs=[vm, vm],
        scratch_shapes=scratch,
        compiler_params=pltpu.CompilerParams(
            collective_id=0, has_side_effects=True, vmem_limit_bytes=56 << 20
        ),
        name="fused",
    )(col_index.T, load, new_slot, rhs, diag, off, coup)
    return pl.pallas_call(
        last_kernel,
        out_shape=[jax.ShapeDtypeStruct(rhs.shape, f32)] * 2,
        in_specs=[vm, vm],
        out_specs=[vm, vm],
        name="last",
    )(weights, basis)


def solution(mesh):
    return jax.shard_map(
        local,
        mesh=mesh,
        in_specs=(
            P(("group", "bulk"), None, None),
            P(("group", "bulk"), None, None),
            P(("group", "bulk"), None, None, None),
            P(("group", "bulk"), None, None, None),
            P(),
            P(),
            P(),
        ),
        out_specs=(P(("group", "bulk"), None, None), P(("group", "bulk"), None, None)),
        check_vma=False,
    )
```
